32 devices in a mesh: dp: 8 (over z, x), tensor: 4 (over y, core).
Axes of the slice: x: 2, y: 2, z: 4, core: 2. Of those that a mesh axis runs over, the one named last changes fastest.
Arguments:
- tokens_long: bfloat16 [16, 512, 1024], P('dp'), may hold values from -6 to 6
- tokens_short: bfloat16 [32, 128, 1024], P('dp'), may hold values from -6 to 6
- lengths_long: int32 [16], P('dp'), may hold values from 129 to 512
- lengths_short: int32 [32], P('dp'), may hold values from 32 to 128
- weight_project: bfloat16 [1024, 3072], P('dp'), may hold values from -0.1875 to 0.1875
- weight_output: bfloat16 [1024, 1024], P('dp'), may hold values from -0.75 to 0.75
- weight_in: bfloat16 [1024, 4096], P('dp', 'tensor'), may hold values from -0.1875 to 0.1875
- weight_down: bfloat16 [4096, 1024], P('tensor', 'dp'), may hold values from -0.09375 to 0.09375
- bias_query: float32 [1024], replicated, may hold values from -6 to 6
- bias_value: float32 [1024], replicated, may hold values from -3 to 3
- bias_output: float32 [1024], replicated, may hold values from -6 to 6
- gain_one: float32 [1024], replicated, may hold values from 0.5 to 1.5
- shift_one: float32 [1024], replicated, may hold values from -6 to 6
- bias_hidden: float32 [4096], P('tensor'), may hold values from -6 to 6
- bias_down: float32 [1024], replicated, may hold values from -6 to 6
- gain_two: float32 [1024], replicated, may hold values from 0.5 to 1.5
- shift_two: float32 [1024], replicated, may hold values from -6 to 6
- cotangent_long: bfloat16 [16, 512, 1024], P('dp'), may hold values from -6 to 6
- cotangent_short: bfloat16 [32, 128, 1024], P('dp'), may hold values from -6 to 6
Outputs:
- layer_long: bfloat16 [16, 512, 1024], P('dp')
- layer_short: bfloat16 [32, 128, 1024], P('dp')
- delta_long: bfloat16 [16, 512, 1024], P('dp')
- delta_short: bfloat16 [32, 128, 1024], P('dp')
- delta_query: float32 [1024], replicated
- delta_value: float32 [1024], replicated
- delta_output: float32 [1024], replicated
- delta_shift_one: float32 [1024], replicated
- delta_hidden: float32 [4096], P('tensor')
- delta_down: float32 [1024], replicated
- delta_shift_two: float32 [1024], replicated
The draws below stay inside these ranges and needn't reach their ends.
All inputs are finite; a program needn't handle non-finite values.
Results may differ from the reference program's by a relative error of at most 0.017.
Values may be sent and summed in bfloat16 or wider, within the bound.
No kernel may reach another device: no remote copies, remote signals or barrier semaphores. Data moves between devices by JAX's collectives and lax.ppermute only.
A program may use at most 256 MiB of HBM per device.

```python
import math
import jax
import jax.numpy as jnp
from jax import lax

D = 1024
H = 16
DH = 64
FF = 4096
LA = 512
LB = 128
NA = 16
NB = 32


def set_ends(values, stream_key, least, top_value):
    dims = values.shape
    index_at = [jax.random.randint(jax.random.fold_in(stream_key, axis), (), 0, dims[axis]) for axis in range(len(dims))]
    values = values.at[tuple(index_at)].set(least)
    longest = dims.index(max(dims))
    index_at[longest] = (index_at[longest] + 1) % dims[longest]
    return values.at[tuple(index_at)].set(top_value)


def shard_levels(own_key, dims, pieces, smallest, high):
    def one(dim, blocks):
        heights = jax.random.uniform(jax.random.fold_in(jax.random.fold_in(own_key, 6), dim), (blocks,), jnp.float32, smallest / len(pieces), high / len(pieces))
        return jnp.repeat(jnp.exp(heights), dims[dim] // blocks).reshape((-1,) + (1,) * (len(dims) - dim - 1))

    factor_of = one(*pieces[0])
    for cut in pieces[1:]:
        factor_of = factor_of * one(*cut)
    return factor_of


def scatter_about(own_key, extent, scale, bound, split=(), held_as=jnp.bfloat16):
    entries = jax.random.normal(own_key, extent, jnp.float32) * scale
    if len(split) > 0:
        entries = shard_levels(own_key, extent, split, -0.22, 0.18) * entries
    return jnp.clip(entries, min=-bound, max=bound).astype(held_as)


def setup_inputs(seed: int = 0) -> dict:
    streams_of = jax.random.split(jax.random.key(seed), 20)
    return {
        "tokens_long": scatter_about(streams_of[0], (NA, LA, D), 1.0, 6.0, ((0, 8),)),
        "tokens_short": scatter_about(streams_of[1], (NB, LB, D), 1.0, 6.0, ((0, 8),)),
        "lengths_long": set_ends(jax.random.randint(streams_of[2], (NA,), LB + 1, LA + 1), jax.random.fold_in(streams_of[2], 1), LB + 1, LA).astype(jnp.int32),
        "lengths_short": set_ends(jax.random.randint(streams_of[3], (NB,), LB // 4, LB + 1), jax.random.fold_in(streams_of[3], 1), LB // 4, LB).astype(jnp.int32),
        "weight_project": scatter_about(streams_of[4], (D, 3 * D), D ** -0.5, 0.1875, ((0, 8),)),
        "weight_output": scatter_about(streams_of[5], (D, D), DH ** -0.5, 0.75, ((0, 8),)),
        "weight_in": scatter_about(streams_of[6], (D, FF), D ** -0.5, 0.1875, ((0, 8), (1, 4))),
        "weight_down": scatter_about(streams_of[7], (FF, D), FF ** -0.5, 0.09375, ((0, 4), (1, 8))),
        "bias_query": scatter_about(streams_of[8], (D,), 1.0, 6.0, (), jnp.float32),
        "bias_value": scatter_about(streams_of[9], (D,), 0.2, 3.0, (), jnp.float32),
        "bias_output": scatter_about(streams_of[10], (D,), 0.5, 6.0, (), jnp.float32),
        "gain_one": jnp.clip(1.0 + 0.1 * jax.random.normal(streams_of[11], (D,), jnp.float32), 0.5, 1.5),
        "shift_one": scatter_about(streams_of[12], (D,), 0.5, 6.0, (), jnp.float32),
        "bias_hidden": scatter_about(streams_of[13], (FF,), 0.5, 6.0, ((0, 4),), jnp.float32),
        "bias_down": scatter_about(streams_of[14], (D,), 0.5, 6.0, (), jnp.float32),
        "gain_two": jnp.clip(1.0 + 0.1 * jax.random.normal(streams_of[15], (D,), jnp.float32), 0.5, 1.5),
        "shift_two": scatter_about(streams_of[16], (D,), 0.5, 6.0, (), jnp.float32),
        "cotangent_long": scatter_about(streams_of[17], (NA, LA, D), 1.0, 6.0, ((0, 8),)),
        "cotangent_short": scatter_about(streams_of[18], (NB, LB, D), 1.0, 6.0, ((0, 8),)),
    }


EPSILON = 1e-05
MASKED = -1000000000.0

@jax.custom_vjp
def low(v):
    return lax.optimization_barrier(v.astype(jnp.bfloat16)).astype(jnp.float32)

@jax.custom_vjp
def low_back(v):
    return v

def low_keep(v):
    return (low(v), None)

def low_pass(kept, grad):
    return (grad,)

def back_keep(v):
    return (v, None)

def back_low(kept, grad):
    return (low(grad),)
low.defvjp(low_keep, low_pass)
low_back.defvjp(back_keep, back_low)

def high_dot(left, right):
    return jnp.dot(left, right, precision=lax.Precision.HIGHEST)

def normalize(residual, gain, shift):
    center = residual - lax.optimization_barrier(jnp.mean(residual, axis=-1, keepdims=True))
    spread = lax.optimization_barrier(jnp.mean(center * center, axis=-1, keepdims=True))
    return center * lax.rsqrt(spread + EPSILON) * gain + shift

def layer(inputs, lengths, biases, weights, gain_pair):
    bias_query, bias_value, bias_output, shift_one, bias_hidden, bias_down, shift_two = biases
    weight_project, weight_output, weight_in, weight_down = weights
    gain_one, gain_two = gain_pair
    seq_count, seq_len, width = inputs.shape
    rows = inputs.reshape(seq_count * seq_len, width)
    projected = low_back(high_dot(rows, weight_project))
    query = low(projected[:, :width] + bias_query)
    keyed = low(projected[:, width:2 * width])
    valued = low(projected[:, 2 * width:] + bias_value)
    head_shape = (seq_count, seq_len, H, DH)
    scores = jnp.einsum('bqhd,bkhd->bhqk', query.reshape(head_shape), keyed.reshape(head_shape), precision=lax.Precision.HIGHEST) * (1.0 / math.sqrt(DH))
    position = jnp.arange(seq_len, dtype=jnp.int32)
    valid = position[None, :] < lengths[:, None]
    scores = low_back(jnp.where(valid[:, None, None, :], scores, MASKED))
    probability = low(jax.nn.softmax(scores, axis=-1))
    attended = jnp.einsum('bhqk,bkhd->bqhd', probability, valued.reshape(head_shape), precision=lax.Precision.HIGHEST)
    attended = low(low_back(attended.reshape(seq_count * seq_len, width)))
    residual_one = rows + low_back(high_dot(attended, weight_output)) + bias_output
    normed_one = normalize(residual_one, gain_one, shift_one)
    pre_gelu = low_back(high_dot(low(normed_one), weight_in)) + bias_hidden
    hidden = low(jax.nn.gelu(pre_gelu, approximate=False))
    residual_two = normed_one + low_back(high_dot(hidden, weight_down)) + bias_down
    return normalize(residual_two, gain_two, shift_two).reshape(seq_count, seq_len, width)

def run_bucket(inputs, lengths, cotangent, biases, weights, gain_pair):
    seq_count, seq_len, width = inputs.shape
    group_size = math.gcd(seq_count, max(1, 4096 // seq_len))
    groups = seq_count // group_size
    stacked = inputs.astype(jnp.float32).reshape(groups, group_size, seq_len, width)
    stacked_len = lengths.astype(jnp.int32).reshape(groups, group_size)
    stacked_grad = cotangent.astype(jnp.float32).reshape(groups, group_size, seq_len, width)

    def one_group(carry, item):
        group_in, group_len, group_grad = item

        def forward(layer_in, bias_set):
            return layer(layer_in, group_len, bias_set, weights, gain_pair)
        layer_out, pull = jax.vjp(forward, group_in, biases)
        grad_in, grad_bias = pull(group_grad)
        carry = jax.tree.map(jnp.add, carry, grad_bias)
        return (carry, (layer_out, grad_in))
    initial = jax.tree.map(jnp.zeros_like, biases)
    totals, (outputs, gradients) = lax.scan(one_group, initial, (stacked, stacked_len, stacked_grad))
    outputs = outputs.reshape(seq_count, seq_len, width).astype(jnp.bfloat16)
    gradients = gradients.reshape(seq_count, seq_len, width).astype(jnp.bfloat16)
    return (outputs, gradients, totals)

def reference(tokens_long, tokens_short, lengths_long, lengths_short, weight_project, weight_output, weight_in, weight_down, bias_query, bias_value, bias_output, gain_one, shift_one, bias_hidden, bias_down, gain_two, shift_two, cotangent_long, cotangent_short):
    weights = (weight_project.astype(jnp.float32), weight_output.astype(jnp.float32), weight_in.astype(jnp.float32), weight_down.astype(jnp.float32))
    biases = (bias_query, bias_value, bias_output, shift_one, bias_hidden, bias_down, shift_two)
    gain_pair = (gain_one, gain_two)
    layer_long, delta_long, sums_long = run_bucket(tokens_long, lengths_long, cotangent_long, biases, weights, gain_pair)
    layer_short, delta_short, sums_short = run_bucket(tokens_short, lengths_short, cotangent_short, biases, weights, gain_pair)
    totals = jax.tree.map(jnp.add, sums_long, sums_short)
    return (layer_long, layer_short, delta_long, delta_short, totals[0], totals[1], totals[2], totals[3], totals[4], totals[5], totals[6])
```

```python
import functools
import math

import jax
import jax.numpy as jnp
from jax import lax
from jax.experimental import pallas as pl
from jax.experimental.pallas import tpu as pltpu
from jax.sharding import PartitionSpec as P

H = 16
DH = 64
PAIR = 2 * DH
BLOCKS = 8
TILE = 256

EPSILON = 1e-05
MASKED = -1000000000.0
F32 = jnp.float32
BF16 = jnp.bfloat16

NN = (((1,), (0,)), ((), ()))
NT = (((1,), (1,)), ((), ()))
TN = (((0,), (0,)), ((), ()))

ANY = pl.BlockSpec(memory_space=pl.ANY)
VMEM = pl.BlockSpec(memory_space=pltpu.VMEM)
SMEM = pl.BlockSpec(memory_space=pltpu.SMEM)

CORE, SEQ, HALF, RANK, LEN_LONG, LEN_SHORT = range(BLOCKS, BLOCKS + 6)


def dot(a, b, dims):
    return lax.dot_general(a, b, dims, preferred_element_type=F32)


def call(body, outs, ins, in_specs, scratch, flops, nbytes, out_specs=None, vmem=56, exps=0):
    if out_specs is None:
        out_specs = [VMEM] * len(outs)
    return pl.pallas_call(
        body,
        out_shape=[jax.ShapeDtypeStruct(s, d) for s, d in outs],
        in_specs=in_specs,
        out_specs=out_specs,
        scratch_shapes=scratch,
        compiler_params=pltpu.CompilerParams(vmem_limit_bytes=vmem << 20),
        cost_estimate=pl.CostEstimate(
            flops=int(flops), bytes_accessed=int(nbytes), transcendentals=int(exps)
        ),
        name=body.func.__name__ if isinstance(body, functools.partial) else body.__name__,
    )(*ins)


def columns(i, width):
    return pl.ds(pl.multiple_of(i * width, width), width)


def project_kernel(
    info, tokens_long, tokens_short, wp, wo, *rest
):
    blocks = BLOCKS - 1
    mine, other = rest[:blocks], rest[blocks : 2 * blocks]
    bq, bv = rest[2 * blocks : 2 * blocks + 2]
    q_out, k_out, v_out, w_out = rest[2 * blocks + 2 : 2 * blocks + 6]
    x, sem = rest[2 * blocks + 6 :]
    width = wo.shape[1]
    rows = wp.shape[0]
    long_len, short_len = tokens_long.shape[1], tokens_short.shape[1]
    part = q_out.shape[0] - short_len
    half = 2 * width
    core = info[CORE]
    copies = [
        pltpu.make_async_copy(
            tokens_long.at[info[SEQ]], x.at[pl.ds(0, long_len)], sem.at[0]
        ),
        pltpu.make_async_copy(
            tokens_short.at[info[RANK]], x.at[pl.ds(long_len, short_len)], sem.at[1]
        ),
    ]
    own = columns(info[0], rows)
    copies.append(pltpu.make_async_copy(wp, w_out.at[own, pl.ds(0, 3 * width)], sem.at[2]))
    copies.append(pltpu.make_async_copy(wo, w_out.at[own, pl.ds(3 * width, width)], sem.at[3]))
    for j in range(blocks):
        at = columns(info[j + 1], rows)
        copies.append(
            pltpu.make_async_copy(mine[j], w_out.at[at, columns(core, half)], sem.at[4 + 2 * j])
        )
        copies.append(
            pltpu.make_async_copy(
                other[j], w_out.at[at, columns(1 - core, half)], sem.at[5 + 2 * j]
            )
        )
    for copy in copies:
        copy.start()
    for copy in copies:
        copy.wait()
    scale = 1.0 / math.sqrt(DH)
    mine_rows = columns(info[HALF], part)

    def step(i, carry):
        at = columns(i, TILE)
        wq = w_out[:, at]
        bias = bq[:, at]
        q_out[0:part, at] = ((dot(x[mine_rows, :], wq, NN) + bias).astype(BF16) * scale).astype(
            BF16
        )
        q_out[part : part + short_len, at] = (
            (dot(x[long_len : long_len + short_len, :], wq, NN) + bias).astype(BF16) * scale
        ).astype(BF16)
        wk = w_out[:, pl.ds(pl.multiple_of(width + i * TILE, TILE), TILE)]
        k_out[:, at] = dot(x[...], wk, NN).astype(BF16)
        wv = w_out[:, pl.ds(pl.multiple_of(2 * width + i * TILE, TILE), TILE)]
        v_out[:, at] = (dot(x[...], wv, NN) + bv[:, at]).astype(BF16)
        return carry

    lax.fori_loop(0, width // TILE, step, 0)


def own_lanes(value, head):
    lane = lax.broadcasted_iota(jnp.int32, value.shape, 1)
    keep = lane < DH if head == 0 else lane >= DH
    return jnp.where(keep, value, jnp.zeros_like(value))


def attend_kernel(info, q, k, v, att, p_long, p_short):
    part = p_long.shape[2]
    long_len, short_len = p_long.shape[1], p_short.shape[1]

    def group(pair, q_at, k_at, length, p_out):
        at = columns(pair, PAIR)
        queries = q[pl.ds(*q_at), at]
        keys = k[pl.ds(*k_at), at]
        values = v[pl.ds(*k_at), at].T
        position = lax.broadcasted_iota(jnp.int32, (k_at[1], q_at[1]), 0)
        outs = []
        for head in range(2):
            scores = dot(keys, own_lanes(queries, head), NT)
            scores = jnp.where(position < length, scores, MASKED)
            highest = jnp.max(scores, axis=0, keepdims=True)
            exponent = jnp.exp(scores - highest)
            total = jnp.sum(exponent, axis=0, keepdims=True)
            low = (exponent * (1.0 / total)).astype(BF16)
            p_out[2 * pair + head] = low
            outs.append(dot(values[head * DH : (head + 1) * DH, :], low, NN))
        att[pl.ds(*q_at), at] = jnp.concatenate(outs, axis=0).T.astype(BF16)

    def step(pair, carry):
        group(pair, (0, part), (0, long_len), info[LEN_LONG], p_long)
        group(pair, (part, short_len), (long_len, short_len), info[LEN_SHORT], p_short)
        return carry

    lax.fori_loop(0, H // 2, step, 0)


def moments(residual):
    center = residual - jnp.mean(residual, axis=-1, keepdims=True)
    spread = jnp.mean(center * center, axis=-1, keepdims=True)
    inverse = lax.rsqrt(spread + EPSILON)
    return center * inverse, inverse


def pull_norm(scaled, unit, inverse):
    first = jnp.mean(scaled, axis=-1, keepdims=True)
    second = jnp.mean(scaled * unit, axis=-1, keepdims=True)
    return inverse * (scaled - first - unit * second)


def output_kernel(
    info, att, tokens_long, tokens_short, weights, bias, gain, shift,
    unit_out, inverse_out, feed_out, x, wo, sem,
):
    width = att.shape[1]
    short_len = tokens_short.shape[1]
    part = att.shape[0] - short_len
    copies = [
        pltpu.make_async_copy(weights.at[:, pl.ds(3 * width, width)], wo, sem.at[0]),
        pltpu.make_async_copy(
            tokens_long.at[info[SEQ], columns(info[HALF], part)], x.at[pl.ds(0, part)], sem.at[1]
        ),
        pltpu.make_async_copy(
            tokens_short.at[info[RANK]], x.at[pl.ds(part, short_len)], sem.at[2]
        ),
    ]
    for copy in copies:
        copy.start()
    for copy in copies:
        copy.wait()

    def step(i, carry):
        at = columns(i, TILE)
        unit_out[:, at] = x[:, at].astype(F32) + dot(att[...], wo[:, at], NN) + bias[:, at]
        return carry

    lax.fori_loop(0, width // TILE, step, 0)

    def rows(i, carry):
        at = columns(i, 64)
        unit, inverse = moments(unit_out[at, :])
        unit_out[at, :] = unit
        inverse_out[at, :] = jnp.broadcast_to(inverse, (64, 128))
        feed_out[at, :] = (unit * gain[...] + shift[...]).astype(BF16)
        return carry

    lax.fori_loop(0, att.shape[0] // 64, rows, 0)


ERF_TOP = (
    0.00022905065861350646, 0.0034082910107109506, 0.050955695062380861,
    0.18520832239976145, 1.128379143519084,
)
ERF_BOTTOM = (
    -1.1791602954361697e-7, 0.000023547966471313185, 0.0010179625278914885,
    0.014070470171167667, 0.11098505178285362, 0.49746925110067538, 1.0,
)


def horner(x, terms):
    total = terms[0]
    for term in terms[1:]:
        total = total * x + term
    return total


def gelu_pair(value):
    bound = 3.7439211627767994
    t = jnp.clip(value * math.sqrt(0.5), -bound, bound)
    square = t * t
    erf = t * horner(square, ERF_TOP) / horner(square, ERF_BOTTOM)
    phi = 0.5 + 0.5 * erf
    density = jnp.exp(value * value * -0.5) * (1.0 / math.sqrt(2.0 * math.pi))
    return value * phi, phi + value * density


def load_block(info, pieces, target, sem):
    rows = pieces[0].shape[0] // 2
    copies = []
    for j, piece in enumerate(pieces):
        at = columns(info[j], rows)
        for side in range(2):
            copies.append(
                pltpu.make_async_copy(
                    piece.at[pl.ds(side * rows, rows)],
                    target.at[side, at],
                    sem.at[2 * j + side],
                )
            )
    return copies


def feed_step(feed, weights, bias_row, slope_out, total):
    tiles = feed.shape[1] // TILE

    def step(i, carry):
        at = columns(i, TILE)
        value = dot(feed[...], weights[0, :, at], NN) + bias_row[:, at]
        act, slope = gelu_pair(value)
        slope_out[:, at] = slope.astype(BF16)
        total[...] += dot(act.astype(BF16), weights[1, :, at], NT)
        return carry

    lax.fori_loop(0, tiles, step, 0)


def feed_kernel(info, feed, bias, *rest):
    pieces = rest[: 2 * BLOCKS]
    slope_out, total, weights, sem = rest[2 * BLOCKS :]
    loads = [
        load_block(info, pieces[b * BLOCKS : (b + 1) * BLOCKS], weights.at[b], sem.at[b])
        for b in range(2)
    ]
    for load in loads:
        for copy in load:
            copy.start()
    total[...] = jnp.zeros_like(total)
    for b in range(2):
        for copy in loads[b]:
            copy.wait()
        feed_step(feed, weights.at[b], bias.at[pl.ds(b, 1)], slope_out.at[b], total)


def feed_last_kernel(
    info, feed, bias, before, unit_one, gain_one, shift_one, bias_down, gain_two, shift_two,
    cot_long, cot_short, *rest,
):
    pieces = rest[: 2 * BLOCKS]
    (
        slope_out, layer_out, delta_out, low_out, sums_out,
        total, cot, weights, sem, small,
    ) = rest[2 * BLOCKS :]
    short_len = cot_short.shape[1]
    part = feed.shape[0] - short_len
    loads = [
        load_block(info, pieces[b * BLOCKS : (b + 1) * BLOCKS], weights.at[b], sem.at[b])
        for b in range(2)
    ]
    for load in loads:
        for copy in load:
            copy.start()
    extra = [
        pltpu.make_async_copy(
            cot_long.at[info[SEQ], columns(info[HALF], part)], cot.at[pl.ds(0, part)], small.at[0]
        ),
        pltpu.make_async_copy(
            cot_short.at[info[RANK]], cot.at[pl.ds(part, short_len)], small.at[1]
        ),
    ]
    for copy in extra:
        copy.start()
    total[...] = before[...]
    for b in range(2):
        for copy in loads[b]:
            copy.wait()
        feed_step(feed, weights.at[b], bias.at[pl.ds(b, 1)], slope_out.at[b], total)
    for copy in extra:
        copy.wait()
    sums_out[...] = jnp.zeros_like(sums_out)

    def rows(i, carry):
        at = columns(i, 64)
        normed = unit_one[at, :] * gain_one[...] + shift_one[...]
        unit, inverse = moments(normed + (total[at, :] + bias_down[...]))
        layer_out[at, :] = (unit * gain_two[...] + shift_two[...]).astype(BF16)
        g = cot[at, :].astype(F32)
        delta = pull_norm(g * gain_two[...], unit, inverse)
        delta_out[at, :] = delta
        low_out[at, :] = delta.astype(BF16)
        sums_out[0:1, :] += jnp.sum(g, axis=0, keepdims=True)
        sums_out[1:2, :] += jnp.sum(delta, axis=0, keepdims=True)
        return carry

    lax.fori_loop(0, feed.shape[0] // 64, rows, 0)


def back_kernel(info, delta_two, low_two, slope_a, slope_b, unit_one, inverse_one, gain_one,
                weights_w, *rest):
    pieces = rest[: 4 * BLOCKS]
    (
        hidden_out, delta_out, att_out, sums_out,
        total, low, weights, wo, sem, small,
    ) = rest[4 * BLOCKS :]
    width = delta_two.shape[1]
    tiles = width // TILE
    loads = [
        load_block(info, pieces[b * BLOCKS : (b + 1) * BLOCKS], weights.at[b % 2], sem.at[b % 2])
        for b in range(4)
    ]
    last = pltpu.make_async_copy(weights_w.at[:, pl.ds(3 * width, width)], wo, small.at[0])
    for b in range(2):
        for copy in loads[b]:
            copy.start()
    last.start()
    total[...] = delta_two[...]
    for b in range(4):
        for copy in loads[b]:
            copy.wait()
        slopes = slope_a if b < 2 else slope_b
        held = weights.at[b % 2]

        def step(i, carry):
            at = columns(i, TILE)
            grad = dot(low_two[...], held[1, :, at], NN) * slopes[b % 2, :, at].astype(F32)
            hidden_out[b : b + 1, at] = jnp.sum(grad, axis=0, keepdims=True)
            total[...] += dot(grad.astype(BF16), held[0, :, at], NT)
            return carry

        lax.fori_loop(0, tiles, step, 0)
        if b + 2 < 4:
            for copy in loads[b + 2]:
                copy.start()
    sums_out[...] = jnp.zeros_like(sums_out)

    def rows(i, carry):
        at = columns(i, 64)
        grad = total[at, :]
        delta = pull_norm(grad * gain_one[...], unit_one[at, :], inverse_one[at, 0:1])
        delta_out[at, :] = delta
        low[at, :] = delta.astype(BF16)
        sums_out[0:1, :] += jnp.sum(grad, axis=0, keepdims=True)
        sums_out[1:2, :] += jnp.sum(delta, axis=0, keepdims=True)
        return carry

    lax.fori_loop(0, total.shape[0] // 64, rows, 0)
    last.wait()

    def spread(i, carry):
        at = columns(i, TILE)
        att_out[:, at] = dot(low[...], wo[at, :], NT).astype(BF16)
        return carry

    lax.fori_loop(0, tiles, spread, 0)


def attend_back_kernel(info, q, k, v, grad, p_long, p_short,
                       dq_out, keep_out, send_out, short_out, sums_out, pool):
    part = p_long.shape[2]
    long_len, short_len = p_long.shape[1], p_short.shape[1]
    width = q.shape[1]
    scale = 1.0 / math.sqrt(DH)

    def group(pair, q_at, k_at, p_in, target):
        at = columns(pair, PAIR)
        after = pl.ds(pl.multiple_of(width + pair * PAIR, PAIR), PAIR)
        queries = q[pl.ds(*q_at), at]
        keys = k[pl.ds(*k_at), at]
        keys_t = keys.T
        values = v[pl.ds(*k_at), at]
        grads = grad[pl.ds(*q_at), at]
        dq, dk, dv = [], 0.0, 0.0
        for head in range(2):
            low = p_in[2 * pair + head]
            prob = low.astype(F32)
            own = own_lanes(grads, head)
            dp = dot(values, own, NT)
            inner = jnp.sum(dp * prob, axis=0, keepdims=True)
            ds = (prob * (dp - inner)).astype(BF16)
            dq.append(dot(keys_t[head * DH : (head + 1) * DH, :], ds, NN))
            dk += dot(ds, own_lanes(queries, head), NN)
            dv += dot(low, own, NN)
        dq = (jnp.concatenate(dq, axis=0) * scale).T
        dq_out[pl.ds(*q_at), at] = dq.astype(BF16)
        target[:, at] = dk.astype(BF16)
        target[:, after] = dv.astype(BF16)
        return jnp.sum(dq, axis=0, keepdims=True), jnp.sum(dv, axis=0, keepdims=True)

    def step(pair, carry):
        at = columns(pair, PAIR)
        a, b = group(pair, (0, part), (0, long_len), p_long, pool)
        c, d = group(pair, (part, short_len), (long_len, short_len), p_short, short_out)
        sums_out[0:1, at] = a + c
        sums_out[1:2, at] = b + d
        return carry

    lax.fori_loop(0, H // 2, step, 0)
    keep_out[...] = pool[columns(info[HALF], part), :]
    send_out[...] = pool[columns(1 - info[HALF], part), :]


def input_kernel(delta_one, dq, keep, received, short, weights_w, out, dkv, weights, sem):
    part = keep.shape[0]
    width = dq.shape[1]
    load = pltpu.make_async_copy(weights_w.at[:, pl.ds(0, 3 * width)], weights, sem.at[0])
    load.start()
    dkv[0:part, :] = (keep[...].astype(F32) + received[...].astype(F32)).astype(BF16)
    dkv[part:, :] = short[...]
    load.wait()

    def step(i, carry):
        at = columns(i, TILE)
        total = delta_one[:, at] + dot(dq[...], weights[at, 0:width], NT)
        total += dot(dkv[...], weights[at, width : 3 * width], NT)
        out[:, at] = total.astype(BF16)
        return carry

    lax.fori_loop(0, width // TILE, step, 0)


def place_kernel(info, own, core, far, far_core, long_out, short_out, sem):
    short_len = short_out.shape[1]
    part = own.shape[0] - short_len
    rank = info[RANK]
    parts = long_out.shape[1] // part
    copies = []
    for j, piece in enumerate((own, core, far, far_core)):
        flip = (0, 1, 2, 3)[j]
        bit0 = rank % 2 if flip % 2 == 0 else 1 - rank % 2
        bit1 = rank // 2 if flip // 2 == 0 else 1 - rank // 2
        who = bit1 * 2 + bit0
        copies.append(
            pltpu.make_async_copy(
                piece.at[pl.ds(0, part)],
                long_out.at[who // parts, columns(who % parts, part)],
                sem.at[2 * j],
            )
        )
        copies.append(
            pltpu.make_async_copy(
                piece.at[pl.ds(part, short_len)], short_out.at[who], sem.at[2 * j + 1]
            )
        )
    for copy in copies:
        copy.start()
    for copy in copies:
        copy.wait()


def flip_pairs(size, bit):
    return [(i, i ^ bit) for i in range(size)]


def ring_of(size):
    return list(range(0, size, 2)) + list(range(size - 1, 0, -2))


def gather_blocks(piece, size):
    if size != BLOCKS:
        whole = lax.all_gather(piece, "dp", axis=0, tiled=False)
        return whole
    ring = ring_of(size)
    forward = [(ring[i], ring[(i + 1) % size]) for i in range(size)]
    backward = [(ring[i], ring[(i - 1) % size]) for i in range(size)]
    found = [piece]
    a = b = piece
    for j in range(size // 2):
        a = lax.ppermute(a, "dp", forward)
        found.append(a)
        if j < size // 2 - 1:
            b = lax.ppermute(b, "dp", backward)
            found.append(b)
    return found


def block_places(size):
    if size != BLOCKS:
        return jnp.arange(BLOCKS, dtype=jnp.int32)
    ring = ring_of(size)
    place = [ring.index(d) for d in range(size)]
    steps = [0]
    for j in range(1, size // 2 + 1):
        steps.append(-j)
        if j < size // 2:
            steps.append(j)
    table = [[ring[(place[d] + s) % size] for s in steps] for d in range(size)]
    return jnp.array(table, jnp.int32)[lax.axis_index("dp")]


def local(
    dp, tensor,
    tokens_long, tokens_short, lengths_long, lengths_short,
    weight_project, weight_output, weight_in, weight_down,
    bias_query, bias_value, bias_output, gain_one, shift_one, bias_hidden, bias_down,
    gain_two, shift_two, cotangent_long, cotangent_short,
):
    long_count, long_len, width = tokens_long.shape
    short_count, short_len, _ = tokens_short.shape
    parts = tensor // long_count
    assert tensor == 4 and parts == 2 and short_count == tensor
    part = long_len // parts
    rows = part + short_len
    keys = long_len + short_len
    units = weight_in.shape[1]

    rank = lax.axis_index("tensor")
    core, seq, half = rank % 2, rank // parts, rank % parts
    info = jnp.concatenate(
        [
            block_places(dp),
            jnp.stack(
                [core, seq, half, rank, lengths_long[seq], lengths_short[rank]]
            ).astype(jnp.int32),
        ]
    )
    core_pairs = flip_pairs(tensor, 1)
    far_pairs = flip_pairs(tensor, 2)

    def to_core(x):
        return lax.ppermute(x, "tensor", core_pairs)

    def to_far(x):
        return lax.ppermute(x, "tensor", far_pairs)

    both = jnp.concatenate([weight_project, weight_output], axis=1)
    down_t = weight_down.T
    if dp == BLOCKS:
        share = lax.dynamic_slice_in_dim(both, core * 2 * width, 2 * width, axis=1)
        w_mine = gather_blocks(share, dp)[1:]
        w_other = [to_core(w) for w in w_mine]
        own_wp, own_wo = weight_project, weight_output
        f_own = gather_blocks(jnp.concatenate([weight_in, down_t], axis=0), dp)
    else:
        whole = lax.all_gather(both, "dp", axis=0, tiled=True)
        step = width // BLOCKS
        cut = [whole[j * step : (j + 1) * step] for j in range(BLOCKS)]
        own_wp, own_wo = cut[0][:, : 3 * width], cut[0][:, 3 * width :]
        w_mine = [
            lax.dynamic_slice_in_dim(w, core * 2 * width, 2 * width, axis=1) for w in cut[1:]
        ]
        w_other = [
            lax.dynamic_slice_in_dim(w, (1 - core) * 2 * width, 2 * width, axis=1)
            for w in cut[1:]
        ]
        full_in = lax.all_gather(weight_in, "dp", axis=0, tiled=True)
        full_down = lax.all_gather(down_t, "dp", axis=0, tiled=True)
        f_own = [
            jnp.concatenate(
                [full_in[j * step : (j + 1) * step], full_down[j * step : (j + 1) * step]], axis=0
            )
            for j in range(BLOCKS)
        ]
    f_far = [to_far(f) for f in f_own]
    f_core = [to_core(f) for f in f_own]
    f_far_core = [to_core(f) for f in f_far]

    hidden_row = bias_hidden.reshape(1, units)
    near_bias = jnp.concatenate([hidden_row, to_far(hidden_row)], axis=0)
    across = to_core(near_bias)
    bias_a = jnp.concatenate([near_bias[0:1], across[0:1]], axis=0)
    bias_b = jnp.concatenate([near_bias[1:2], across[1:2]], axis=0)

    def row(vector):
        return vector.reshape(1, width)

    q, k, v, weights = call(
        project_kernel,
        [((rows, width), BF16), ((keys, width), BF16), ((keys, width), BF16),
         ((width, 4 * width), BF16)],
        [info, tokens_long, tokens_short, own_wp, own_wo, *w_mine, *w_other,
         row(bias_query), row(bias_value)],
        [SMEM] + [ANY] * (4 + 2 * (BLOCKS - 1)) + [VMEM] * 2,
        [pltpu.VMEM((keys, width), BF16), pltpu.SemaphoreType.DMA((4 + 2 * (BLOCKS - 1),))],
        2 * width * width * (rows + 2 * keys), 8 * width * width * 2,
    )
    att, p_long, p_short = call(
        attend_kernel,
        [((rows, width), BF16), ((H, long_len, part), BF16), ((H, short_len, short_len), BF16)],
        [info, q, k, v],
        [SMEM] + [VMEM] * 3,
        [],
        4 * width * (long_len * part + short_len * short_len), 8 << 20,
        exps=H * (long_len * part + short_len * short_len),
    )
    unit_one, inverse_one, feed = call(
        output_kernel,
        [((rows, width), F32), ((rows, 128), F32), ((rows, width), BF16)],
        [info, att, tokens_long, tokens_short, weights, row(bias_output), row(gain_one),
         row(shift_one)],
        [SMEM, VMEM, ANY, ANY, ANY, VMEM, VMEM, VMEM],
        [pltpu.VMEM((rows, width), BF16), pltpu.VMEM((width, width), BF16),
         pltpu.SemaphoreType.DMA((3,))],
        2 * width * width * rows, 6 << 20,
    )
    slope_a, before = call(
        feed_kernel,
        [((2, rows, units), BF16), ((rows, width), F32)],
        [info, feed, bias_a, *f_own, *f_core],
        [SMEM, VMEM, VMEM] + [ANY] * (2 * BLOCKS),
        [pltpu.VMEM((2, 2, width, units), BF16), pltpu.SemaphoreType.DMA((2, 2 * BLOCKS))],
        8 * width * units * rows, 12 << 20,
    )
    slope_b, layer, delta_two, low_two, sums_a = call(
        feed_last_kernel,
        [((2, rows, units), BF16), ((rows, width), BF16), ((rows, width), F32),
         ((rows, width), BF16), ((2, width), F32)],
        [info, feed, bias_b, before, unit_one, row(gain_one), row(shift_one), row(bias_down),
         row(gain_two), row(shift_two), cotangent_long, cotangent_short, *f_far, *f_far_core],
        [SMEM] + [VMEM] * 9 + [ANY] * (2 + 2 * BLOCKS),
        [pltpu.VMEM((rows, width), F32), pltpu.VMEM((rows, width), BF16),
         pltpu.VMEM((2, 2, width, units), BF16), pltpu.SemaphoreType.DMA((2, 2 * BLOCKS)),
         pltpu.SemaphoreType.DMA((2,))],
        8 * width * units * rows, 16 << 20,
    )
    hidden_sums, delta_one, grad_att, sums_b = call(
        back_kernel,
        [((4, units), F32), ((rows, width), F32), ((rows, width), BF16), ((2, width), F32)],
        [info, delta_two, low_two, slope_a, slope_b, unit_one, inverse_one, row(gain_one), weights,
         *f_own, *f_core, *f_far, *f_far_core],
        [SMEM] + [VMEM] * 7 + [ANY] * (1 + 4 * BLOCKS),
        [pltpu.VMEM((rows, width), F32), pltpu.VMEM((rows, width), BF16),
         pltpu.VMEM((2, 2, width, units), BF16), pltpu.VMEM((width, width), BF16),
         pltpu.SemaphoreType.DMA((2, 2 * BLOCKS)), pltpu.SemaphoreType.DMA((1,))],
        18 * width * units * rows, 26 << 20,
    )
    dq, keep, send, short, sums_c = call(
        attend_back_kernel,
        [((rows, width), BF16), ((part, 2 * width), BF16), ((part, 2 * width), BF16),
         ((short_len, 2 * width), BF16), ((2, width), F32)],
        [info, q, k, v, grad_att, p_long, p_short],
        [SMEM] + [VMEM] * 6,
        [pltpu.VMEM((long_len, 2 * width), BF16)],
        8 * width * (long_len * part + short_len * short_len), 12 << 20,
    )
    received = to_core(send)
    (delta_rows,) = call(
        input_kernel,
        [((rows, width), BF16)],
        [delta_one, dq, keep, received, short, weights],
        [VMEM] * 5 + [ANY],
        [pltpu.VMEM((rows, 2 * width), BF16), pltpu.VMEM((width, 3 * width), BF16),
         pltpu.SemaphoreType.DMA((1,))],
        6 * width * width * rows, 10 << 20,
    )

    def spread(x):
        far = to_far(x)
        return x, to_core(x), far, to_core(far)

    def place(x):
        return call(
            place_kernel,
            [((long_count, long_len, width), BF16), ((short_count, short_len, width), BF16)],
            [info, *spread(x)],
            [SMEM] + [VMEM] * 4,
            [pltpu.SemaphoreType.DMA((8,))],
            0, 16 * rows * width,
            out_specs=[ANY, ANY],
        )

    layer_long, layer_short = place(layer)
    delta_long, delta_short = place(delta_rows)

    over = to_core(jnp.stack([hidden_sums[1], hidden_sums[3]]))
    mine = hidden_sums[0] + over[0]
    theirs = hidden_sums[2] + over[1]
    mine = mine + to_far(theirs.reshape(1, units))[0]
    vectors = jnp.concatenate([sums_a, sums_b, sums_c], axis=0)
    vectors = vectors + to_core(vectors)
    vectors = vectors + to_far(vectors)
    vectors = jnp.concatenate([vectors, mine.reshape(-1, width)], axis=0)
    bit = 1
    while bit < dp:
        vectors = vectors + lax.ppermute(vectors, "dp", flip_pairs(dp, bit))
        bit *= 2
    return (
        layer_long, layer_short, delta_long, delta_short,
        vectors[4], vectors[5], vectors[3], vectors[2],
        vectors[6:].reshape(units), vectors[1], vectors[0],
    )


def solution(mesh):
    in_specs = (
        P("dp", None, None), P("dp", None, None), P("dp"), P("dp"),
        P("dp", None), P("dp", None), P("dp", "tensor"), P("tensor", "dp"),
        P(), P(), P(), P(), P(), P("tensor"), P(), P(), P(),
        P("dp", None, None), P("dp", None, None),
    )
    out_specs = (
        P("dp", None, None), P("dp", None, None), P("dp", None, None), P("dp", None, None),
        P(), P(), P(), P(), P("tensor"), P(), P(),
    )
    body = functools.partial(local, mesh.shape["dp"], mesh.shape["tensor"])
    return jax.shard_map(body, mesh=mesh, in_specs=in_specs, out_specs=out_specs, check_vma=False)
```

```python
import functools
import math

import jax
import jax.numpy as jnp
from jax import lax
from jax.experimental import pallas as pl
from jax.experimental.pallas import tpu as pltpu
from jax.sharding import PartitionSpec as P

H = 16
DH = 64
PAIR = 2 * DH
BLOCKS = 8
TILE = 256
WIDE = 512
STRIP = 32
GROUP = 2
PROJECT_MIB, ATTEND_MIB, OUTPUT_MIB, FEED_MIB = 24, 24, 20, 28
MIDDLE_MIB, BACK_MIB, EARLY_MIB, LATE_MIB = 44, 28, 20, 20

EPSILON = 1e-05
MASKED = -1000000000.0
F32 = jnp.float32
BF16 = jnp.bfloat16

NN = (((1,), (0,)), ((), ()))
NT = (((1,), (1,)), ((), ()))
TN = (((0,), (0,)), ((), ()))

ANY = pl.BlockSpec(memory_space=pl.ANY)
VMEM = pl.BlockSpec(memory_space=pltpu.VMEM)
SMEM = pl.BlockSpec(memory_space=pltpu.SMEM)

CORE, SEQ, HALF, RANK, LEN_LONG, LEN_SHORT = range(BLOCKS, BLOCKS + 6)


def dot(a, b, dims):
    return lax.dot_general(a, b, dims, preferred_element_type=F32)


def call(body, outs, ins, in_specs, scratch, flops, nbytes, out_specs=None, vmem=56, exps=0,
         grid=()):
    if out_specs is None:
        out_specs = [VMEM] * len(outs)
    return pl.pallas_call(
        body,
        grid=grid,
        out_shape=[jax.ShapeDtypeStruct(s, d) for s, d in outs],
        in_specs=in_specs,
        out_specs=out_specs,
        scratch_shapes=scratch,
        compiler_params=pltpu.CompilerParams(vmem_limit_bytes=vmem << 20),
        cost_estimate=pl.CostEstimate(
            flops=int(flops), bytes_accessed=int(nbytes), transcendentals=int(exps)
        ),
        name=body.func.__name__ if isinstance(body, functools.partial) else body.__name__,
    )(*ins)


def columns(i, width):
    return pl.ds(pl.multiple_of(i * width, width), width)


def project_kernel(info, tokens_long, tokens_short, *rest):
    blocks, rest = rest[:BLOCKS + 1], rest[BLOCKS + 1 :]
    bq, bv, q_out, k_out, v_out, w_out, x, held, sem = rest
    rows, width = blocks[0].shape[0], bq.shape[1]
    long_len, short_len = tokens_long.shape[1], tokens_short.shape[1]
    part = q_out.shape[0] - short_len
    pairs = [
        (tokens_long.at[info[SEQ]], x.at[pl.ds(0, long_len)]),
        (tokens_short.at[info[RANK]], x.at[pl.ds(long_len, short_len)]),
    ]
    for j in range(BLOCKS - 1):
        pairs.append((blocks[j], held.at[columns(info[j], rows)]))
    for j in range(2):
        half = info[CORE] if j == 0 else 1 - info[CORE]
        at = columns(2 * info[BLOCKS - 1] + half, rows // 2)
        pairs.append((blocks[BLOCKS - 1 + j], held.at[at]))
    copies = [pltpu.make_async_copy(a, b, sem.at[i]) for i, (a, b) in enumerate(pairs)]
    for copy in copies:
        copy.start()
    for copy in copies:
        copy.wait()
    store = pltpu.make_async_copy(held, w_out, sem.at[len(copies)])
    store.start()
    scale = 1.0 / math.sqrt(DH)
    mine_rows = columns(info[HALF], part)
    for i in range(width // WIDE):
        at = slice(i * WIDE, (i + 1) * WIDE)
        wq = held[:, at]
        bias = bq[:, at]
        q_out[0:part, at] = ((dot(x[mine_rows, :], wq, NN) + bias).astype(BF16) * scale).astype(
            BF16
        )
        q_out[part:, at] = ((dot(x[long_len:, :], wq, NN) + bias).astype(BF16) * scale).astype(
            BF16
        )
        wk = held[:, width + i * WIDE : width + (i + 1) * WIDE]
        k_out[:, at] = dot(x[...], wk, NN).astype(BF16)
        wv = held[:, 2 * width + i * WIDE : 2 * width + (i + 1) * WIDE]
        v_out[:, at] = (dot(x[...], wv, NN) + bv[:, at]).astype(BF16)
    store.wait()


def split_pair(value, axis):
    index = lax.broadcasted_iota(jnp.int32, value.shape, axis)
    zero = jnp.zeros_like(value)
    return jnp.concatenate(
        [jnp.where(index < DH, value, zero), jnp.where(index < DH, zero, value)], axis=1 - axis
    )


def attend_kernel(info, q, k, v, att, p_long, p_short):
    part = p_long.shape[2] // 2
    long_len, short_len = p_long.shape[1], p_short.shape[1]
    places = (
        (slice(0, part), slice(0, long_len), info[LEN_LONG], p_long),
        (
            slice(part, part + short_len), slice(long_len, long_len + short_len),
            info[LEN_SHORT], p_short,
        ),
    )
    work = [
        (pair, slice(pair * PAIR, (pair + 1) * PAIR), *place)
        for place in places
        for pair in range(q.shape[1] // PAIR)
    ]
    held = [
        dot(k[k_at, at], split_pair(q[q_at, at].T, 0), NN) for _, at, q_at, k_at, _, _ in work
    ]
    lows = []
    for (pair, at, q_at, k_at, length, p_out), scores in zip(work, held):
        position = lax.broadcasted_iota(jnp.int32, scores.shape, 0)
        scores = jnp.where(position < length, scores, MASKED)
        highest = jnp.max(scores, axis=0, keepdims=True)
        exponent = jnp.exp(scores - highest)
        total = jnp.sum(exponent, axis=0, keepdims=True)
        low = (exponent * (1.0 / total)).astype(BF16)
        p_out[pair] = low
        lows.append(low)
    for (pair, at, q_at, k_at, length, p_out), low in zip(work, lows):
        count = q_at.stop - q_at.start
        out = dot(v[k_at, at].T, low, NN)
        out = jnp.concatenate([out[:DH, :count], out[DH:, count:]], axis=0)
        att[q_at, at] = out.T.astype(BF16)


def moments(residual):
    center = residual - jnp.mean(residual, axis=-1, keepdims=True)
    spread = jnp.mean(center * center, axis=-1, keepdims=True)
    inverse = lax.rsqrt(spread + EPSILON)
    return center * inverse, inverse


def pull_norm(scaled, unit, inverse):
    first = jnp.mean(scaled, axis=-1, keepdims=True)
    second = jnp.mean(scaled * unit, axis=-1, keepdims=True)
    return inverse * (scaled - first - unit * second)


def output_kernel(
    info, att, tokens_long, tokens_short, weights, bias, gain, shift,
    unit_out, inverse_out, feed_out, x, wo, sem,
):
    width = att.shape[1]
    short_len = tokens_short.shape[1]
    part = att.shape[0] - short_len
    copies = [
        pltpu.make_async_copy(weights.at[:, pl.ds(3 * width, width)], wo, sem.at[0]),
        pltpu.make_async_copy(
            tokens_long.at[info[SEQ], columns(info[HALF], part)], x.at[pl.ds(0, part)], sem.at[1]
        ),
        pltpu.make_async_copy(
            tokens_short.at[info[RANK]], x.at[pl.ds(part, short_len)], sem.at[2]
        ),
    ]
    for copy in copies:
        copy.start()
    for copy in copies:
        copy.wait()

    for i in range(width // WIDE):
        at = slice(i * WIDE, (i + 1) * WIDE)
        unit_out[:, at] = x[:, at].astype(F32) + dot(att[...], wo[:, at], NN) + bias[:, at]

    def rows(i, carry):
        at = columns(i, STRIP)
        unit, inverse = moments(unit_out[at, :])
        unit_out[at, :] = unit
        inverse_out[at, :] = jnp.broadcast_to(inverse, (STRIP, 128))
        feed_out[at, :] = (unit * gain[...] + shift[...]).astype(BF16)
        return carry

    lax.fori_loop(0, att.shape[0] // STRIP, rows, 0, unroll=2)


def gelu_pair(value):
    phi = 0.5 + 0.5 * lax.erf(value * math.sqrt(0.5))
    density = jnp.exp(value * value * -0.5) * (1.0 / math.sqrt(2.0 * math.pi))
    return value * phi, phi + value * density


NEAR = BLOCKS + 1
FAR = BLOCKS + 2


def load_feed(info, pieces, target, sem):
    split = [0, BLOCKS - 1] if len(pieces) == FAR else [BLOCKS - 1]
    copies = []

    def add(piece, where):
        copies.append(pltpu.make_async_copy(piece, where, sem.at[len(copies)]))

    at = 0
    for j in range(BLOCKS):
        if j in split:
            add(pieces[at], target.at[info[CORE], :, info[j]])
            add(pieces[at + 1], target.at[1 - info[CORE], :, info[j]])
            at += 2
        else:
            add(pieces[at], target.at[:, :, info[j]])
            at += 1
    return copies


def side_of(weights, b, side, at):
    value = weights[b, side, :, :, at]
    return value.reshape(value.shape[0] * value.shape[1], value.shape[2])


def feed_step(feed, weights, b, bias_row, slope_out, total):
    for i in range(feed.shape[1] // WIDE):
        at = slice(i * WIDE, (i + 1) * WIDE)
        value = dot(feed[...], side_of(weights, b, 0, at), NN) + bias_row[:, at]
        act, slope = gelu_pair(value)
        slope_out[:, at] = slope.astype(BF16)
        total[...] += dot(act.astype(BF16), side_of(weights, b, 1, at), NT)


def feed_kernel(info, feed, bias, *rest):
    pieces, (slope_out, total, weights, sem) = rest[:NEAR], rest[NEAR:]
    copies = load_feed(info, pieces, weights, sem)
    for copy in copies:
        copy.start()
    total[...] = jnp.zeros_like(total)
    for copy in copies:
        copy.wait()
    for b in range(2):
        feed_step(feed, weights, b, bias.at[pl.ds(b, 1)], slope_out.at[b], total)


def middle_kernel(
    info, feed, bias, before, slope_near, unit_one, inverse_one, gain_one, shift_one, bias_down,
    gain_two, shift_two, cot_long, cot_short, weights_w, *rest,
):
    pieces, rest = rest[: NEAR + FAR], rest[NEAR + FAR :]
    (
        layer_out, layer_short_out, hidden_out, delta_out, att_out, sums_out,
        total, low, slope_far, cot, slopes, held, wo, sem, small,
    ) = rest
    width = feed.shape[1]
    count = feed.shape[0]
    short_len = cot_short.shape[1]
    part = count - short_len
    loads = [
        load_feed(info, pieces[:NEAR], held.at[0], sem.at[0]),
        load_feed(info, pieces[NEAR:], held.at[1], sem.at[1]),
    ]
    near = pltpu.make_async_copy(slope_near, slopes, small.at[2])
    last = pltpu.make_async_copy(weights_w.at[:, pl.ds(3 * width, width)], wo, small.at[3])
    extra = [
        pltpu.make_async_copy(
            cot_long.at[info[SEQ], columns(info[HALF], part)], cot.at[pl.ds(0, part)], small.at[0]
        ),
        pltpu.make_async_copy(
            cot_short.at[info[RANK]], cot.at[pl.ds(part, short_len)], small.at[1]
        ),
    ]
    for copy in loads[1] + extra + [near] + loads[0] + [last]:
        copy.start()
    total[...] = before[...]
    for copy in loads[1]:
        copy.wait()
    for b in range(2):
        feed_step(feed, held.at[1], b, bias.at[pl.ds(b, 1)], slope_far.at[b], total)
    for copy in extra:
        copy.wait()
    sums_out[...] = jnp.zeros_like(sums_out)

    def second(i, carry, target, shift):
        to = columns(i, STRIP)
        at = pl.ds(pl.multiple_of(shift + i * STRIP, STRIP), STRIP)
        normed = unit_one[at, :] * gain_one[...] + shift_one[...]
        unit, inverse = moments(normed + (total[at, :] + bias_down[...]))
        target[to, :] = (unit * gain_two[...] + shift_two[...]).astype(BF16)
        g = cot[at, :].astype(F32)
        delta = pull_norm(g * gain_two[...], unit, inverse)
        total[at, :] = delta
        low[at, :] = delta.astype(BF16)
        sums_out[0:1, :] += jnp.sum(g, axis=0, keepdims=True)
        sums_out[1:2, :] += jnp.sum(delta, axis=0, keepdims=True)
        return carry

    for target, shift in ((layer_out, 0), (layer_short_out, part)):
        body = functools.partial(second, target=target, shift=shift)
        lax.fori_loop(0, target.shape[0] // STRIP, body, 0, unroll=2)
    near.wait()
    for b in (2, 3, 0, 1):
        if b == 0:
            for copy in loads[0]:
                copy.wait()
        weights = held.at[b // 2]
        for i in range(width // WIDE):
            at = slice(i * WIDE, (i + 1) * WIDE)
            slope = slopes[b, :, at] if b < 2 else slope_far[b - 2, :, at]
            grad = dot(low[...], side_of(weights, b % 2, 1, at), NN) * slope.astype(F32)
            hidden_out[b : b + 1, at] = jnp.sum(grad, axis=0, keepdims=True)
            total[...] += dot(grad.astype(BF16), side_of(weights, b % 2, 0, at), NT)

    def first(i, carry):
        at = columns(i, STRIP)
        grad = total[at, :]
        delta = pull_norm(grad * gain_one[...], unit_one[at, :], inverse_one[at, 0:1])
        delta_out[at, :] = delta
        low[at, :] = delta.astype(BF16)
        sums_out[2:3, :] += jnp.sum(grad, axis=0, keepdims=True)
        sums_out[3:4, :] += jnp.sum(delta, axis=0, keepdims=True)
        return carry

    lax.fori_loop(0, count // STRIP, first, 0, unroll=2)
    last.wait()
    att_out[...] = dot(low[...], wo[...], NT).astype(BF16)


def attend_back_kernel(info, q, k, v, grad, p_long, p_short,
                       dq_out, keep_out, send_out, short_out, sums_out, pool):
    part = p_long.shape[2] // 2
    long_len, short_len = p_long.shape[1], p_short.shape[1]
    scale = 1.0 / math.sqrt(DH)
    places = (
        (slice(0, part), slice(0, long_len), p_long, pool),
        (
            slice(part, part + short_len), slice(long_len, long_len + short_len),
            p_short, short_out,
        ),
    )
    work = [
        (pair, slice(pair * PAIR, (pair + 1) * PAIR), *place)
        for pair in range(q.shape[1] // PAIR)
        for place in places
    ]
    held = [
        dot(v[k_at, at], split_pair(grad[q_at, at].T, 0), NN) for _, at, q_at, k_at, _, _ in work
    ]
    steps = []
    for (pair, at, q_at, k_at, p_in, target), dp in zip(work, held):
        prob = p_in[pair].astype(F32)
        inner = jnp.sum(dp * prob, axis=0, keepdims=True)
        steps.append((prob * (dp - inner)).astype(BF16))
    sums_out[...] = jnp.zeros_like(sums_out)
    for (pair, at, q_at, k_at, p_in, target), ds in zip(work, steps):
        count = q_at.stop - q_at.start
        dv = dot(p_in[pair], split_pair(grad[q_at, at], 1), NN)
        dk = dot(ds, split_pair(q[q_at, at], 1), NN)
        dq = dot(k[k_at, at].T, ds, NN)
        dq = (jnp.concatenate([dq[:DH, :count], dq[DH:, count:]], axis=0) * scale).T
        dq_out[q_at, at] = dq.astype(BF16)
        target[0, :, at] = dk.astype(BF16)
        target[1, :, at] = dv.astype(BF16)
        sums_out[0:1, at] += jnp.sum(dq, axis=0, keepdims=True)
        sums_out[1:2, at] += jnp.sum(dv, axis=0, keepdims=True)
    keep_out[...] = pool[:, columns(info[HALF], part), :]
    send_out[...] = pool[:, columns(1 - info[HALF], part), :]


def early_kernel(delta_one, dq, short, weights_w, rest_out, short_out, wq, wkv, sem):
    part = rest_out.shape[0]
    width = dq.shape[1]
    loads = [
        pltpu.make_async_copy(weights_w.at[:, pl.ds(0, width)], wq, sem.at[0]),
        pltpu.make_async_copy(weights_w.at[:, pl.ds(width, 2 * width)], wkv, sem.at[1]),
    ]
    for load in loads:
        load.start()
    loads[0].wait()
    totals = []
    for i in range(width // WIDE):
        at = slice(i * WIDE, (i + 1) * WIDE)
        total = delta_one[:, at] + dot(dq[...], wq[at, :], NT)
        rest_out[:, at] = total[:part]
        totals.append(total[part:])
    loads[1].wait()
    for i in range(width // WIDE):
        at = slice(i * WIDE, (i + 1) * WIDE)
        total = totals[i] + dot(short[0], wkv[at, 0:width], NT)
        short_out[:, at] = (total + dot(short[1], wkv[at, width:], NT)).astype(BF16)


def late_kernel(rest, keep, received, weights_w, out, wkv, sem):
    width = rest.shape[1]
    load = pltpu.make_async_copy(weights_w.at[:, pl.ds(width, 2 * width)], wkv, sem.at[0])
    load.start()
    dk, dv = [
        (keep[side].astype(F32) + received[side].astype(F32)).astype(BF16) for side in range(2)
    ]
    load.wait()
    for i in range(width // WIDE):
        at = slice(i * WIDE, (i + 1) * WIDE)
        total = rest[:, at] + dot(dk, wkv[at, 0:width], NT)
        out[:, at] = (total + dot(dv, wkv[at, width:], NT)).astype(BF16)


def place_kernel(info, *rest):
    pieces, (long_out, short_out, sem) = rest[:-3], rest[-3:]
    rank = info[RANK]
    part = long_out.shape[0] * long_out.shape[1] // 4
    parts = long_out.shape[1] // part
    copies = []
    for flip in range(4):
        low = rank % 2 if flip % 2 == 0 else 1 - rank % 2
        high = rank // 2 if flip // 2 == 0 else 1 - rank // 2
        who = high * 2 + low
        long_rows, short_rows = pieces[flip], pieces[4 + flip]
        target = long_out.at[who // parts, columns(who % parts, part)]
        copies.append(pltpu.make_async_copy(long_rows, target, sem.at[2 * flip]))
        copies.append(pltpu.make_async_copy(short_rows, short_out.at[who], sem.at[2 * flip + 1]))
    for copy in copies:
        copy.start()
    for copy in copies:
        copy.wait()


def flip_pairs(size, bit):
    return [(i, i ^ bit) for i in range(size)]


def ring_of(size):
    return list(range(0, size, 2)) + list(range(size - 1, 0, -2))


def ring_move(dp, tensor):
    ring = ring_of(dp)
    pairs = []
    for i in range(dp):
        for t in range(tensor):
            to = ring[(i + 1) % dp] if t % 2 == 0 else ring[(i - 1) % dp]
            pairs.append((ring[i] * tensor + t, to * tensor + t))
    return lambda x: lax.ppermute(x, ("dp", "tensor"), pairs)


def tie(value, *after):
    return lax.optimization_barrier((value, *after))[0]


def scoped(name, move, x):
    with jax.named_scope(name):
        return move(x)


class Moves:
    def __init__(self, **start):
        self.held = dict(start)

    def __getitem__(self, names):
        return [self.held[n] for n in names.split()]

    def tie(self, value, names):
        return lax.optimization_barrier((value, *self[names]))[0]

    def go(self, name, source, move, after=""):
        value = self.held[source] if isinstance(source, str) else source
        if after:
            value = self.tie(value, after)
        with jax.named_scope(name):
            self.held[name] = move(value)


def block_places(size, core):
    if size != BLOCKS:
        return jnp.arange(BLOCKS, dtype=jnp.int32)
    ring = ring_of(size)
    place = [ring.index(d) for d in range(size)]
    table = []
    for sign in (-1, 1):
        steps = [0] + [sign * j for j in (1, 2, 3)] + [-sign * j for j in (1, 2, 3)] + [4]
        table.append([[ring[(place[d] + s) % size] for s in steps] for d in range(size)])
    return jnp.array(table, jnp.int32)[core, lax.axis_index("dp")]


def local(
    dp, tensor,
    tokens_long, tokens_short, lengths_long, lengths_short,
    weight_project, weight_output, weight_in, weight_down,
    bias_query, bias_value, bias_output, gain_one, shift_one, bias_hidden, bias_down,
    gain_two, shift_two, cotangent_long, cotangent_short,
):
    long_count, long_len, width = tokens_long.shape
    short_count, short_len, _ = tokens_short.shape
    parts = tensor // long_count
    assert tensor == 4 and parts == 2 and short_count == tensor
    part = long_len // parts
    rows = part + short_len
    keys = long_len + short_len
    units = weight_in.shape[1]

    rank = lax.axis_index("tensor")
    core, seq, half = rank % 2, rank // parts, rank % parts
    info = jnp.concatenate(
        [
            block_places(dp, core),
            jnp.stack(
                [core, seq, half, rank, lengths_long[seq], lengths_short[rank]]
            ).astype(jnp.int32),
        ]
    )
    core_pairs = flip_pairs(tensor, 1)
    far_pairs = flip_pairs(tensor, 2)

    def to_core(x):
        return lax.ppermute(x, "tensor", core_pairs)

    def to_far(x):
        return lax.ppermute(x, "tensor", far_pairs)

    def by_parity(mine, other):
        first = jnp.where(core == 0, mine, other)
        return jnp.stack([first, jnp.where(core == 0, other, mine)])

    def own_half(x, index):
        return lax.dynamic_slice_in_dim(x, index * (x.shape[0] // 2), x.shape[0] // 2, axis=0)

    both = jnp.concatenate([weight_project, weight_output], axis=1)
    f = jnp.stack([weight_in, weight_down.T])
    hidden_row = bias_hidden.reshape(1, units)
    if dp == BLOCKS:
        round_ring = ring_move(dp, tensor)
        s = Moves(w0=both, f=f, b=hidden_row)
        h = s.held
        s.go("c0", "f", to_core)
        s.go("w1", "w0", round_ring)
        s.go("by", "b", to_far)
        s.go("y0", "f", to_far)
        h["bb"] = jnp.concatenate(s["b by"], axis=0)
        h["f0"] = by_parity(f, h["c0"])
        s.go("f1", "f0", round_ring)
        s.go("bc", "bb", to_core)
        s.go("v1", "w1", to_core)
        s.go("w2", "w1", round_ring, "y0 by")
        s.go("d0", "y0", to_core)
        s.go("f2", "f1", round_ring, "bc")
        s.go("y1", "f1", to_far, "y0")
        s.go("w3", "w2", round_ring, "f1 v1 d0")
        s.go("c1", "f1", to_core)
        s.go("v2", "w2", to_core)
        s.go("f3", "f2", round_ring, "y1 c1")
        s.go("y2", "f2", to_far, "y1")
        s.go("w4", own_half(h["w3"], core), round_ring, "f2 v2")
        s.go("v3", "w3", to_core)
        s.go("f4", own_half(h["f3"], core)[0], round_ring, "y2")
        s.go("y3", "f3", to_far, "y2")
        s.go("v4", "w4", to_core)
        near_bias, across = s["bb bc"]
        blocks = s["w0 w1 w2 w3 v1 v2 v3 w4 v4"]
        blocks[0] = s.tie(blocks[0], "f3 y2")
    else:
        s = None

        def cut(whole, axis):
            return jnp.split(whole, BLOCKS, axis=axis)

        blocks = cut(lax.all_gather(both, "dp", axis=0, tiled=True), 0)
        last = blocks.pop()
        blocks += [own_half(last, core), own_half(last, 1 - core)]
        full = lax.all_gather(f, "dp", axis=1, tiled=True)
        full = by_parity(full, to_core(full))
        across = to_far(full)
        near = cut(full, 2)
        last = near.pop()
        near += [own_half(last, core)[0], own_half(last, 1 - core)[0]]
        far = cut(across, 2)
        first, last = far[0], far.pop()
        far = [own_half(first, core)[0], own_half(first, 1 - core)[0]] + far[1:]
        far += [own_half(last, core)[0], own_half(last, 1 - core)[0]]
        near_bias = jnp.concatenate([hidden_row, to_far(hidden_row)], axis=0)
        across = to_core(near_bias)
    bias_a, bias_b = [by_parity(near_bias[j], across[j]) for j in range(2)]

    def row(vector):
        return vector.reshape(1, width)

    def lanes(*lead):
        return pl.BlockSpec((*lead, GROUP * PAIR), lambda i: (0,) * len(lead) + (i,))

    def heads(*last):
        return pl.BlockSpec((GROUP, *last), lambda i: (i, 0, 0))

    q, k, v, weights = call(
        project_kernel,
        [((rows, width), BF16), ((keys, width), BF16), ((keys, width), BF16),
         ((width, 4 * width), BF16)],
        [info, tokens_long, tokens_short, *blocks, row(bias_query), row(bias_value)],
        [SMEM] + [ANY] * (BLOCKS + 3) + [VMEM] * 2,
        [pltpu.VMEM((keys, width), BF16), pltpu.VMEM((width, 4 * width), BF16),
         pltpu.SemaphoreType.DMA((BLOCKS + 4,))],
        2 * width * width * (rows + 2 * keys), 16 << 20,
        out_specs=[VMEM, VMEM, VMEM, ANY],
        vmem=PROJECT_MIB,
    )
    if s is not None:
        h["q"] = q
        for j in "234":
            s.go("c" + j, "f" + j, to_core, "q")
        for j in "12":
            s.go("d" + j, "y" + j, to_core, "q")
        near = s["f0 f1 f2 f3 c1 c2 c3 f4 c4"]
        q = s.tie(q, "f4")
    att, p_long, p_short = call(
        attend_kernel,
        [((rows, width), BF16), ((H // 2, long_len, 2 * part), BF16), ((H // 2, short_len, 2 * short_len), BF16)],
        [info, q, k, v],
        [SMEM, lanes(rows), lanes(keys), lanes(keys)],
        [],
        4 * width * (long_len * part + short_len * short_len), 8 << 20,
        exps=H * (long_len * part + short_len * short_len),
        out_specs=[lanes(rows), heads(long_len, 2 * part), heads(short_len, 2 * short_len)],
        vmem=ATTEND_MIB,
        grid=(H // (2 * GROUP),),
    )
    unit_one, inverse_one, feed = call(
        output_kernel,
        [((rows, width), F32), ((rows, 128), F32), ((rows, width), BF16)],
        [info, att, tokens_long, tokens_short, weights, row(bias_output), row(gain_one),
         row(shift_one)],
        [SMEM, VMEM, ANY, ANY, ANY, VMEM, VMEM, VMEM],
        [pltpu.VMEM((rows, width), BF16), pltpu.VMEM((width, width), BF16),
         pltpu.SemaphoreType.DMA((3,))],
        2 * width * width * rows, 6 << 20,
        vmem=OUTPUT_MIB,
    )
    if s is not None:
        h["feed"] = feed
        s.go("y4", "f4", to_far, "feed y3")
        s.go("d3", "y3", to_core, "feed")
        feed = s.tie(feed, "y3")
    slope_a, before = call(
        feed_kernel,
        [((2, rows, units), BF16), ((rows, width), F32)],
        [info, feed, bias_a, *near],
        [SMEM, VMEM, VMEM] + [ANY] * NEAR,
        [pltpu.VMEM((2, 2, BLOCKS, width // BLOCKS, units), BF16),
         pltpu.SemaphoreType.DMA((FAR,))],
        8 * width * units * rows, 12 << 20,
        vmem=FEED_MIB,
    )
    if s is not None:
        h["before"] = before
        s.go("d4", "y4", to_core, "before")
        far = s["y0 d0 y1 y2 y3 d1 d2 d3 y4 d4"]
    layer, layer_short_rows, hidden_sums, delta_one, grad_att, sums_a = call(
        middle_kernel,
        [((part, width), BF16), ((short_len, width), BF16), ((4, units), F32),
         ((rows, width), F32), ((rows, width), BF16), ((4, width), F32)],
        [info, feed, bias_b, before, slope_a, unit_one, inverse_one, row(gain_one), row(shift_one),
         row(bias_down), row(gain_two), row(shift_two), cotangent_long, cotangent_short, weights,
         *near, *far],
        [SMEM, VMEM, VMEM, VMEM, ANY] + [VMEM] * 7 + [ANY] * (3 + NEAR + FAR),
        [pltpu.VMEM((rows, width), F32), pltpu.VMEM((rows, width), BF16),
         pltpu.VMEM((2, rows, units), BF16), pltpu.VMEM((rows, width), BF16),
         pltpu.VMEM((2, rows, units), BF16), pltpu.VMEM((2, 2, 2, BLOCKS, width // BLOCKS, units), BF16),
         pltpu.VMEM((width, width), BF16), pltpu.SemaphoreType.DMA((2, FAR)), pltpu.SemaphoreType.DMA((4,))],
        26 * width * units * rows, 26 << 20,
        vmem=MIDDLE_MIB,
    )
    layer_far = scoped("layer_far", to_far, layer)
    layer_core = scoped("layer_core", to_core, layer)
    dq, keep, send, short, sums_c = call(
        attend_back_kernel,
        [((rows, width), BF16), ((2, part, width), BF16), ((2, part, width), BF16),
         ((2, short_len, width), BF16), ((2, width), F32)],
        [info, q, k, v, grad_att, p_long, p_short],
        [SMEM, lanes(rows), lanes(keys), lanes(keys), lanes(rows), heads(long_len, 2 * part),
         heads(short_len, 2 * short_len)],
        [pltpu.VMEM((2, long_len, GROUP * PAIR), BF16)],
        8 * width * (long_len * part + short_len * short_len), 12 << 20,
        out_specs=[lanes(rows), lanes(2, part), lanes(2, part), lanes(2, short_len), lanes(2)],
        vmem=BACK_MIB,
        grid=(H // (2 * GROUP),),
    )
    received = scoped("keys_core", to_core, send)
    vectors = jnp.concatenate([sums_a, sums_c], axis=0)
    count = vectors.shape[0]
    over = scoped("sums_far", to_far, jnp.concatenate([vectors, hidden_sums[2:]], axis=0))
    dq = tie(dq, layer_far, layer_core)
    rest, delta_near = call(
        early_kernel,
        [((part, width), F32), ((short_len, width), BF16)],
        [delta_one, dq, short, weights],
        [VMEM] * 3 + [ANY],
        [pltpu.VMEM((width, width), BF16), pltpu.VMEM((width, 2 * width), BF16),
         pltpu.SemaphoreType.DMA((2,))],
        2 * width * width * (rows + 2 * short_len), 10 << 20,
        vmem=EARLY_MIB,
    )
    layer_far_core = scoped("layer_far_core", to_core, tie(layer_far, rest))
    layer_short_far = scoped("layer_short_far", to_far, tie(layer_short_rows, rest))
    layer_short_core = scoped("layer_short_core", to_core, tie(layer_short_rows, rest))
    vectors = vectors + tie(over, rest)[:count]
    paired = hidden_sums[:2] + over[count:]
    kept, given = [
        lax.dynamic_slice_in_dim(paired, which, 1, axis=0) for which in (core, 1 - core)
    ]
    over = scoped("sums_core", to_core, jnp.concatenate([vectors, given], axis=0))
    vectors = jnp.concatenate([vectors, kept], axis=0) + over
    near_far = scoped("delta_near_far", to_far, delta_near)
    received = tie(received, layer_short_far, layer_short_core, layer_far_core, vectors)
    (delta_rows,) = call(
        late_kernel,
        [((part, width), BF16)],
        [rest, keep, received, weights],
        [VMEM] * 3 + [ANY],
        [pltpu.VMEM((width, 2 * width), BF16), pltpu.SemaphoreType.DMA((1,))],
        4 * width * width * part, 8 << 20,
        vmem=LATE_MIB,
    )
    rows_far = scoped("delta_far", to_far, delta_rows)
    vectors, near_far, layer_short_far, delta_near = lax.optimization_barrier(
        (vectors, near_far, layer_short_far, delta_near, delta_rows)
    )[:4]
    bit = 1
    while bit < dp:
        vectors = vectors + scoped(
            f"sums_{bit}", lambda x: lax.ppermute(x, "dp", flip_pairs(dp, bit)), vectors
        )
        bit *= 2

    def place(*pieces):
        return call(
            place_kernel,
            [((long_count, long_len, width), BF16), ((short_count, short_len, width), BF16)],
            [info, *pieces],
            [SMEM] + [VMEM] * len(pieces),
            [pltpu.SemaphoreType.DMA((8,))],
            0, 16 * rows * width,
            out_specs=[ANY, ANY],
            vmem=16,
        )

    layer_long, layer_short = place(
        layer, layer_core, layer_far, layer_far_core,
        layer_short_rows, layer_short_core, layer_short_far,
        scoped("layer_short_far_core", to_core, layer_short_far),
    )
    near_core = scoped("delta_near_core", to_core, delta_near)
    near_far_core = scoped("delta_near_far_core", to_core, near_far)
    rows_core = scoped("delta_core", to_core, delta_rows)
    rows_far = tie(rows_far, layer_long, vectors, near_core, near_far_core, rows_core)
    rows_far_core = scoped("delta_far_core", to_core, rows_far)
    delta_long, delta_short = place(
        delta_rows, rows_core, rows_far, rows_far_core,
        delta_near, near_core, near_far, near_far_core,
    )
    return (
        layer_long, layer_short, delta_long, delta_short,
        vectors[4], vectors[5], vectors[3], vectors[2],
        vectors[6], vectors[1], vectors[0],
    )


def solution(mesh):
    in_specs = (
        P("dp", None, None), P("dp", None, None), P("dp"), P("dp"),
        P("dp", None), P("dp", None), P("dp", "tensor"), P("tensor", "dp"),
        P(), P(), P(), P(), P(), P("tensor"), P(), P(), P(),
        P("dp", None, None), P("dp", None, None),
    )
    out_specs = (
        P("dp", None, None), P("dp", None, None), P("dp", None, None), P("dp", None, None),
        P(), P(), P(), P(), P("tensor"), P(), P(),
    )
    body = functools.partial(local, mesh.shape["dp"], mesh.shape["tensor"])
    return jax.shard_map(body, mesh=mesh, in_specs=in_specs, out_specs=out_specs, check_vma=False)
```

```python
import functools
import math

import jax
import jax.numpy as jnp
from jax import lax
from jax.experimental import pallas as pl
from jax.experimental.pallas import tpu as pltpu
from jax.sharding import PartitionSpec as P

H = 16
DH = 64
PAIR = 2 * DH
BLOCKS = 8
TILE = 256
WIDE = 512
STRIP = 32
GROUP = 2
PROJECT_MIB, ATTEND_MIB = 56, 56
MIDDLE_MIB, BACK_MIB, EARLY_MIB, LATE_MIB = 56, 56, 56, 56

EPSILON = 1e-05
MASKED = -1000000000.0
F32 = jnp.float32
BF16 = jnp.bfloat16

NN = (((1,), (0,)), ((), ()))
NT = (((1,), (1,)), ((), ()))
TN = (((0,), (0,)), ((), ()))

ANY = pl.BlockSpec(memory_space=pl.ANY)
VMEM = pl.BlockSpec(memory_space=pltpu.VMEM)
SMEM = pl.BlockSpec(memory_space=pltpu.SMEM)

CORE, SEQ, HALF, RANK, LEN_LONG, LEN_SHORT = range(BLOCKS, BLOCKS + 6)


def dot(a, b, dims):
    return lax.dot_general(a, b, dims, preferred_element_type=F32)


def call(body, outs, ins, in_specs, scratch, flops, nbytes, out_specs=None, vmem=56, exps=0,
         grid=()):
    if out_specs is None:
        out_specs = [VMEM] * len(outs)
    return pl.pallas_call(
        body,
        grid=grid,
        out_shape=[jax.ShapeDtypeStruct(s, d) for s, d in outs],
        in_specs=in_specs,
        out_specs=out_specs,
        scratch_shapes=scratch,
        compiler_params=pltpu.CompilerParams(vmem_limit_bytes=vmem << 20),
        cost_estimate=pl.CostEstimate(
            flops=int(flops), bytes_accessed=int(nbytes), transcendentals=int(exps)
        ),
        name=body.func.__name__ if isinstance(body, functools.partial) else body.__name__,
    )(*ins)


def columns(i, width):
    return pl.ds(pl.multiple_of(i * width, width), width)


def run_all(copies, what):
    for copy in copies:
        getattr(copy, what)()


def load_columns(info, blocks, chunk, target, sem):
    rows, width = blocks[0].shape[0], target.shape[1]
    places = [columns(info[j], rows) for j in range(BLOCKS - 1)]
    for half in (info[CORE], 1 - info[CORE]):
        places.append(columns(2 * info[BLOCKS - 1] + half, rows // 2))
    at = pl.ds(chunk * width, width)
    return [
        pltpu.make_async_copy(block.at[:, at], target.at[place], sem.at[j])
        for j, (block, place) in enumerate(zip(blocks, places))
    ]


def project_kernel(info, tokens_long, tokens_short, *rest):
    blocks, rest = rest[:BLOCKS + 1], rest[BLOCKS + 1 :]
    bq, bv, q_out, k_out, v_out, x, held, q, k, v, sem, small = rest
    width = bq.shape[1]
    long_len, short_len = tokens_long.shape[1], tokens_short.shape[1]
    part = q_out.shape[0] - short_len
    loads = [load_columns(info, blocks, c, held.at[c], sem.at[c]) for c in range(3)]
    tokens = [
        pltpu.make_async_copy(tokens_long.at[info[SEQ]], x.at[pl.ds(0, long_len)], small.at[0]),
        pltpu.make_async_copy(
            tokens_short.at[info[RANK]], x.at[pl.ds(long_len, short_len)], small.at[1]
        ),
    ]
    run_all(tokens, "start")
    for load in loads:
        run_all(load, "start")
    run_all(tokens, "wait")
    scale = 1.0 / math.sqrt(DH)
    mine_rows = columns(info[HALF], part)
    stores = []

    def store(source, target):
        stores.append(pltpu.make_async_copy(source, target, small.at[2 + len(stores)]))
        stores[-1].start()

    for chunk, (result, target) in enumerate(((q, q_out), (k, k_out), (v, v_out))):
        run_all(loads[chunk], "wait")
        for i in range(width // WIDE):
            at = slice(i * WIDE, (i + 1) * WIDE)
            w = held[chunk, :, at]
            if chunk == 0:
                for to, rows_at in ((slice(0, part), mine_rows), (slice(part, None), None)):
                    some = x[rows_at, :] if rows_at is not None else x[long_len:, :]
                    value = (dot(some, w, NN) + bq[:, at]).astype(BF16)
                    q[to, at] = (value * scale).astype(BF16)
            elif chunk == 1:
                k[:, at] = dot(x[...], w, NN).astype(BF16)
            else:
                v[:, at] = (dot(x[...], w, NN) + bv[:, at]).astype(BF16)
        store(result, target)
    run_all(stores, "wait")


def join_kernel(first, second, out):
    width = first.shape[1]
    out[:, :width] = first[...]
    out[:, width:] = second[...]


def split_pair(value, axis):
    index = lax.broadcasted_iota(jnp.int32, value.shape, axis)
    zero = jnp.zeros_like(value)
    return jnp.concatenate(
        [jnp.where(index < DH, value, zero), jnp.where(index < DH, zero, value)], axis=1 - axis
    )


def attend_kernel(
    info, q, k, v, bias, gain, shift, tokens_long, tokens_short, *rest
):
    blocks, rest = rest[:BLOCKS + 1], rest[BLOCKS + 1 :]
    p_long, p_short, unit_out, inverse_out, feed_out, w_out, att, x, matrix, sem, small = rest
    part = p_long.shape[2] // 2
    long_len, short_len = p_long.shape[1], p_short.shape[1]
    width = att.shape[1]
    step, steps = pl.program_id(0), pl.num_programs(0)
    copies = [
        pltpu.make_async_copy(
            tokens_long.at[info[SEQ], columns(info[HALF], part)],
            x.at[pl.ds(0, part)],
            small.at[0],
        ),
        pltpu.make_async_copy(
            tokens_short.at[info[RANK]], x.at[pl.ds(part, short_len)], small.at[1]
        ),
    ]
    for c in (3, 0, 1, 2):
        copies += load_columns(info, blocks, c, matrix.at[c], sem.at[c])
    stores = [pltpu.make_async_copy(matrix.at[c], w_out.at[c], small.at[2 + c]) for c in range(4)]

    @pl.when(step == 0)
    def _():
        run_all(copies, "start")

    @pl.when(step == steps // 2)
    def _():
        run_all(copies, "wait")
        run_all(stores, "start")

    places = (
        (slice(0, part), slice(0, long_len), info[LEN_LONG], p_long),
        (
            slice(part, part + short_len), slice(long_len, long_len + short_len),
            info[LEN_SHORT], p_short,
        ),
    )
    work = [
        (pair, slice(pair * PAIR, (pair + 1) * PAIR), *place)
        for place in places
        for pair in range(q.shape[1] // PAIR)
    ]
    held = [
        dot(k[k_at, at], split_pair(q[q_at, at].T, 0), NN) for _, at, q_at, k_at, _, _ in work
    ]
    lows = []
    for (pair, at, q_at, k_at, length, p_out), scores in zip(work, held):
        position = lax.broadcasted_iota(jnp.int32, scores.shape, 0)
        scores = jnp.where(position < length, scores, MASKED)
        highest = jnp.max(scores, axis=0, keepdims=True)
        exponent = jnp.exp(scores - highest)
        total = jnp.sum(exponent, axis=0, keepdims=True)
        low = (exponent * (1.0 / total)).astype(BF16)
        p_out[pair] = low
        lows.append(low)
    for (pair, at, q_at, k_at, length, p_out), low in zip(work, lows):
        count = q_at.stop - q_at.start
        out = dot(v[k_at, at].T, low, NN)
        out = jnp.concatenate([out[:DH, :count], out[DH:, count:]], axis=0)
        to = pl.ds(pl.multiple_of(step * q.shape[1] + at.start, PAIR), PAIR)
        att[q_at, to] = out.T.astype(BF16)

    @pl.when(step == steps - 1)
    def _():
        for i in range(width // WIDE):
            at = slice(i * WIDE, (i + 1) * WIDE)
            unit_out[:, at] = x[:, at].astype(F32) + dot(att[...], matrix[3, :, at], NN) + bias[:, at]

        def rows(i, carry):
            at = columns(i, STRIP)
            unit, inverse = moments(unit_out[at, :])
            unit_out[at, :] = unit
            inverse_out[at, :] = jnp.broadcast_to(inverse, (STRIP, 128))
            feed_out[at, :] = (unit * gain[...] + shift[...]).astype(BF16)
            return carry

        lax.fori_loop(0, att.shape[0] // STRIP, rows, 0, unroll=2)
        run_all(stores, "wait")


def moments(residual):
    center = residual - jnp.mean(residual, axis=-1, keepdims=True)
    spread = jnp.mean(center * center, axis=-1, keepdims=True)
    inverse = lax.rsqrt(spread + EPSILON)
    return center * inverse, inverse


def pull_norm(scaled, unit, inverse):
    first = jnp.mean(scaled, axis=-1, keepdims=True)
    second = jnp.mean(scaled * unit, axis=-1, keepdims=True)
    return inverse * (scaled - first - unit * second)


def gelu_pair(value):
    phi = 0.5 + 0.5 * lax.erf(value * math.sqrt(0.5))
    density = jnp.exp(value * value * -0.5) * (1.0 / math.sqrt(2.0 * math.pi))
    return value * phi, phi + value * density


NEAR_PLAN = [(j, None) for j in range(BLOCKS - 1)] + [(BLOCKS - 1, CORE), (BLOCKS - 1, -1)]
FAR_PLAN = (
    [(0, CORE), (0, -1), (1, None), (2, None), (3, 0), (3, 1)]
    + [(4, None), (5, None), (6, 0), (6, 1), (BLOCKS - 1, CORE), (BLOCKS - 1, -1)]
)
NEAR, FAR = len(NEAR_PLAN), len(FAR_PLAN)


def load_feed(info, plan, pieces, target, sem):
    copies = [[], []]
    for piece, (place, parity) in zip(pieces, plan):
        for which in range(2):
            if parity in (CORE, -1):
                own = info[CORE] if parity == CORE else 1 - info[CORE]
                source, where, late = piece, target.at[own, :, info[place]], 0
            elif parity is None:
                source, where, late = piece.at[which], target.at[which, :, info[place]], which
            else:
                source, where, late = piece, target.at[parity, :, info[place]], parity
            if parity is None or which == 0:
                at = len(copies[0]) + len(copies[1])
                copies[late].append(pltpu.make_async_copy(source, where, sem.at[at]))
    return copies


def side_of(weights, b, side, at):
    value = weights[b, side, :, :, at]
    return value.reshape(value.shape[0] * value.shape[1], value.shape[2])


def feed_step(feed, weights, b, bias_row, slope_out, total):
    for i in range(feed.shape[1] // WIDE):
        at = slice(i * WIDE, (i + 1) * WIDE)
        value = dot(feed[...], side_of(weights, b, 0, at), NN) + bias_row[:, at]
        act, slope = gelu_pair(value)
        slope_out[:, at] = slope.astype(BF16)
        total[...] += dot(act.astype(BF16), side_of(weights, b, 1, at), NT)


def middle_kernel(
    info, feed, bias, unit_one, inverse_one, gain_one, shift_one, bias_down, gain_two, shift_two,
    cot_long, cot_short, weights, *rest,
):
    pieces, rest = rest[: NEAR + FAR], rest[NEAR + FAR :]
    (
        layer_out, hidden_out, delta_out, att_out, sums_out,
        total, low, slopes, cot, held, wo, sem, small,
    ) = rest
    width = feed.shape[1]
    count = feed.shape[0]
    short_len = cot_short.shape[1]
    part = count - short_len
    loads = load_feed(info, NEAR_PLAN, pieces[:NEAR], held.at[pl.ds(0, 2)], sem.at[0])
    loads += load_feed(info, FAR_PLAN, pieces[NEAR:], held.at[pl.ds(2, 2)], sem.at[1])
    last = [pltpu.make_async_copy(weights.at[3], wo, small.at[0])]
    extra = [
        pltpu.make_async_copy(
            cot_long.at[info[SEQ], columns(info[HALF], part)],
            cot.at[pl.ds(0, part)],
            small.at[1],
        ),
        pltpu.make_async_copy(
            cot_short.at[info[RANK]], cot.at[pl.ds(part, short_len)], small.at[2]
        ),
    ]
    for load in loads:
        run_all(load, "start")
    run_all(extra + last, "start")
    total[...] = jnp.zeros_like(total)
    for b in range(4):
        run_all(loads[b], "wait")
        feed_step(feed, held, b, bias.at[pl.ds(b, 1)], slopes.at[b], total)
    run_all(extra, "wait")
    sums_out[...] = jnp.zeros_like(sums_out)

    def second(i, carry):
        at = columns(i, STRIP)
        normed = unit_one[at, :] * gain_one[...] + shift_one[...]
        unit, inverse = moments(normed + (total[at, :] + bias_down[...]))
        layer_out[at, :] = (unit * gain_two[...] + shift_two[...]).astype(BF16)
        g = cot[at, :].astype(F32)
        delta = pull_norm(g * gain_two[...], unit, inverse)
        total[at, :] = delta
        low[at, :] = delta.astype(BF16)
        sums_out[0:1, :] += jnp.sum(g, axis=0, keepdims=True)
        sums_out[1:2, :] += jnp.sum(delta, axis=0, keepdims=True)
        return carry

    lax.fori_loop(0, count // STRIP, second, 0, unroll=2)
    for b in range(4):
        for i in range(width // WIDE):
            at = slice(i * WIDE, (i + 1) * WIDE)
            grad = dot(low[...], side_of(held, b, 1, at), NN) * slopes[b, :, at].astype(F32)
            hidden_out[b : b + 1, at] = jnp.sum(grad, axis=0, keepdims=True)
            total[...] += dot(grad.astype(BF16), side_of(held, b, 0, at), NT)

    def first(i, carry):
        at = columns(i, STRIP)
        grad = total[at, :]
        delta = pull_norm(grad * gain_one[...], unit_one[at, :], inverse_one[at, 0:1])
        delta_out[at, :] = delta
        low[at, :] = delta.astype(BF16)
        sums_out[2:3, :] += jnp.sum(grad, axis=0, keepdims=True)
        sums_out[3:4, :] += jnp.sum(delta, axis=0, keepdims=True)
        return carry

    lax.fori_loop(0, count // STRIP, first, 0, unroll=2)
    run_all(last, "wait")
    att_out[...] = dot(low[...], wo[...], NT).astype(BF16)


def attend_back_kernel(info, q, k, v, grad, p_long, p_short,
                       dq_out, keep_out, send_out, short_out, sums_out, pool):
    part = p_long.shape[2] // 2
    long_len, short_len = p_long.shape[1], p_short.shape[1]
    scale = 1.0 / math.sqrt(DH)
    places = (
        (slice(0, part), slice(0, long_len), p_long, pool),
        (
            slice(part, part + short_len), slice(long_len, long_len + short_len),
            p_short, short_out,
        ),
    )
    work = [
        (pair, slice(pair * PAIR, (pair + 1) * PAIR), *place)
        for pair in range(q.shape[1] // PAIR)
        for place in places
    ]
    held = [
        dot(v[k_at, at], split_pair(grad[q_at, at].T, 0), NN) for _, at, q_at, k_at, _, _ in work
    ]
    steps = []
    for (pair, at, q_at, k_at, p_in, target), dp in zip(work, held):
        prob = p_in[pair].astype(F32)
        inner = jnp.sum(dp * prob, axis=0, keepdims=True)
        steps.append((prob * (dp - inner)).astype(BF16))
    sums_out[...] = jnp.zeros_like(sums_out)
    for (pair, at, q_at, k_at, p_in, target), ds in zip(work, steps):
        count = q_at.stop - q_at.start
        dv = dot(p_in[pair], split_pair(grad[q_at, at], 1), NN)
        dk = dot(ds, split_pair(q[q_at, at], 1), NN)
        dq = dot(k[k_at, at].T, ds, NN)
        dq = (jnp.concatenate([dq[:DH, :count], dq[DH:, count:]], axis=0) * scale).T
        dq_out[q_at, at] = dq.astype(BF16)
        target[0, :, at] = dk.astype(BF16)
        target[1, :, at] = dv.astype(BF16)
        sums_out[0:1, at] += jnp.sum(dq, axis=0, keepdims=True)
        sums_out[1:2, at] += jnp.sum(dv, axis=0, keepdims=True)
    keep_out[...] = pool[:, columns(info[HALF], part), :]
    send_out[...] = pool[:, columns(1 - info[HALF], part), :]


def early_kernel(
    delta_one, dq, short, weights, rest_out, short_out, delta, grad, near, w, small, sem
):
    part = rest_out.shape[0]
    width = w.shape[1]
    pairs = [(dq, grad), (delta_one, delta), (short, near)]
    loads = [pltpu.make_async_copy(a, b, small.at[i]) for i, (a, b) in enumerate(pairs)]
    parts = [[pltpu.make_async_copy(weights.at[c], w.at[c], sem.at[c])] for c in range(3)]
    run_all(loads[:1] + parts[0] + loads[1:] + parts[1] + parts[2], "start")
    run_all(loads[:2] + parts[0], "wait")
    totals = []
    for i in range(width // WIDE):
        at = slice(i * WIDE, (i + 1) * WIDE)
        total = delta[:, at] + dot(grad[...], w[0, at, :], NT)
        rest_out[:, at] = total[:part]
        totals.append(total[part:])
    run_all(loads[2:] + parts[1] + parts[2], "wait")
    for i in range(width // WIDE):
        at = slice(i * WIDE, (i + 1) * WIDE)
        total = totals[i] + dot(near[0], w[1, at, :], NT)
        short_out[:, at] = (total + dot(near[1], w[2, at, :], NT)).astype(BF16)


def late_kernel(
    rest_in, keep, received, weights, out, delta, mine, other, w, small, sem
):
    width = w.shape[1]
    pairs = [(keep, mine), (received, other), (rest_in, delta)]
    loads = [pltpu.make_async_copy(a, b, small.at[i]) for i, (a, b) in enumerate(pairs)]
    parts = [[pltpu.make_async_copy(weights.at[1 + c], w.at[c], sem.at[c])] for c in range(2)]
    run_all(loads[:2] + parts[0] + loads[2:] + parts[1], "start")
    run_all(loads[:2], "wait")
    dk, dv = [
        (mine[side].astype(F32) + other[side].astype(F32)).astype(BF16) for side in range(2)
    ]
    run_all(loads[2:] + parts[0], "wait")
    totals = []
    for i in range(width // WIDE):
        at = slice(i * WIDE, (i + 1) * WIDE)
        totals.append(delta[:, at] + dot(dk, w[0, at, :], NT))
    run_all(parts[1], "wait")
    for i in range(width // WIDE):
        at = slice(i * WIDE, (i + 1) * WIDE)
        out[:, at] = (totals[i] + dot(dv, w[1, at, :], NT)).astype(BF16)


def place_kernel(info, *rest):
    pieces, (long_out, short_out, sem) = rest[:-3], rest[-3:]
    rank = info[RANK]
    part = long_out.shape[0] * long_out.shape[1] // 4
    parts = long_out.shape[1] // part
    copies = []
    for flip in range(4):
        low = rank % 2 if flip % 2 == 0 else 1 - rank % 2
        high = rank // 2 if flip // 2 == 0 else 1 - rank // 2
        who = high * 2 + low
        if len(pieces) == 4:
            long_rows = pieces[flip].at[pl.ds(0, part)]
            short_rows = pieces[flip].at[pl.ds(part, short_out.shape[1])]
        else:
            long_rows, short_rows = pieces[flip], pieces[4 + flip]
        target = long_out.at[who // parts, columns(who % parts, part)]
        copies.append(pltpu.make_async_copy(long_rows, target, sem.at[2 * flip]))
        copies.append(pltpu.make_async_copy(short_rows, short_out.at[who], sem.at[2 * flip + 1]))
    for copy in copies:
        copy.start()
    for copy in copies:
        copy.wait()


def flip_pairs(size, bit):
    return [(i, i ^ bit) for i in range(size)]


def ring_of(size):
    return list(range(0, size, 2)) + list(range(size - 1, 0, -2))


def ring_move(dp, tensor):
    ring = ring_of(dp)
    pairs = []
    for i in range(dp):
        for t in range(tensor):
            to = ring[(i + 1) % dp] if t % 2 == 0 else ring[(i - 1) % dp]
            pairs.append((ring[i] * tensor + t, to * tensor + t))
    return lambda x: lax.ppermute(x, ("dp", "tensor"), pairs)


def tie(value, *after):
    return lax.optimization_barrier((value, *after))[0]


def scoped(name, move, x):
    with jax.named_scope(name):
        return move(x)


class Moves:
    def __init__(self, **start):
        self.held = dict(start)

    def __getitem__(self, names):
        return [self.held[n] for n in names]

    def tie(self, value, *names):
        return lax.optimization_barrier((value, *self[names]))[0]

    def go(self, name, source, move, *after):
        value = self.held[source] if isinstance(source, str) else source
        if after:
            value = self.tie(value, *after)
        with jax.named_scope(name):
            self.held[name] = move(value)


def block_places(size, core):
    if size != BLOCKS:
        return jnp.arange(BLOCKS, dtype=jnp.int32)
    ring = ring_of(size)
    place = [ring.index(d) for d in range(size)]
    table = []
    for sign in (-1, 1):
        steps = [0] + [sign * j for j in (1, 2, 3)] + [-sign * j for j in (1, 2, 3)] + [4]
        table.append([[ring[(place[d] + s) % size] for s in steps] for d in range(size)])
    return jnp.array(table, jnp.int32)[core, lax.axis_index("dp")]


def local(
    dp, tensor,
    tokens_long, tokens_short, lengths_long, lengths_short,
    weight_project, weight_output, weight_in, weight_down,
    bias_query, bias_value, bias_output, gain_one, shift_one, bias_hidden, bias_down,
    gain_two, shift_two, cotangent_long, cotangent_short,
):
    long_count, long_len, width = tokens_long.shape
    short_count, short_len, _ = tokens_short.shape
    parts = tensor // long_count
    assert tensor == 4 and parts == 2 and short_count == tensor
    part = long_len // parts
    rows = part + short_len
    keys = long_len + short_len
    units = weight_in.shape[1]

    rank = lax.axis_index("tensor")
    core, seq, half = rank % 2, rank // parts, rank % parts
    info = jnp.concatenate(
        [
            block_places(dp, core),
            jnp.stack(
                [core, seq, half, rank, lengths_long[seq], lengths_short[rank]]
            ).astype(jnp.int32),
        ]
    )
    core_pairs = flip_pairs(tensor, 1)
    far_pairs = flip_pairs(tensor, 2)

    def to_core(x):
        return lax.ppermute(x, "tensor", core_pairs)

    def to_far(x):
        return lax.ppermute(x, "tensor", far_pairs)

    def by_parity(mine, other):
        first = jnp.where(core == 0, mine, other)
        return jnp.stack([first, jnp.where(core == 0, other, mine)])

    def own_half(x, index):
        return lax.dynamic_slice_in_dim(x, index * (x.shape[0] // 2), x.shape[0] // 2, axis=0)

    (both,) = call(
        join_kernel,
        [((weight_project.shape[0], 4 * width), BF16)],
        [weight_project, weight_output],
        [VMEM] * 2,
        [],
        0, 4 << 20,
        vmem=16,
    )
    f = jnp.stack([weight_in, weight_down.T])
    hidden_row = bias_hidden.reshape(1, units)
    if dp == BLOCKS:
        round_ring = ring_move(dp, tensor)
        s = Moves(w0=both, f=f, b=hidden_row, info=info)
        h = s.held
        s.go("c0", "f", to_core)
        s.go("by", "b", to_far)
        s.go("y0", "f", to_far, "by")
        h["bb"] = jnp.concatenate(s["b", "by"], axis=0)
        s.go("bc", "bb", to_core)
        s.go("w1", "w0", round_ring)
        h["f0"] = by_parity(f, h["c0"])
        s.go("f1", "f0", round_ring)
        s.go("v1", "w1", to_core)
        s.go("w2", "w1", round_ring, "y0", "info")
        s.go("d0", "y0", to_core, "bc")
        s.go("f2", "f1", round_ring)
        s.go("y1", "f1", to_far, "y0")
        s.go("w3", "w2", round_ring, "f1", "v1", "d0")
        s.go("c1", "f1", to_core)
        s.go("v2", "w2", to_core)
        s.go("f3", "f2", round_ring, "y1", "c1")
        s.go("y2", "f2", to_far, "y1")
        s.go("w4", own_half(h["w3"], core), round_ring, "f2", "v2")
        s.go("v3", "w3", to_core)
        s.go("c2", "f2", to_core)
        s.go("d1", "y1", to_core)
        s.go("f4", own_half(h["f3"], core)[0], round_ring, "y2")
        s.go("y3a", h["f3"][0], to_far, "y2", "w3")
        s.go("y3b", h["y2"][1], round_ring, "v3")
        s.go("v4", "w4", to_core, "y2")
        blocks = s["w0", "w1", "w2", "w3", "v1", "v2", "v3", "w4", "v4"]
        blocks[0] = s.tie(blocks[0], "f3", "y2", "c2", "d1")
    else:
        s = None

        def cut(whole, axis):
            return jnp.split(whole, BLOCKS, axis=axis)

        blocks = cut(lax.all_gather(both, "dp", axis=0, tiled=True), 0)
        last = blocks.pop()
        blocks += [own_half(last, core), own_half(last, 1 - core)]
        full = lax.all_gather(f, "dp", axis=1, tiled=True)
        full = by_parity(full, to_core(full))
        across = to_far(full)
        near = cut(full, 2)
        last = near.pop()
        near += [own_half(last, core)[0], own_half(last, 1 - core)[0]]
        far = cut(across, 2)
        pick = {CORE: core, -1: 1 - core}
        far = [
            far[j] if parity is None else own_half(far[j], pick.get(parity, parity))[0]
            for j, parity in FAR_PLAN
        ]
        near_bias = jnp.concatenate([hidden_row, to_far(hidden_row)], axis=0)
        across = to_core(near_bias)

    def row(vector):
        return vector.reshape(1, width)

    def lanes(*lead):
        return pl.BlockSpec((*lead, GROUP * PAIR), lambda i: (0,) * len(lead) + (i,))

    def heads(*last):
        return pl.BlockSpec((GROUP, *last), lambda i: (i, 0, 0))

    q, k, v = call(
        project_kernel,
        [((rows, width), BF16), ((keys, width), BF16), ((keys, width), BF16)],
        [info, tokens_long, tokens_short, *blocks, row(bias_query), row(bias_value)],
        [SMEM] + [ANY] * (BLOCKS + 3) + [VMEM] * 2,
        [pltpu.VMEM((keys, width), BF16), pltpu.VMEM((3, width, width), BF16),
         pltpu.VMEM((rows, width), BF16), pltpu.VMEM((keys, width), BF16),
         pltpu.VMEM((keys, width), BF16), pltpu.SemaphoreType.DMA((3, BLOCKS + 1)),
         pltpu.SemaphoreType.DMA((5,))],
        2 * width * width * (rows + 2 * keys), 10 << 20,
        out_specs=[ANY] * 3,
        vmem=PROJECT_MIB,
    )
    if s is not None:
        h["q"] = q
        s.go("c3", "f3", to_core, "q")
        s.go("c4", "f4", to_core, "q")
        s.go("d2", "y2", to_core, "q")
        s.go("d3a", "y3a", to_core, "q")
        near = s["f0", "f1", "f2", "f3", "c1", "c2", "c3", "f4", "c4"]
        s.go("y4", jnp.where(core == 0, h["y3a"], h["y3b"]), round_ring, "q")
        q = s.tie(q, "y3a", "y3b", "f4")

    def whole(*shape):
        return pl.BlockSpec(shape, lambda i: (0,) * len(shape))

    p_long, p_short, unit_one, inverse_one, feed, weights = call(
        attend_kernel,
        [((H // 2, long_len, 2 * part), BF16), ((H // 2, short_len, 2 * short_len), BF16),
         ((rows, width), F32), ((rows, 128), F32), ((rows, width), BF16),
         ((4, width, width), BF16)],
        [info, q, k, v, row(bias_output), row(gain_one), row(shift_one), tokens_long,
         tokens_short, *blocks],
        [SMEM, lanes(rows), lanes(keys), lanes(keys)] + [whole(1, width)] * 3
        + [ANY] * (BLOCKS + 3),
        [pltpu.VMEM((rows, width), BF16), pltpu.VMEM((rows, width), BF16),
         pltpu.VMEM((4, width, width), BF16), pltpu.SemaphoreType.DMA((4, BLOCKS + 1)),
         pltpu.SemaphoreType.DMA((6,))],
        4 * width * (long_len * part + short_len * short_len) + 2 * width * width * rows, 14 << 20,
        exps=H * (long_len * part + short_len * short_len),
        out_specs=[heads(long_len, 2 * part), heads(short_len, 2 * short_len),
                   whole(rows, width), whole(rows, 128), whole(rows, width), ANY],
        vmem=ATTEND_MIB,
        grid=(H // (2 * GROUP),),
    )
    if s is not None:
        h["feed"] = feed
        s.go("d3b", "y3b", to_core, "feed")
        s.go("d4", "y4", to_core, "feed")
        near_bias, across = s["bb", "bc"]
        far = s["y0", "d0", "y1", "y2", "y3a", "y3b", "d1", "d2", "d3a", "d3b", "y4", "d4"]
    bias_rows = jnp.concatenate([by_parity(near_bias[j], across[j]) for j in range(2)], axis=0)
    layer, hidden_sums, delta_one, grad_att, sums_a = call(
        middle_kernel,
        [((rows, width), BF16), ((4, units), F32),
         ((rows, width), F32), ((rows, width), BF16), ((4, width), F32)],
        [info, feed, bias_rows, unit_one, inverse_one, row(gain_one), row(shift_one),
         row(bias_down), row(gain_two), row(shift_two), cotangent_long, cotangent_short, weights,
         *near, *far],
        [SMEM] + [VMEM] * 9 + [ANY] * (3 + NEAR + FAR),
        [pltpu.VMEM((rows, width), F32), pltpu.VMEM((rows, width), BF16),
         pltpu.VMEM((4, rows, units), BF16), pltpu.VMEM((rows, width), BF16),
         pltpu.VMEM((4, 2, BLOCKS, width // BLOCKS, units), BF16),
         pltpu.VMEM((width, width), BF16), pltpu.SemaphoreType.DMA((2, 2 * FAR)),
         pltpu.SemaphoreType.DMA((3,))],
        34 * width * units * rows, 26 << 20,
        vmem=MIDDLE_MIB,
    )
    layer_far = scoped("layer_far", to_far, layer)
    layer_core = scoped("layer_core", to_core, layer)
    dq, keep, send, short, sums_c = call(
        attend_back_kernel,
        [((rows, width), BF16), ((2, part, width), BF16), ((2, part, width), BF16),
         ((2, short_len, width), BF16), ((2, width), F32)],
        [info, q, k, v, grad_att, p_long, p_short],
        [SMEM, lanes(rows), lanes(keys), lanes(keys), lanes(rows), heads(long_len, 2 * part),
         heads(short_len, 2 * short_len)],
        [pltpu.VMEM((2, long_len, GROUP * PAIR), BF16)],
        8 * width * (long_len * part + short_len * short_len), 12 << 20,
        out_specs=[lanes(rows), lanes(2, part), lanes(2, part), lanes(2, short_len), lanes(2)],
        vmem=BACK_MIB,
        grid=(H // (2 * GROUP),),
    )
    received = scoped("keys_core", to_core, send)
    vectors = jnp.concatenate([sums_a, sums_c], axis=0)
    count = vectors.shape[0]
    paired = hidden_sums.reshape(2, 2, units)
    kept, given = [
        lax.dynamic_index_in_dim(paired, which, axis=1, keepdims=False) for which in (core, 1 - core)
    ]
    over = scoped("sums_core", to_core, jnp.concatenate([vectors, given], axis=0))
    rest, delta_near = call(
        early_kernel,
        [((part, width), F32), ((short_len, width), BF16)],
        [delta_one, tie(dq, layer_core), short, weights],
        [ANY] * 4,
        [pltpu.VMEM((rows, width), F32), pltpu.VMEM((rows, width), BF16),
         pltpu.VMEM((2, short_len, width), BF16), pltpu.VMEM((3, width, width), BF16),
         pltpu.SemaphoreType.DMA((3,)), pltpu.SemaphoreType.DMA((3,))],
        2 * width * width * (rows + 2 * short_len), 10 << 20,
        vmem=EARLY_MIB,
    )
    over = tie(over, rest)
    vectors, kept = vectors + over[:count], kept + over[count:]
    over = scoped("sums_far", to_far, jnp.concatenate([vectors, kept[1:]], axis=0))
    near_far = scoped("delta_near_far", to_far, delta_near)
    near_core = scoped("delta_near_core", to_core, delta_near)
    (delta_rows,) = call(
        late_kernel,
        [((part, width), BF16)],
        [rest, keep, tie(received, layer_far, near_core), weights],
        [ANY] * 4,
        [pltpu.VMEM((part, width), F32), pltpu.VMEM((2, part, width), BF16),
         pltpu.VMEM((2, part, width), BF16), pltpu.VMEM((2, width, width), BF16),
         pltpu.SemaphoreType.DMA((3,)), pltpu.SemaphoreType.DMA((2,))],
        4 * width * width * part, 8 << 20,
        vmem=LATE_MIB,
    )
    rows_far = scoped("delta_far", to_far, delta_rows)
    over, near_far, layer_far, delta_near = lax.optimization_barrier(
        (over, near_far, layer_far, delta_near, delta_rows)
    )[:4]
    vectors = jnp.concatenate([vectors, kept[:1]], axis=0) + over
    bit = 1
    while bit < dp:
        vectors = vectors + scoped(
            f"sums_{bit}", lambda x: lax.ppermute(x, "dp", flip_pairs(dp, bit)), vectors
        )
        bit *= 2

    def place(*pieces):
        return call(
            place_kernel,
            [((long_count, long_len, width), BF16), ((short_count, short_len, width), BF16)],
            [info, *pieces],
            [SMEM] + [VMEM] * len(pieces),
            [pltpu.SemaphoreType.DMA((8,))],
            0, 16 * rows * width,
            out_specs=[ANY, ANY],
            vmem=16,
        )

    layer_long, layer_short = place(
        layer, layer_core, layer_far, scoped("layer_far_core", to_core, layer_far)
    )
    near_far_core = scoped("delta_near_far_core", to_core, near_far)
    rows_core = scoped("delta_core", to_core, delta_rows)
    rows_far = tie(rows_far, layer_long, vectors, near_core, near_far_core, rows_core)
    rows_far_core = scoped("delta_far_core", to_core, rows_far)
    delta_long, delta_short = place(
        delta_rows, rows_core, rows_far, rows_far_core,
        delta_near, near_core, near_far, near_far_core,
    )
    return (
        layer_long, layer_short, delta_long, delta_short,
        vectors[4], vectors[5], vectors[3], vectors[2],
        vectors[6], vectors[1], vectors[0],
    )


def solution(mesh):
    in_specs = (
        P("dp", None, None), P("dp", None, None), P("dp"), P("dp"),
        P("dp", None), P("dp", None), P("dp", "tensor"), P("tensor", "dp"),
        P(), P(), P(), P(), P(), P("tensor"), P(), P(), P(),
        P("dp", None, None), P("dp", None, None),
    )
    out_specs = (
        P("dp", None, None), P("dp", None, None), P("dp", None, None), P("dp", None, None),
        P(), P(), P(), P(), P("tensor"), P(), P(),
    )
    body = functools.partial(local, mesh.shape["dp"], mesh.shape["tensor"])
    return jax.shard_map(body, mesh=mesh, in_specs=in_specs, out_specs=out_specs, check_vma=False)
```

```python
import functools
import math

import jax
import jax.numpy as jnp
from jax import lax
from jax.experimental import pallas as pl
from jax.experimental.pallas import tpu as pltpu
from jax.sharding import PartitionSpec as P

H = 16
DH = 64
PAIR = 2 * DH
BLOCKS = 8
TILE = 256
WIDE = 1024
STRIP = 128
GROUP = 2
PROJECT_MIB, ATTEND_MIB = 56, 56
MIDDLE_MIB, BACK_MIB, LATE_MIB = 56, 56, 56

EPSILON = 1e-05
MASKED = -1000000000.0
F32 = jnp.float32
BF16 = jnp.bfloat16

NN = (((1,), (0,)), ((), ()))
NT = (((1,), (1,)), ((), ()))
TN = (((0,), (0,)), ((), ()))

ANY = pl.BlockSpec(memory_space=pl.ANY)
VMEM = pl.BlockSpec(memory_space=pltpu.VMEM)
SMEM = pl.BlockSpec(memory_space=pltpu.SMEM)

CORE, SEQ, HALF, RANK, LEN_LONG, LEN_SHORT = range(BLOCKS, BLOCKS + 6)


def dot(a, b, dims):
    return lax.dot_general(a, b, dims, preferred_element_type=F32)


def call(body, outs, ins, in_specs, scratch, flops, nbytes, out_specs=None, vmem=56, exps=0,
         grid=()):
    if out_specs is None:
        out_specs = [VMEM] * len(outs)
    return pl.pallas_call(
        body,
        grid=grid,
        out_shape=[jax.ShapeDtypeStruct(s, d) for s, d in outs],
        in_specs=in_specs,
        out_specs=out_specs,
        scratch_shapes=scratch,
        compiler_params=pltpu.CompilerParams(vmem_limit_bytes=vmem << 20),
        cost_estimate=pl.CostEstimate(
            flops=int(flops), bytes_accessed=int(nbytes), transcendentals=int(exps)
        ),
        name=body.func.__name__ if isinstance(body, functools.partial) else body.__name__,
    )(*ins)


def columns(i, width):
    return pl.ds(pl.multiple_of(i * width, width), width)


def run_all(copies, what):
    for copy in copies:
        getattr(copy, what)()


def load_columns(info, blocks, chunk, target, sem):
    rows, width = blocks[0].shape[0], target.shape[1]
    places = [columns(info[j], rows) for j in range(BLOCKS - 1)]
    for half in (info[CORE], 1 - info[CORE]):
        places.append(columns(2 * info[BLOCKS - 1] + half, rows // 2))
    at = pl.ds(chunk * width, width)
    return [
        pltpu.make_async_copy(block.at[:, at], target.at[place], sem.at[j])
        for j, (block, place) in enumerate(zip(blocks, places))
    ]


def project_kernel(info, tokens_long, tokens_short, *rest):
    blocks, rest = rest[:BLOCKS + 1], rest[BLOCKS + 1 :]
    bq, bv, q_out, k_out, v_out, w_out, x, own, held, q, k, v, sem, small = rest
    width = bq.shape[1]
    long_len, short_len = tokens_long.shape[1], tokens_short.shape[1]
    part = q_out.shape[0] - short_len
    loads = [load_columns(info, blocks, c, held.at[c], sem.at[c]) for c in range(3)]
    long_rows, short_rows = tokens_long.at[info[SEQ]], tokens_short.at[info[RANK]]
    pairs = [
        (long_rows.at[columns(info[HALF], part)], own.at[pl.ds(0, part)]),
        (short_rows, own.at[pl.ds(part, short_len)]),
        (long_rows, x.at[pl.ds(0, long_len)]),
        (short_rows, x.at[pl.ds(long_len, short_len)]),
    ]
    tokens = [pltpu.make_async_copy(a, b, small.at[i]) for i, (a, b) in enumerate(pairs)]
    run_all(tokens[:2] + loads[0] + tokens[2:] + loads[1] + loads[2], "start")
    scale = 1.0 / math.sqrt(DH)
    stores = []

    def store(source, target):
        stores.append(pltpu.make_async_copy(source, target, small.at[4 + len(stores)]))
        stores[-1].start()

    for chunk, (result, target) in enumerate(((q, q_out), (k, k_out), (v, v_out))):
        run_all((tokens[:2] if chunk == 0 else tokens[2:] if chunk == 1 else []) + loads[chunk], "wait")
        for i in range(width // WIDE):
            at = slice(i * WIDE, (i + 1) * WIDE)
            w = held[chunk, :, at]
            if chunk == 0:
                q[:, at] = ((dot(own[...], w, NN) + bq[:, at]).astype(BF16) * scale).astype(BF16)
            elif chunk == 1:
                k[:, at] = dot(x[...], w, NN).astype(BF16)
            else:
                v[:, at] = (dot(x[...], w, NN) + bv[:, at]).astype(BF16)
        store(result, target)
        store(held.at[chunk], w_out.at[chunk])
    run_all(stores, "wait")


def join_kernel(first, second, out):
    width = first.shape[1]
    out[:, :width] = first[...]
    out[:, width:] = second[...]


def split_pair(value, axis):
    index = lax.broadcasted_iota(jnp.int32, value.shape, axis)
    zero = jnp.zeros_like(value)
    return jnp.concatenate(
        [jnp.where(index < DH, value, zero), jnp.where(index < DH, zero, value)], axis=1 - axis
    )


def attend_kernel(
    info, q, k, v, bias, gain, shift, tokens_long, tokens_short, *rest
):
    blocks, rest = rest[:BLOCKS + 1], rest[BLOCKS + 1 :]
    p_long, p_short, unit_out, inverse_out, feed_out, att, x, wo, sem, small = rest
    part = p_long.shape[2] // 2
    long_len, short_len = p_long.shape[1], p_short.shape[1]
    width = att.shape[1]
    step, steps = pl.program_id(0), pl.num_programs(0)
    copies = [
        pltpu.make_async_copy(
            tokens_long.at[info[SEQ], columns(info[HALF], part)],
            x.at[pl.ds(0, part)],
            small.at[0],
        ),
        pltpu.make_async_copy(
            tokens_short.at[info[RANK]], x.at[pl.ds(part, short_len)], small.at[1]
        ),
    ]
    copies += load_columns(info, blocks, 3, wo, sem)

    @pl.when(step == 0)
    def _():
        run_all(copies, "start")

    places = (
        (slice(0, part), slice(0, long_len), info[LEN_LONG], p_long),
        (
            slice(part, part + short_len), slice(long_len, long_len + short_len),
            info[LEN_SHORT], p_short,
        ),
    )
    work = [
        (pair, slice(pair * PAIR, (pair + 1) * PAIR), *place)
        for place in places
        for pair in range(q.shape[1] // PAIR)
    ]
    held = [
        dot(k[k_at, at], split_pair(q[q_at, at].T, 0), NN) for _, at, q_at, k_at, _, _ in work
    ]
    lows = []
    for (pair, at, q_at, k_at, length, p_out), scores in zip(work, held):
        position = lax.broadcasted_iota(jnp.int32, scores.shape, 0)
        scores = jnp.where(position < length, scores, MASKED)
        highest = jnp.max(scores, axis=0, keepdims=True)
        exponent = jnp.exp(scores - highest)
        total = jnp.sum(exponent, axis=0, keepdims=True)
        low = (exponent * (1.0 / total)).astype(BF16)
        p_out[pair] = low
        lows.append(low)
    for (pair, at, q_at, k_at, length, p_out), low in zip(work, lows):
        count = q_at.stop - q_at.start
        out = dot(v[k_at, at].T, low, NN)
        out = jnp.concatenate([out[:DH, :count], out[DH:, count:]], axis=0)
        to = pl.ds(pl.multiple_of(step * q.shape[1] + at.start, PAIR), PAIR)
        att[q_at, to] = out.T.astype(BF16)

    @pl.when(step == steps - 1)
    def _():
        run_all(copies, "wait")
        for i in range(width // WIDE):
            at = slice(i * WIDE, (i + 1) * WIDE)
            unit_out[:, at] = x[:, at].astype(F32) + dot(att[...], wo[:, at], NN) + bias[:, at]

        def rows(i, carry):
            at = columns(i, STRIP)
            unit, inverse = moments(unit_out[at, :])
            unit_out[at, :] = unit
            inverse_out[at, :] = jnp.broadcast_to(inverse, (STRIP, 128))
            feed_out[at, :] = (unit * gain[...] + shift[...]).astype(BF16)
            return carry

        lax.fori_loop(0, att.shape[0] // STRIP, rows, 0)


def moments(residual):
    center = residual - jnp.mean(residual, axis=-1, keepdims=True)
    spread = jnp.mean(center * center, axis=-1, keepdims=True)
    inverse = lax.rsqrt(spread + EPSILON)
    return center * inverse, inverse


def pull_norm(scaled, unit, inverse):
    first = jnp.mean(scaled, axis=-1, keepdims=True)
    second = jnp.mean(scaled * unit, axis=-1, keepdims=True)
    return inverse * (scaled - first - unit * second)


def gelu_pair(value):
    phi = 0.5 + 0.5 * lax.erf(value * math.sqrt(0.5))
    density = jnp.exp(value * value * -0.5) * (1.0 / math.sqrt(2.0 * math.pi))
    return value * phi, phi + value * density


NEAR_PLAN = [(j, None) for j in range(BLOCKS - 1)] + [(BLOCKS - 1, CORE), (BLOCKS - 1, -1)]
FAR_PLAN = (
    [(0, CORE), (0, -1), (1, None), (2, None), (3, 0), (3, 1)]
    + [(4, None), (5, None), (6, 0), (6, 1), (BLOCKS - 1, CORE), (BLOCKS - 1, -1)]
)
NEAR, FAR = len(NEAR_PLAN), len(FAR_PLAN)


def load_feed(info, plan, pieces, target, sem):
    copies = [[], []]
    for piece, (place, parity) in zip(pieces, plan):
        for which in range(2):
            if parity in (CORE, -1):
                own = info[CORE] if parity == CORE else 1 - info[CORE]
                source, where, late = piece, target.at[own, :, info[place]], 0
            elif parity is None:
                source, where, late = piece.at[which], target.at[which, :, info[place]], which
            else:
                source, where, late = piece, target.at[parity, :, info[place]], parity
            if parity is None or which == 0:
                at = len(copies[0]) + len(copies[1])
                copies[late].append(pltpu.make_async_copy(source, where, sem.at[at]))
    return copies


def side_of(weights, b, side, at):
    value = weights[b, side, :, :, at]
    return value.reshape(value.shape[0] * value.shape[1], value.shape[2])


def feed_step(feed, weights, b, bias_row, slope_out, total):
    for i in range(feed.shape[1] // WIDE):
        at = slice(i * WIDE, (i + 1) * WIDE)
        value = dot(feed[...], side_of(weights, b, 0, at), NN) + bias_row[:, at]
        act, slope = gelu_pair(value)
        slope_out[:, at] = slope.astype(BF16)
        total[...] += dot(act.astype(BF16), side_of(weights, b, 1, at), NT)


def middle_kernel(
    info, feed, bias, unit_one, inverse_one, gain_one, shift_one, bias_down, gain_two, shift_two,
    cot_long, cot_short, *rest,
):
    blocks, rest = rest[:BLOCKS + 1], rest[BLOCKS + 1 :]
    pieces, rest = rest[: NEAR + FAR], rest[NEAR + FAR :]
    (
        layer_out, hidden_out, delta_out, att_out, sums_out,
        total, low, slopes, cot, held, wo, sem, small,
    ) = rest
    width = feed.shape[1]
    count = feed.shape[0]
    short_len = cot_short.shape[1]
    part = count - short_len
    loads = load_feed(info, NEAR_PLAN, pieces[:NEAR], held.at[pl.ds(0, 2)], sem.at[0])
    loads += load_feed(info, FAR_PLAN, pieces[NEAR:], held.at[pl.ds(2, 2)], sem.at[1])
    last = load_columns(info, blocks, 3, wo, small)
    extra = [
        pltpu.make_async_copy(
            cot_long.at[info[SEQ], columns(info[HALF], part)],
            cot.at[pl.ds(0, part)],
            small.at[BLOCKS + 1],
        ),
        pltpu.make_async_copy(
            cot_short.at[info[RANK]], cot.at[pl.ds(part, short_len)], small.at[BLOCKS + 2]
        ),
    ]
    for load in loads:
        run_all(load, "start")
    run_all(extra + last, "start")
    total[...] = jnp.zeros_like(total)
    for b in range(4):
        run_all(loads[b], "wait")
        feed_step(feed, held, b, bias.at[pl.ds(b, 1)], slopes.at[b], total)
    run_all(extra, "wait")
    sums_out[...] = jnp.zeros_like(sums_out)

    def second(i, carry):
        at = columns(i, STRIP)
        normed = unit_one[at, :] * gain_one[...] + shift_one[...]
        unit, inverse = moments(normed + (total[at, :] + bias_down[...]))
        layer_out[at, :] = (unit * gain_two[...] + shift_two[...]).astype(BF16)
        g = cot[at, :].astype(F32)
        delta = pull_norm(g * gain_two[...], unit, inverse)
        total[at, :] = delta
        low[at, :] = delta.astype(BF16)
        sums_out[0:1, :] += jnp.sum(g, axis=0, keepdims=True)
        sums_out[1:2, :] += jnp.sum(delta, axis=0, keepdims=True)
        return carry

    lax.fori_loop(0, count // STRIP, second, 0)
    for b in range(4):
        for i in range(width // WIDE):
            at = slice(i * WIDE, (i + 1) * WIDE)
            grad = dot(low[...], side_of(held, b, 1, at), NN) * slopes[b, :, at].astype(F32)
            hidden_out[b : b + 1, at] = jnp.sum(grad, axis=0, keepdims=True)
            total[...] += dot(grad.astype(BF16), side_of(held, b, 0, at), NT)

    def first(i, carry):
        at = columns(i, STRIP)
        grad = total[at, :]
        delta = pull_norm(grad * gain_one[...], unit_one[at, :], inverse_one[at, 0:1])
        delta_out[at, :] = delta
        low[at, :] = delta.astype(BF16)
        sums_out[2:3, :] += jnp.sum(grad, axis=0, keepdims=True)
        sums_out[3:4, :] += jnp.sum(delta, axis=0, keepdims=True)
        return carry

    lax.fori_loop(0, count // STRIP, first, 0)
    run_all(last, "wait")
    att_out[...] = dot(low[...], wo[...], NT).astype(BF16)


def attend_back_kernel(
    info, q, k, v, grad, p_long, p_short, delta_one, weights,
    keep_out, send_out, sums_out, rest_out, near_out, pool, near_pool, dq_all, short, delta, w, sem,
):
    part = p_long.shape[2] // 2
    long_len, short_len = p_long.shape[1], p_short.shape[1]
    width = dq_all.shape[1]
    step, steps = pl.program_id(0), pl.num_programs(0)
    loads = [pltpu.make_async_copy(weights.at[c], w.at[c], sem.at[c]) for c in range(3)]
    loads.append(pltpu.make_async_copy(delta_one, delta, sem.at[3]))

    @pl.when(step == 0)
    def _():
        run_all(loads, "start")

    scale = 1.0 / math.sqrt(DH)
    places = (
        (slice(0, part), slice(0, long_len), p_long, pool),
        (
            slice(part, part + short_len), slice(long_len, long_len + short_len),
            p_short, near_pool,
        ),
    )
    work = [
        (pair, slice(pair * PAIR, (pair + 1) * PAIR), *place)
        for pair in range(q.shape[1] // PAIR)
        for place in places
    ]
    held = [
        dot(v[k_at, at], split_pair(grad[q_at, at].T, 0), NN) for _, at, q_at, k_at, _, _ in work
    ]
    rounded = []
    for (pair, at, q_at, k_at, p_in, target), dp in zip(work, held):
        prob = p_in[pair].astype(F32)
        inner = jnp.sum(dp * prob, axis=0, keepdims=True)
        rounded.append((prob * (dp - inner)).astype(BF16))
    sums_out[...] = jnp.zeros_like(sums_out)
    for (pair, at, q_at, k_at, p_in, target), ds in zip(work, rounded):
        count = q_at.stop - q_at.start
        dv = dot(p_in[pair], split_pair(grad[q_at, at], 1), NN)
        dk = dot(ds, split_pair(q[q_at, at], 1), NN)
        dq = dot(k[k_at, at].T, ds, NN)
        dq = (jnp.concatenate([dq[:DH, :count], dq[DH:, count:]], axis=0) * scale).T
        to = pl.ds(pl.multiple_of(step * q.shape[1] + at.start, PAIR), PAIR)
        dq_all[q_at, to] = dq.astype(BF16)
        target[0, :, at] = dk.astype(BF16)
        target[1, :, at] = dv.astype(BF16)
        sums_out[0:1, at] += jnp.sum(dq, axis=0, keepdims=True)
        sums_out[1:2, at] += jnp.sum(dv, axis=0, keepdims=True)
    keep_out[...] = pool[:, columns(info[HALF], part), :]
    send_out[...] = pool[:, columns(1 - info[HALF], part), :]
    short[:, :, columns(step, q.shape[1])] = near_pool[...]

    @pl.when(step == steps - 1)
    def _():
        run_all(loads, "wait")
        for i in range(width // WIDE):
            at = slice(i * WIDE, (i + 1) * WIDE)
            total = delta[:, at] + dot(dq_all[...], w[0, at, :], NT)
            rest_out[:, at] = total[:part]
            total = total[part:] + dot(short[0], w[1, at, :], NT)
            near_out[:, at] = (total + dot(short[1], w[2, at, :], NT)).astype(BF16)


def late_kernel(
    rest_in, keep, received, weights, out, delta, mine, other, w, small, sem
):
    width = w.shape[1]
    pairs = [(keep, mine), (received, other), (rest_in, delta)]
    loads = [pltpu.make_async_copy(a, b, small.at[i]) for i, (a, b) in enumerate(pairs)]
    parts = [[pltpu.make_async_copy(weights.at[1 + c], w.at[c], sem.at[c])] for c in range(2)]
    run_all(loads[:2] + parts[0] + loads[2:] + parts[1], "start")
    run_all(loads[:2], "wait")
    dk, dv = [
        (mine[side].astype(F32) + other[side].astype(F32)).astype(BF16) for side in range(2)
    ]
    run_all(loads[2:] + parts[0], "wait")
    totals = []
    for i in range(width // WIDE):
        at = slice(i * WIDE, (i + 1) * WIDE)
        totals.append(delta[:, at] + dot(dk, w[0, at, :], NT))
    run_all(parts[1], "wait")
    for i in range(width // WIDE):
        at = slice(i * WIDE, (i + 1) * WIDE)
        out[:, at] = (totals[i] + dot(dv, w[1, at, :], NT)).astype(BF16)


def place_kernel(info, *rest):
    pieces, (long_out, short_out, sem) = rest[:-3], rest[-3:]
    rank = info[RANK]
    part = long_out.shape[0] * long_out.shape[1] // 4
    parts = long_out.shape[1] // part
    copies = []
    for flip in range(4):
        low = rank % 2 if flip % 2 == 0 else 1 - rank % 2
        high = rank // 2 if flip // 2 == 0 else 1 - rank // 2
        who = high * 2 + low
        if len(pieces) == 4:
            long_rows = pieces[flip].at[pl.ds(0, part)]
            short_rows = pieces[flip].at[pl.ds(part, short_out.shape[1])]
        else:
            long_rows, short_rows = pieces[flip], pieces[4 + flip]
        target = long_out.at[who // parts, columns(who % parts, part)]
        copies.append(pltpu.make_async_copy(long_rows, target, sem.at[2 * flip]))
        copies.append(pltpu.make_async_copy(short_rows, short_out.at[who], sem.at[2 * flip + 1]))
    for copy in copies:
        copy.start()
    for copy in copies:
        copy.wait()


def flip_pairs(size, bit):
    return [(i, i ^ bit) for i in range(size)]


def ring_of(size):
    return list(range(0, size, 2)) + list(range(size - 1, 0, -2))


def ring_move(dp, tensor):
    ring = ring_of(dp)
    pairs = []
    for i in range(dp):
        for t in range(tensor):
            to = ring[(i + 1) % dp] if t % 2 == 0 else ring[(i - 1) % dp]
            pairs.append((ring[i] * tensor + t, to * tensor + t))
    return lambda x: lax.ppermute(x, ("dp", "tensor"), pairs)


def tie(value, *after):
    return lax.optimization_barrier((value, *after))[0]


def scoped(name, move, x):
    with jax.named_scope(name):
        return move(x)


class Moves:
    def __init__(self, **start):
        self.held = dict(start)

    def __getitem__(self, names):
        return [self.held[n] for n in names]

    def tie(self, value, *names):
        return lax.optimization_barrier((value, *self[names]))[0]

    def go(self, name, source, move, *after):
        value = self.held[source] if isinstance(source, str) else source
        if after:
            value = self.tie(value, *after)
        with jax.named_scope(name):
            self.held[name] = move(value)


def block_places(size, core):
    if size != BLOCKS:
        return jnp.arange(BLOCKS, dtype=jnp.int32)
    ring = ring_of(size)
    place = [ring.index(d) for d in range(size)]
    table = []
    for sign in (-1, 1):
        steps = [0] + [sign * j for j in (1, 2, 3)] + [-sign * j for j in (1, 2, 3)] + [4]
        table.append([[ring[(place[d] + s) % size] for s in steps] for d in range(size)])
    return jnp.array(table, jnp.int32)[core, lax.axis_index("dp")]


def local(
    dp, tensor,
    tokens_long, tokens_short, lengths_long, lengths_short,
    weight_project, weight_output, weight_in, weight_down,
    bias_query, bias_value, bias_output, gain_one, shift_one, bias_hidden, bias_down,
    gain_two, shift_two, cotangent_long, cotangent_short,
):
    long_count, long_len, width = tokens_long.shape
    short_count, short_len, _ = tokens_short.shape
    parts = tensor // long_count
    assert tensor == 4 and parts == 2 and short_count == tensor
    part = long_len // parts
    rows = part + short_len
    keys = long_len + short_len
    units = weight_in.shape[1]

    rank = lax.axis_index("tensor")
    core, seq, half = rank % 2, rank // parts, rank % parts
    info = jnp.concatenate(
        [
            block_places(dp, core),
            jnp.stack(
                [core, seq, half, rank, lengths_long[seq], lengths_short[rank]]
            ).astype(jnp.int32),
        ]
    )
    core_pairs = flip_pairs(tensor, 1)
    far_pairs = flip_pairs(tensor, 2)

    def to_core(x):
        return lax.ppermute(x, "tensor", core_pairs)

    def to_far(x):
        return lax.ppermute(x, "tensor", far_pairs)

    def by_parity(mine, other):
        first = jnp.where(core == 0, mine, other)
        return jnp.stack([first, jnp.where(core == 0, other, mine)])

    def own_half(x, index):
        return lax.dynamic_slice_in_dim(x, index * (x.shape[0] // 2), x.shape[0] // 2, axis=0)

    (both,) = call(
        join_kernel,
        [((weight_project.shape[0], 4 * width), BF16)],
        [weight_project, weight_output],
        [VMEM] * 2,
        [],
        0, 4 << 20,
        vmem=16,
    )
    f = jnp.stack([weight_in, weight_down.T])
    hidden_row = bias_hidden.reshape(1, units)
    if dp == BLOCKS:
        round_ring = ring_move(dp, tensor)
        s = Moves(w0=both, f=f, b=hidden_row, info=info)
        h = s.held
        s.go("c0", "f", to_core)
        s.go("by", "b", to_far)
        s.go("y0", "f", to_far, "by")
        h["bb"] = jnp.concatenate(s["b", "by"], axis=0)
        s.go("bc", "bb", to_core)
        s.go("w1", "w0", round_ring)
        h["f0"] = by_parity(f, h["c0"])
        s.go("f1", "f0", round_ring)
        s.go("v1", "w1", to_core)
        s.go("w2", "w1", round_ring, "y0", "info")
        s.go("d0", "y0", to_core, "bc")
        s.go("f2", "f1", round_ring)
        s.go("y1", "f1", to_far, "y0")
        s.go("w3", "w2", round_ring, "f1", "v1", "d0")
        s.go("c1", "f1", to_core)
        s.go("v2", "w2", to_core)
        s.go("f3", "f2", round_ring, "y1", "c1")
        s.go("y2", "f2", to_far, "y1")
        s.go("w4", own_half(h["w3"], core), round_ring, "f2", "v2")
        s.go("v3", "w3", to_core)
        s.go("c2", "f2", to_core)
        s.go("d1", "y1", to_core)
        s.go("f4", own_half(h["f3"], core)[0], round_ring, "y2")
        s.go("y3a", h["f3"][0], to_far, "y2", "w3")
        s.go("y3b", h["y2"][1], round_ring, "v3")
        s.go("v4", "w4", to_core, "y2")
        blocks = s["w0", "w1", "w2", "w3", "v1", "v2", "v3", "w4", "v4"]
        blocks[0] = s.tie(blocks[0], "f3", "y2", "c2", "d1")
    else:
        s = None

        def cut(whole, axis):
            return jnp.split(whole, BLOCKS, axis=axis)

        blocks = cut(lax.all_gather(both, "dp", axis=0, tiled=True), 0)
        last = blocks.pop()
        blocks += [own_half(last, core), own_half(last, 1 - core)]
        full = lax.all_gather(f, "dp", axis=1, tiled=True)
        full = by_parity(full, to_core(full))
        across = to_far(full)
        near = cut(full, 2)
        last = near.pop()
        near += [own_half(last, core)[0], own_half(last, 1 - core)[0]]
        far = cut(across, 2)
        pick = {CORE: core, -1: 1 - core}
        far = [
            far[j] if parity is None else own_half(far[j], pick.get(parity, parity))[0]
            for j, parity in FAR_PLAN
        ]
        near_bias = jnp.concatenate([hidden_row, to_far(hidden_row)], axis=0)
        across = to_core(near_bias)

    def row(vector):
        return vector.reshape(1, width)

    def lanes(*lead):
        return pl.BlockSpec((*lead, GROUP * PAIR), lambda i: (0,) * len(lead) + (i,))

    def heads(*last):
        return pl.BlockSpec((GROUP, *last), lambda i: (i, 0, 0))

    q, k, v, weights = call(
        project_kernel,
        [((rows, width), BF16), ((keys, width), BF16), ((keys, width), BF16),
         ((3, width, width), BF16)],
        [info, tokens_long, tokens_short, *blocks, row(bias_query), row(bias_value)],
        [SMEM] + [ANY] * (BLOCKS + 3) + [VMEM] * 2,
        [pltpu.VMEM((keys, width), BF16), pltpu.VMEM((rows, width), BF16),
         pltpu.VMEM((3, width, width), BF16),
         pltpu.VMEM((rows, width), BF16), pltpu.VMEM((keys, width), BF16),
         pltpu.VMEM((keys, width), BF16), pltpu.SemaphoreType.DMA((3, BLOCKS + 1)),
         pltpu.SemaphoreType.DMA((10,))],
        2 * width * width * (rows + 2 * keys), 10 << 20,
        out_specs=[ANY] * 4,
        vmem=PROJECT_MIB,
    )
    if s is not None:
        h["q"] = q
        s.go("c3", "f3", to_core, "q")
        s.go("c4", "f4", to_core, "q")
        s.go("d2", "y2", to_core, "q")
        s.go("d3a", "y3a", to_core, "q")
        near = s["f0", "f1", "f2", "f3", "c1", "c2", "c3", "f4", "c4"]
        s.go("y4", jnp.where(core == 0, h["y3a"], h["y3b"]), round_ring, "q")
        q = s.tie(q, "y3a", "y3b", "f4")

    def whole(*shape):
        return pl.BlockSpec(shape, lambda i: (0,) * len(shape))

    p_long, p_short, unit_one, inverse_one, feed = call(
        attend_kernel,
        [((H // 2, long_len, 2 * part), BF16), ((H // 2, short_len, 2 * short_len), BF16),
         ((rows, width), F32), ((rows, 128), F32), ((rows, width), BF16)],
        [info, q, k, v, row(bias_output), row(gain_one), row(shift_one), tokens_long,
         tokens_short, *blocks],
        [SMEM, lanes(rows), lanes(keys), lanes(keys)] + [whole(1, width)] * 3
        + [ANY] * (BLOCKS + 3),
        [pltpu.VMEM((rows, width), BF16), pltpu.VMEM((rows, width), BF16),
         pltpu.VMEM((width, width), BF16), pltpu.SemaphoreType.DMA((BLOCKS + 1,)),
         pltpu.SemaphoreType.DMA((2,))],
        4 * width * (long_len * part + short_len * short_len) + 2 * width * width * rows, 14 << 20,
        exps=H * (long_len * part + short_len * short_len),
        out_specs=[heads(long_len, 2 * part), heads(short_len, 2 * short_len),
                   whole(rows, width), whole(rows, 128), whole(rows, width)],
        vmem=ATTEND_MIB,
        grid=(H // (2 * GROUP),),
    )
    if s is not None:
        h["feed"] = feed
        s.go("d3b", "y3b", to_core, "feed")
        s.go("d4", "y4", to_core, "feed")
        near_bias, across = s["bb", "bc"]
        far = s["y0", "d0", "y1", "y2", "y3a", "y3b", "d1", "d2", "d3a", "d3b", "y4", "d4"]
    bias_rows = jnp.concatenate([by_parity(near_bias[j], across[j]) for j in range(2)], axis=0)
    layer, hidden_sums, delta_one, grad_att, sums_a = call(
        middle_kernel,
        [((rows, width), BF16), ((4, units), F32),
         ((rows, width), F32), ((rows, width), BF16), ((4, width), F32)],
        [info, feed, bias_rows, unit_one, inverse_one, row(gain_one), row(shift_one),
         row(bias_down), row(gain_two), row(shift_two), cotangent_long, cotangent_short, *blocks,
         *near, *far],
        [SMEM] + [VMEM] * 9 + [ANY] * (3 + BLOCKS + NEAR + FAR),
        [pltpu.VMEM((rows, width), F32), pltpu.VMEM((rows, width), BF16),
         pltpu.VMEM((4, rows, units), BF16), pltpu.VMEM((rows, width), BF16),
         pltpu.VMEM((4, 2, BLOCKS, width // BLOCKS, units), BF16),
         pltpu.VMEM((width, width), BF16), pltpu.SemaphoreType.DMA((2, 2 * FAR)),
         pltpu.SemaphoreType.DMA((BLOCKS + 3,))],
        34 * width * units * rows, 26 << 20,
        vmem=MIDDLE_MIB,
    )
    layer_far = scoped("layer_far", to_far, layer)
    layer_core = scoped("layer_core", to_core, layer)
    keep, send, sums_c, rest, delta_near = call(
        attend_back_kernel,
        [((2, part, width), BF16), ((2, part, width), BF16), ((2, width), F32),
         ((part, width), F32), ((short_len, width), BF16)],
        [info, q, k, v, grad_att, p_long, p_short, delta_one, weights],
        [SMEM, lanes(rows), lanes(keys), lanes(keys), lanes(rows), heads(long_len, 2 * part),
         heads(short_len, 2 * short_len), ANY, ANY],
        [pltpu.VMEM((2, long_len, GROUP * PAIR), BF16),
         pltpu.VMEM((2, short_len, GROUP * PAIR), BF16), pltpu.VMEM((rows, width), BF16),
         pltpu.VMEM((2, short_len, width), BF16), pltpu.VMEM((rows, width), F32),
         pltpu.VMEM((3, width, width), BF16), pltpu.SemaphoreType.DMA((4,))],
        8 * width * (long_len * part + short_len * short_len)
        + 2 * width * width * (rows + 2 * short_len), 20 << 20,
        out_specs=[lanes(2, part), lanes(2, part), lanes(2), whole(part, width),
                   whole(short_len, width)],
        vmem=BACK_MIB,
        grid=(H // (2 * GROUP),),
    )
    received = scoped("keys_core", to_core, send)
    vectors = jnp.concatenate([sums_a, sums_c], axis=0)
    count = vectors.shape[0]
    paired = hidden_sums.reshape(2, 2, units)
    kept, given = [
        lax.dynamic_index_in_dim(paired, which, axis=1, keepdims=False) for which in (core, 1 - core)
    ]
    over = jnp.concatenate([vectors, given], axis=0)
    over = scoped("sums_core", to_core, tie(over, layer_core))
    vectors, kept = vectors + over[:count], kept + over[count:]
    over = scoped("sums_far", to_far, jnp.concatenate([vectors, kept[1:]], axis=0))
    near_far = scoped("delta_near_far", to_far, tie(delta_near, layer_far))
    near_core = scoped("delta_near_core", to_core, delta_near)
    (delta_rows,) = call(
        late_kernel,
        [((part, width), BF16)],
        [rest, keep, tie(received, layer_far, layer_core, near_core), weights],
        [ANY] * 4,
        [pltpu.VMEM((part, width), F32), pltpu.VMEM((2, part, width), BF16),
         pltpu.VMEM((2, part, width), BF16), pltpu.VMEM((2, width, width), BF16),
         pltpu.SemaphoreType.DMA((3,)), pltpu.SemaphoreType.DMA((2,))],
        4 * width * width * part, 8 << 20,
        vmem=LATE_MIB,
    )
    rows_far = scoped("delta_far", to_far, delta_rows)
    over, near_far, layer_far, delta_near = lax.optimization_barrier(
        (over, near_far, layer_far, delta_near, delta_rows)
    )[:4]
    vectors = jnp.concatenate([vectors, kept[:1]], axis=0) + over
    bit = 1
    while bit < dp:
        vectors = vectors + scoped(
            f"sums_{bit}", lambda x: lax.ppermute(x, "dp", flip_pairs(dp, bit)), vectors
        )
        bit *= 2

    def place(*pieces):
        return call(
            place_kernel,
            [((long_count, long_len, width), BF16), ((short_count, short_len, width), BF16)],
            [info, *pieces],
            [SMEM] + [VMEM] * len(pieces),
            [pltpu.SemaphoreType.DMA((8,))],
            0, 16 * rows * width,
            out_specs=[ANY, ANY],
            vmem=16,
        )

    layer_long, layer_short = place(
        layer, layer_core, layer_far, scoped("layer_far_core", to_core, layer_far)
    )
    near_far_core = scoped("delta_near_far_core", to_core, near_far)
    rows_core = scoped("delta_core", to_core, delta_rows)
    rows_far = tie(rows_far, layer_long, vectors, near_core, near_far_core, rows_core)
    rows_far_core = scoped("delta_far_core", to_core, rows_far)
    delta_long, delta_short = place(
        delta_rows, rows_core, rows_far, rows_far_core,
        delta_near, near_core, near_far, near_far_core,
    )
    return (
        layer_long, layer_short, delta_long, delta_short,
        vectors[4], vectors[5], vectors[3], vectors[2],
        vectors[6], vectors[1], vectors[0],
    )


def solution(mesh):
    in_specs = (
        P("dp", None, None), P("dp", None, None), P("dp"), P("dp"),
        P("dp", None), P("dp", None), P("dp", "tensor"), P("tensor", "dp"),
        P(), P(), P(), P(), P(), P("tensor"), P(), P(), P(),
        P("dp", None, None), P("dp", None, None),
    )
    out_specs = (
        P("dp", None, None), P("dp", None, None), P("dp", None, None), P("dp", None, None),
        P(), P(), P(), P(), P("tensor"), P(), P(),
    )
    body = functools.partial(local, mesh.shape["dp"], mesh.shape["tensor"])
    return jax.shard_map(body, mesh=mesh, in_specs=in_specs, out_specs=out_specs, check_vma=False)
```

```python
import functools
import math

import jax
import jax.numpy as jnp
from jax import lax
from jax.experimental import pallas as pl
from jax.experimental.pallas import tpu as pltpu
from jax.sharding import PartitionSpec as P

H = 16
DH = 64
PAIR = 2 * DH
BLOCKS = 8
TILE = 256
WIDE = 1024
STRIP = 192
GROUP = 4
PROJECT_MIB, ATTEND_MIB = 56, 56
MIDDLE_MIB, BACK_MIB, LATE_MIB = 56, 56, 56

EPSILON = 1e-05
MASKED = -1000000000.0
F32 = jnp.float32
BF16 = jnp.bfloat16

NN = (((1,), (0,)), ((), ()))
NT = (((1,), (1,)), ((), ()))
TN = (((0,), (0,)), ((), ()))

ANY = pl.BlockSpec(memory_space=pl.ANY)
VMEM = pl.BlockSpec(memory_space=pltpu.VMEM)
SMEM = pl.BlockSpec(memory_space=pltpu.SMEM)

CORE, SEQ, HALF, RANK, LEN_LONG, LEN_SHORT = range(BLOCKS, BLOCKS + 6)


def dot(a, b, dims):
    return lax.dot_general(a, b, dims, preferred_element_type=F32)


def call(body, outs, ins, in_specs, scratch, flops, nbytes, out_specs=None, vmem=56, exps=0,
         grid=()):
    if out_specs is None:
        out_specs = [VMEM] * len(outs)
    return pl.pallas_call(
        body,
        grid=grid,
        out_shape=[jax.ShapeDtypeStruct(s, d) for s, d in outs],
        in_specs=in_specs,
        out_specs=out_specs,
        scratch_shapes=scratch,
        compiler_params=pltpu.CompilerParams(vmem_limit_bytes=vmem << 20),
        cost_estimate=pl.CostEstimate(
            flops=int(flops), bytes_accessed=int(nbytes), transcendentals=int(exps)
        ),
        name=body.func.__name__ if isinstance(body, functools.partial) else body.__name__,
    )(*ins)


def columns(i, width):
    return pl.ds(pl.multiple_of(i * width, width), width)


def run_all(copies, what):
    for copy in copies:
        getattr(copy, what)()


def load_columns(info, blocks, chunk, target, sem):
    rows, width = blocks[0].shape[0], target.shape[1]
    places = [columns(info[j], rows) for j in range(BLOCKS - 1)]
    for half in (info[CORE], 1 - info[CORE]):
        places.append(columns(2 * info[BLOCKS - 1] + half, rows // 2))
    at = pl.ds(chunk * width, width)
    return [
        pltpu.make_async_copy(block.at[:, at], target.at[place], sem.at[j])
        for j, (block, place) in enumerate(zip(blocks, places))
    ]


def project_kernel(info, tokens_long, tokens_short, *rest):
    blocks, rest = rest[:BLOCKS + 1], rest[BLOCKS + 1 :]
    bq, bv, q_out, k_out, v_out, w_out, x, own, held, q, k, v, sem, small = rest
    width = bq.shape[1]
    long_len, short_len = tokens_long.shape[1], tokens_short.shape[1]
    part = q_out.shape[0] - short_len
    loads = [load_columns(info, blocks, c, held.at[c], sem.at[c]) for c in range(3)]
    long_rows, short_rows = tokens_long.at[info[SEQ]], tokens_short.at[info[RANK]]
    pairs = [
        (long_rows.at[columns(info[HALF], part)], own.at[pl.ds(0, part)]),
        (short_rows, own.at[pl.ds(part, short_len)]),
        (long_rows, x.at[pl.ds(0, long_len)]),
        (short_rows, x.at[pl.ds(long_len, short_len)]),
    ]
    tokens = [pltpu.make_async_copy(a, b, small.at[i]) for i, (a, b) in enumerate(pairs)]
    run_all(tokens[:2] + loads[0] + tokens[2:] + loads[1] + loads[2], "start")
    scale = 1.0 / math.sqrt(DH)
    stores = []

    def store(source, target):
        stores.append(pltpu.make_async_copy(source, target, small.at[4 + len(stores)]))
        stores[-1].start()

    for chunk, (result, target) in enumerate(((q, q_out), (k, k_out), (v, v_out))):
        run_all((tokens[:2] if chunk == 0 else tokens[2:] if chunk == 1 else []) + loads[chunk], "wait")
        for i in range(width // WIDE):
            at = slice(i * WIDE, (i + 1) * WIDE)
            w = held[chunk, :, at]
            if chunk == 0:
                q[:, at] = ((dot(own[...], w, NN) + bq[:, at]).astype(BF16) * scale).astype(BF16)
            elif chunk == 1:
                k[:, at] = dot(x[...], w, NN).astype(BF16)
            else:
                v[:, at] = (dot(x[...], w, NN) + bv[:, at]).astype(BF16)
        store(result, target)
        store(held.at[chunk], w_out.at[chunk])
    run_all(stores, "wait")


def join_kernel(first, second, out):
    width = first.shape[1]
    out[:, :width] = first[...]
    out[:, width:] = second[...]


def split_pair(value, axis):
    index = lax.broadcasted_iota(jnp.int32, value.shape, axis)
    zero = jnp.zeros_like(value)
    return jnp.concatenate(
        [jnp.where(index < DH, value, zero), jnp.where(index < DH, zero, value)], axis=1 - axis
    )


def attend_kernel(
    info, q, k, v, bias, gain, shift, tokens_long, tokens_short, *rest
):
    blocks, rest = rest[:BLOCKS + 1], rest[BLOCKS + 1 :]
    p_long, p_short, unit_out, inverse_out, feed_out, att, x, wo, sem, small = rest
    part = p_long.shape[2] // 2
    long_len, short_len = p_long.shape[1], p_short.shape[1]
    width = att.shape[1]
    step, steps = pl.program_id(0), pl.num_programs(0)
    copies = [
        pltpu.make_async_copy(
            tokens_long.at[info[SEQ], columns(info[HALF], part)],
            x.at[pl.ds(0, part)],
            small.at[0],
        ),
        pltpu.make_async_copy(
            tokens_short.at[info[RANK]], x.at[pl.ds(part, short_len)], small.at[1]
        ),
    ]
    copies += load_columns(info, blocks, 3, wo, sem)

    @pl.when(step == 0)
    def _():
        run_all(copies, "start")

    places = (
        (slice(0, part), slice(0, long_len), info[LEN_LONG], p_long),
        (
            slice(part, part + short_len), slice(long_len, long_len + short_len),
            info[LEN_SHORT], p_short,
        ),
    )
    work = [
        (pair, slice(pair * PAIR, (pair + 1) * PAIR), *place)
        for place in places
        for pair in range(q.shape[1] // PAIR)
    ]
    held = [
        dot(k[k_at, at], split_pair(q[q_at, at].T, 0), NN) for _, at, q_at, k_at, _, _ in work
    ]
    lows = []
    for (pair, at, q_at, k_at, length, p_out), scores in zip(work, held):
        position = lax.broadcasted_iota(jnp.int32, scores.shape, 0)
        scores = jnp.where(position < length, scores, MASKED)
        highest = jnp.max(scores, axis=0, keepdims=True)
        exponent = jnp.exp(scores - highest)
        total = jnp.sum(exponent, axis=0, keepdims=True)
        low = (exponent * (1.0 / total)).astype(BF16)
        p_out[pair] = low
        lows.append(low)
    for (pair, at, q_at, k_at, length, p_out), low in zip(work, lows):
        count = q_at.stop - q_at.start
        out = dot(v[k_at, at].T, low, NN)
        out = jnp.concatenate([out[:DH, :count], out[DH:, count:]], axis=0)
        to = pl.ds(pl.multiple_of(step * q.shape[1] + at.start, PAIR), PAIR)
        att[q_at, to] = out.T.astype(BF16)

    @pl.when(step == steps - 1)
    def _():
        run_all(copies, "wait")
        for i in range(width // WIDE):
            at = slice(i * WIDE, (i + 1) * WIDE)
            unit_out[:, at] = x[:, at].astype(F32) + dot(att[...], wo[:, at], NN) + bias[:, at]

        def rows(i, carry):
            at = columns(i, STRIP)
            unit, inverse = moments(unit_out[at, :])
            unit_out[at, :] = unit
            inverse_out[at, :] = jnp.broadcast_to(inverse, (STRIP, 128))
            feed_out[at, :] = (unit * gain[...] + shift[...]).astype(BF16)
            return carry

        lax.fori_loop(0, att.shape[0] // STRIP, rows, 0)


def moments(residual):
    center = residual - jnp.mean(residual, axis=-1, keepdims=True)
    spread = jnp.mean(center * center, axis=-1, keepdims=True)
    inverse = lax.rsqrt(spread + EPSILON)
    return center * inverse, inverse


def pull_norm(scaled, unit, inverse):
    first = jnp.mean(scaled, axis=-1, keepdims=True)
    second = jnp.mean(scaled * unit, axis=-1, keepdims=True)
    return inverse * (scaled - first - unit * second)


def gelu_pair(value):
    phi = 0.5 + 0.5 * lax.erf(value * math.sqrt(0.5))
    density = jnp.exp(value * value * -0.5) * (1.0 / math.sqrt(2.0 * math.pi))
    return value * phi, phi + value * density


NEAR_PLAN = [(j, None) for j in range(BLOCKS - 1)] + [(BLOCKS - 1, CORE), (BLOCKS - 1, -1)]
FAR_PLAN = (
    [(0, CORE), (0, -1), (1, None), (2, None), (3, 0), (3, 1)]
    + [(4, None), (5, None), (6, 0), (6, 1), (BLOCKS - 1, CORE), (BLOCKS - 1, -1)]
)
NEAR, FAR = len(NEAR_PLAN), len(FAR_PLAN)


def load_feed(info, plan, pieces, target, sem):
    copies = [[], []]
    for piece, (place, parity) in zip(pieces, plan):
        for which in range(2):
            if parity in (CORE, -1):
                own = info[CORE] if parity == CORE else 1 - info[CORE]
                source, where, late = piece, target.at[own, :, info[place]], 0
            elif parity is None:
                source, where, late = piece.at[which], target.at[which, :, info[place]], which
            else:
                source, where, late = piece, target.at[parity, :, info[place]], parity
            if parity is None or which == 0:
                at = len(copies[0]) + len(copies[1])
                copies[late].append(pltpu.make_async_copy(source, where, sem.at[at]))
    return copies


def side_of(weights, b, side, at):
    value = weights[b, side, :, :, at]
    return value.reshape(value.shape[0] * value.shape[1], value.shape[2])


def feed_step(feed, weights, b, bias_row, slope_out, total):
    for i in range(feed.shape[1] // WIDE):
        at = slice(i * WIDE, (i + 1) * WIDE)
        value = dot(feed[...], side_of(weights, b, 0, at), NN) + bias_row[:, at]
        act, slope = gelu_pair(value)
        slope_out[:, at] = slope.astype(BF16)
        total[...] += dot(act.astype(BF16), side_of(weights, b, 1, at), NT)


def middle_kernel(
    info, feed, bias, unit_one, inverse_one, gain_one, shift_one, bias_down, gain_two, shift_two,
    cot_long, cot_short, *rest,
):
    blocks, rest = rest[:BLOCKS + 1], rest[BLOCKS + 1 :]
    pieces, rest = rest[: NEAR + FAR], rest[NEAR + FAR :]
    (
        layer_out, hidden_out, delta_out, att_out, sums_out,
        total, low, slopes, cot, held, wo, layer, sem, small,
    ) = rest
    stores = [
        pltpu.make_async_copy(layer, layer_out, small.at[BLOCKS + 3]),
        pltpu.make_async_copy(total, delta_out, small.at[BLOCKS + 4]),
    ]
    width = feed.shape[1]
    count = feed.shape[0]
    short_len = cot_short.shape[1]
    part = count - short_len
    loads = load_feed(info, NEAR_PLAN, pieces[:NEAR], held.at[pl.ds(0, 2)], sem.at[0])
    loads += load_feed(info, FAR_PLAN, pieces[NEAR:], held.at[pl.ds(2, 2)], sem.at[1])
    last = load_columns(info, blocks, 3, wo, small)
    extra = [
        pltpu.make_async_copy(
            cot_long.at[info[SEQ], columns(info[HALF], part)],
            cot.at[pl.ds(0, part)],
            small.at[BLOCKS + 1],
        ),
        pltpu.make_async_copy(
            cot_short.at[info[RANK]], cot.at[pl.ds(part, short_len)], small.at[BLOCKS + 2]
        ),
    ]
    for load in loads:
        run_all(load, "start")
    run_all(extra + last, "start")
    total[...] = jnp.zeros_like(total)
    for b in range(4):
        run_all(loads[b], "wait")
        feed_step(feed, held, b, bias.at[pl.ds(b, 1)], slopes.at[b], total)
    run_all(extra, "wait")
    sums_out[...] = jnp.zeros_like(sums_out)

    def second(i, carry):
        at = columns(i, STRIP)
        normed = unit_one[at, :] * gain_one[...] + shift_one[...]
        unit, inverse = moments(normed + (total[at, :] + bias_down[...]))
        layer[at, :] = (unit * gain_two[...] + shift_two[...]).astype(BF16)
        g = cot[at, :].astype(F32)
        delta = pull_norm(g * gain_two[...], unit, inverse)
        total[at, :] = delta
        low[at, :] = delta.astype(BF16)
        sums_out[0:1, :] += jnp.sum(g, axis=0, keepdims=True)
        sums_out[1:2, :] += jnp.sum(delta, axis=0, keepdims=True)
        return carry

    lax.fori_loop(0, count // STRIP, second, 0)
    stores[0].start()
    for b in range(4):
        for i in range(width // WIDE):
            at = slice(i * WIDE, (i + 1) * WIDE)
            grad = dot(low[...], side_of(held, b, 1, at), NN) * slopes[b, :, at].astype(F32)
            hidden_out[b : b + 1, at] = jnp.sum(grad, axis=0, keepdims=True)
            total[...] += dot(grad.astype(BF16), side_of(held, b, 0, at), NT)

    def first(i, carry):
        at = columns(i, STRIP)
        grad = total[at, :]
        delta = pull_norm(grad * gain_one[...], unit_one[at, :], inverse_one[at, 0:1])
        total[at, :] = delta
        low[at, :] = delta.astype(BF16)
        sums_out[2:3, :] += jnp.sum(grad, axis=0, keepdims=True)
        sums_out[3:4, :] += jnp.sum(delta, axis=0, keepdims=True)
        return carry

    lax.fori_loop(0, count // STRIP, first, 0)
    stores[1].start()
    run_all(last, "wait")
    att_out[...] = dot(low[...], wo[...], NT).astype(BF16)
    run_all(stores, "wait")


def attend_back_kernel(
    info, q, k, v, grad, p_long, p_short, delta_one, weights,
    keep_out, send_out, sums_out, rest_out, near_out, pool, near_pool, dq_all, short, delta, w, sem,
):
    part = p_long.shape[2] // 2
    long_len, short_len = p_long.shape[1], p_short.shape[1]
    width = dq_all.shape[1]
    step, steps = pl.program_id(0), pl.num_programs(0)
    loads = [pltpu.make_async_copy(weights.at[c], w.at[c], sem.at[c]) for c in range(3)]
    loads.append(pltpu.make_async_copy(delta_one, delta, sem.at[3]))

    @pl.when(step == 0)
    def _():
        run_all(loads, "start")

    scale = 1.0 / math.sqrt(DH)
    places = (
        (slice(0, part), slice(0, long_len), p_long, pool),
        (
            slice(part, part + short_len), slice(long_len, long_len + short_len),
            p_short, near_pool,
        ),
    )
    work = [
        (pair, slice(pair * PAIR, (pair + 1) * PAIR), *place)
        for pair in range(q.shape[1] // PAIR)
        for place in places
    ]
    held = [
        dot(v[k_at, at], split_pair(grad[q_at, at].T, 0), NN) for _, at, q_at, k_at, _, _ in work
    ]
    rounded = []
    for (pair, at, q_at, k_at, p_in, target), dp in zip(work, held):
        prob = p_in[pair].astype(F32)
        inner = jnp.sum(dp * prob, axis=0, keepdims=True)
        rounded.append((prob * (dp - inner)).astype(BF16))
    sums_out[...] = jnp.zeros_like(sums_out)
    for (pair, at, q_at, k_at, p_in, target), ds in zip(work, rounded):
        count = q_at.stop - q_at.start
        dv = dot(p_in[pair], split_pair(grad[q_at, at], 1), NN)
        dk = dot(ds, split_pair(q[q_at, at], 1), NN)
        dq = dot(k[k_at, at].T, ds, NN)
        dq = (jnp.concatenate([dq[:DH, :count], dq[DH:, count:]], axis=0) * scale).T
        to = pl.ds(pl.multiple_of(step * q.shape[1] + at.start, PAIR), PAIR)
        dq_all[q_at, to] = dq.astype(BF16)
        target[0, :, at] = dk.astype(BF16)
        target[1, :, at] = dv.astype(BF16)
        sums_out[0:1, at] += jnp.sum(dq, axis=0, keepdims=True)
        sums_out[1:2, at] += jnp.sum(dv, axis=0, keepdims=True)
    keep_out[...] = pool[:, columns(info[HALF], part), :]
    send_out[...] = pool[:, columns(1 - info[HALF], part), :]
    short[:, :, columns(step, q.shape[1])] = near_pool[...]

    @pl.when(step == steps - 1)
    def _():
        run_all(loads, "wait")
        for i in range(width // WIDE):
            at = slice(i * WIDE, (i + 1) * WIDE)
            total = delta[:, at] + dot(dq_all[...], w[0, at, :], NT)
            rest_out[:, at] = total[:part]
            total = total[part:] + dot(short[0], w[1, at, :], NT)
            near_out[:, at] = (total + dot(short[1], w[2, at, :], NT)).astype(BF16)


def late_kernel(
    rest_in, keep, received, weights, out, delta, mine, other, w, small, sem
):
    width = w.shape[1]
    pairs = [(keep, mine), (received, other), (rest_in, delta)]
    loads = [pltpu.make_async_copy(a, b, small.at[i]) for i, (a, b) in enumerate(pairs)]
    parts = [[pltpu.make_async_copy(weights.at[1 + c], w.at[c], sem.at[c])] for c in range(2)]
    run_all(loads[:2] + parts[0] + loads[2:] + parts[1], "start")
    run_all(loads[:2], "wait")
    dk, dv = [
        (mine[side].astype(F32) + other[side].astype(F32)).astype(BF16) for side in range(2)
    ]
    run_all(loads[2:] + parts[0], "wait")
    totals = []
    for i in range(width // WIDE):
        at = slice(i * WIDE, (i + 1) * WIDE)
        totals.append(delta[:, at] + dot(dk, w[0, at, :], NT))
    run_all(parts[1], "wait")
    for i in range(width // WIDE):
        at = slice(i * WIDE, (i + 1) * WIDE)
        out[:, at] = (totals[i] + dot(dv, w[1, at, :], NT)).astype(BF16)


def place_kernel(info, *rest):
    pieces, (long_out, short_out, sem) = rest[:-3], rest[-3:]
    rank = info[RANK]
    part = long_out.shape[0] * long_out.shape[1] // 4
    parts = long_out.shape[1] // part
    copies = []
    for flip in range(4):
        low = rank % 2 if flip % 2 == 0 else 1 - rank % 2
        high = rank // 2 if flip // 2 == 0 else 1 - rank // 2
        who = high * 2 + low
        if len(pieces) == 4:
            long_rows = pieces[flip].at[pl.ds(0, part)]
            short_rows = pieces[flip].at[pl.ds(part, short_out.shape[1])]
        else:
            long_rows, short_rows = pieces[flip], pieces[4 + flip]
        target = long_out.at[who // parts, columns(who % parts, part)]
        copies.append(pltpu.make_async_copy(long_rows, target, sem.at[2 * flip]))
        copies.append(pltpu.make_async_copy(short_rows, short_out.at[who], sem.at[2 * flip + 1]))
    for copy in copies:
        copy.start()
    for copy in copies:
        copy.wait()


def flip_pairs(size, bit):
    return [(i, i ^ bit) for i in range(size)]


def ring_of(size):
    return list(range(0, size, 2)) + list(range(size - 1, 0, -2))


def ring_move(dp, tensor):
    ring = ring_of(dp)
    pairs = []
    for i in range(dp):
        for t in range(tensor):
            to = ring[(i + 1) % dp] if t % 2 == 0 else ring[(i - 1) % dp]
            pairs.append((ring[i] * tensor + t, to * tensor + t))
    return lambda x: lax.ppermute(x, ("dp", "tensor"), pairs)


def tie(value, *after):
    return lax.optimization_barrier((value, *after))[0]


def scoped(name, move, x):
    with jax.named_scope(name):
        return move(x)


class Moves:
    def __init__(self, **start):
        self.held = dict(start)

    def __getitem__(self, names):
        return [self.held[n] for n in names]

    def tie(self, value, *names):
        return lax.optimization_barrier((value, *self[names]))[0]

    def go(self, name, source, move, *after):
        value = self.held[source] if isinstance(source, str) else source
        if after:
            value = self.tie(value, *after)
        with jax.named_scope(name):
            self.held[name] = move(value)


def block_places(size, core):
    if size != BLOCKS:
        return jnp.arange(BLOCKS, dtype=jnp.int32)
    ring = ring_of(size)
    place = [ring.index(d) for d in range(size)]
    table = []
    for sign in (-1, 1):
        steps = [0] + [sign * j for j in (1, 2, 3)] + [-sign * j for j in (1, 2, 3)] + [4]
        table.append([[ring[(place[d] + s) % size] for s in steps] for d in range(size)])
    return jnp.array(table, jnp.int32)[core, lax.axis_index("dp")]


def local(
    dp, tensor,
    tokens_long, tokens_short, lengths_long, lengths_short,
    weight_project, weight_output, weight_in, weight_down,
    bias_query, bias_value, bias_output, gain_one, shift_one, bias_hidden, bias_down,
    gain_two, shift_two, cotangent_long, cotangent_short,
):
    long_count, long_len, width = tokens_long.shape
    short_count, short_len, _ = tokens_short.shape
    parts = tensor // long_count
    assert tensor == 4 and parts == 2 and short_count == tensor
    part = long_len // parts
    rows = part + short_len
    keys = long_len + short_len
    units = weight_in.shape[1]

    rank = lax.axis_index("tensor")
    core, seq, half = rank % 2, rank // parts, rank % parts
    info = jnp.concatenate(
        [
            block_places(dp, core),
            jnp.stack(
                [core, seq, half, rank, lengths_long[seq], lengths_short[rank]]
            ).astype(jnp.int32),
        ]
    )
    core_pairs = flip_pairs(tensor, 1)
    far_pairs = flip_pairs(tensor, 2)

    def to_core(x):
        return lax.ppermute(x, "tensor", core_pairs)

    def to_far(x):
        return lax.ppermute(x, "tensor", far_pairs)

    def by_parity(mine, other):
        first = jnp.where(core == 0, mine, other)
        return jnp.stack([first, jnp.where(core == 0, other, mine)])

    def own_half(x, index):
        return lax.dynamic_slice_in_dim(x, index * (x.shape[0] // 2), x.shape[0] // 2, axis=0)

    (both,) = call(
        join_kernel,
        [((weight_project.shape[0], 4 * width), BF16)],
        [weight_project, weight_output],
        [VMEM] * 2,
        [],
        0, 4 << 20,
        vmem=16,
    )
    f = jnp.stack([weight_in, weight_down.T])
    hidden_row = bias_hidden.reshape(1, units)
    if dp == BLOCKS:
        round_ring = ring_move(dp, tensor)
        s = Moves(w0=both, f=f, b=hidden_row, info=info)
        h = s.held
        s.go("c0", "f", to_core)
        s.go("by", "b", to_far)
        s.go("y0", "f", to_far, "by")
        h["bb"] = jnp.concatenate(s["b", "by"], axis=0)
        s.go("bc", "bb", to_core)
        s.go("w1", "w0", round_ring)
        h["f0"] = by_parity(f, h["c0"])
        s.go("f1", "f0", round_ring)
        s.go("v1", "w1", to_core)
        s.go("w2", "w1", round_ring, "y0", "info")
        s.go("d0", "y0", to_core, "bc")
        s.go("f2", "f1", round_ring)
        s.go("y1", "f1", to_far, "y0")
        s.go("w3", "w2", round_ring, "f1", "v1", "d0")
        s.go("c1", "f1", to_core)
        s.go("v2", "w2", to_core)
        s.go("f3", "f2", round_ring, "y1", "c1")
        s.go("y2", "f2", to_far, "y1")
        s.go("w4", own_half(h["w3"], core), round_ring, "f2", "v2")
        s.go("v3", "w3", to_core)
        s.go("c2", "f2", to_core)
        s.go("d1", "y1", to_core)
        s.go("f4", own_half(h["f3"], core)[0], round_ring, "y2")
        s.go("y3a", h["f3"][0], to_far, "y2", "w3")
        s.go("y3b", h["y2"][1], round_ring, "v3")
        s.go("v4", "w4", to_core, "y2")
        blocks = s["w0", "w1", "w2", "w3", "v1", "v2", "v3", "w4", "v4"]
        blocks[0] = s.tie(blocks[0], "f3", "y2", "c2", "d1")
    else:
        s = None

        def cut(whole, axis):
            return jnp.split(whole, BLOCKS, axis=axis)

        blocks = cut(lax.all_gather(both, "dp", axis=0, tiled=True), 0)
        last = blocks.pop()
        blocks += [own_half(last, core), own_half(last, 1 - core)]
        full = lax.all_gather(f, "dp", axis=1, tiled=True)
        full = by_parity(full, to_core(full))
        across = to_far(full)
        near = cut(full, 2)
        last = near.pop()
        near += [own_half(last, core)[0], own_half(last, 1 - core)[0]]
        far = cut(across, 2)
        pick = {CORE: core, -1: 1 - core}
        far = [
            far[j] if parity is None else own_half(far[j], pick.get(parity, parity))[0]
            for j, parity in FAR_PLAN
        ]
        near_bias = jnp.concatenate([hidden_row, to_far(hidden_row)], axis=0)
        across = to_core(near_bias)

    def row(vector):
        return vector.reshape(1, width)

    def lanes(*lead):
        return pl.BlockSpec((*lead, GROUP * PAIR), lambda i: (0,) * len(lead) + (i,))

    def heads(*last):
        return pl.BlockSpec((GROUP, *last), lambda i: (i, 0, 0))

    q, k, v, weights = call(
        project_kernel,
        [((rows, width), BF16), ((keys, width), BF16), ((keys, width), BF16),
         ((3, width, width), BF16)],
        [info, tokens_long, tokens_short, *blocks, row(bias_query), row(bias_value)],
        [SMEM] + [ANY] * (BLOCKS + 3) + [VMEM] * 2,
        [pltpu.VMEM((keys, width), BF16), pltpu.VMEM((rows, width), BF16),
         pltpu.VMEM((3, width, width), BF16),
         pltpu.VMEM((rows, width), BF16), pltpu.VMEM((keys, width), BF16),
         pltpu.VMEM((keys, width), BF16), pltpu.SemaphoreType.DMA((3, BLOCKS + 1)),
         pltpu.SemaphoreType.DMA((10,))],
        2 * width * width * (rows + 2 * keys), 10 << 20,
        out_specs=[ANY] * 4,
        vmem=PROJECT_MIB,
    )
    if s is not None:
        h["q"] = q
        s.go("c3", "f3", to_core, "q")
        s.go("c4", "f4", to_core, "q")
        s.go("d2", "y2", to_core, "q")
        s.go("d3a", "y3a", to_core, "q")
        near = s["f0", "f1", "f2", "f3", "c1", "c2", "c3", "f4", "c4"]
        s.go("y4", jnp.where(core == 0, h["y3a"], h["y3b"]), round_ring, "q")
        q = s.tie(q, "y3a", "y3b", "f4")

    def whole(*shape):
        return pl.BlockSpec(shape, lambda i: (0,) * len(shape))

    p_long, p_short, unit_one, inverse_one, feed = call(
        attend_kernel,
        [((H // 2, long_len, 2 * part), BF16), ((H // 2, short_len, 2 * short_len), BF16),
         ((rows, width), F32), ((rows, 128), F32), ((rows, width), BF16)],
        [info, q, k, v, row(bias_output), row(gain_one), row(shift_one), tokens_long,
         tokens_short, *blocks],
        [SMEM, lanes(rows), lanes(keys), lanes(keys)] + [whole(1, width)] * 3
        + [ANY] * (BLOCKS + 3),
        [pltpu.VMEM((rows, width), BF16), pltpu.VMEM((rows, width), BF16),
         pltpu.VMEM((width, width), BF16), pltpu.SemaphoreType.DMA((BLOCKS + 1,)),
         pltpu.SemaphoreType.DMA((2,))],
        4 * width * (long_len * part + short_len * short_len) + 2 * width * width * rows, 14 << 20,
        exps=H * (long_len * part + short_len * short_len),
        out_specs=[heads(long_len, 2 * part), heads(short_len, 2 * short_len),
                   whole(rows, width), whole(rows, 128), whole(rows, width)],
        vmem=ATTEND_MIB,
        grid=(H // (2 * GROUP),),
    )
    if s is not None:
        h["feed"] = feed
        s.go("d3b", "y3b", to_core, "feed")
        s.go("d4", "y4", to_core, "feed")
        near_bias, across = s["bb", "bc"]
        far = s["y0", "d0", "y1", "y2", "y3a", "y3b", "d1", "d2", "d3a", "d3b", "y4", "d4"]
    bias_rows = jnp.concatenate([by_parity(near_bias[j], across[j]) for j in range(2)], axis=0)
    layer, hidden_sums, delta_one, grad_att, sums_a = call(
        middle_kernel,
        [((rows, width), BF16), ((4, units), F32),
         ((rows, width), F32), ((rows, width), BF16), ((4, width), F32)],
        [info, feed, bias_rows, unit_one, inverse_one, row(gain_one), row(shift_one),
         row(bias_down), row(gain_two), row(shift_two), cotangent_long, cotangent_short, *blocks,
         *near, *far],
        [SMEM] + [VMEM] * 9 + [ANY] * (3 + BLOCKS + NEAR + FAR),
        [pltpu.VMEM((rows, width), F32), pltpu.VMEM((rows, width), BF16),
         pltpu.VMEM((4, rows, units), BF16), pltpu.VMEM((rows, width), BF16),
         pltpu.VMEM((4, 2, BLOCKS, width // BLOCKS, units), BF16),
         pltpu.VMEM((width, width), BF16), pltpu.VMEM((rows, width), BF16),
         pltpu.SemaphoreType.DMA((2, 2 * FAR)), pltpu.SemaphoreType.DMA((BLOCKS + 5,))],
        34 * width * units * rows, 26 << 20,
        out_specs=[ANY, VMEM, ANY, VMEM, VMEM],
        vmem=MIDDLE_MIB,
    )
    layer_far = scoped("layer_far", to_far, layer)
    layer_core = scoped("layer_core", to_core, layer)
    keep, send, sums_c, rest, delta_near = call(
        attend_back_kernel,
        [((2, part, width), BF16), ((2, part, width), BF16), ((2, width), F32),
         ((part, width), F32), ((short_len, width), BF16)],
        [info, q, k, v, grad_att, p_long, p_short, delta_one, weights],
        [SMEM, lanes(rows), lanes(keys), lanes(keys), lanes(rows), heads(long_len, 2 * part),
         heads(short_len, 2 * short_len), ANY, ANY],
        [pltpu.VMEM((2, long_len, GROUP * PAIR), BF16),
         pltpu.VMEM((2, short_len, GROUP * PAIR), BF16), pltpu.VMEM((rows, width), BF16),
         pltpu.VMEM((2, short_len, width), BF16), pltpu.VMEM((rows, width), F32),
         pltpu.VMEM((3, width, width), BF16), pltpu.SemaphoreType.DMA((4,))],
        8 * width * (long_len * part + short_len * short_len)
        + 2 * width * width * (rows + 2 * short_len), 20 << 20,
        out_specs=[lanes(2, part), lanes(2, part), lanes(2), whole(part, width),
                   whole(short_len, width)],
        vmem=BACK_MIB,
        grid=(H // (2 * GROUP),),
    )
    received = scoped("keys_core", to_core, send)
    vectors = jnp.concatenate([sums_a, sums_c], axis=0)
    count = vectors.shape[0]
    paired = hidden_sums.reshape(2, 2, units)
    kept, given = [
        lax.dynamic_index_in_dim(paired, which, axis=1, keepdims=False) for which in (core, 1 - core)
    ]
    over = jnp.concatenate([vectors, given], axis=0)
    over = scoped("sums_core", to_core, tie(over, layer_core))
    vectors, kept = vectors + over[:count], kept + over[count:]
    over = scoped("sums_far", to_far, jnp.concatenate([vectors, kept[1:]], axis=0))
    near_far = scoped("delta_near_far", to_far, tie(delta_near, layer_far))
    near_core = scoped("delta_near_core", to_core, delta_near)
    (delta_rows,) = call(
        late_kernel,
        [((part, width), BF16)],
        [rest, keep, tie(received, layer_far, layer_core, near_core), weights],
        [ANY] * 4,
        [pltpu.VMEM((part, width), F32), pltpu.VMEM((2, part, width), BF16),
         pltpu.VMEM((2, part, width), BF16), pltpu.VMEM((2, width, width), BF16),
         pltpu.SemaphoreType.DMA((3,)), pltpu.SemaphoreType.DMA((2,))],
        4 * width * width * part, 8 << 20,
        vmem=LATE_MIB,
    )
    rows_far = scoped("delta_far", to_far, delta_rows)
    over, near_far, layer_far, delta_near = lax.optimization_barrier(
        (over, near_far, layer_far, delta_near, delta_rows)
    )[:4]
    vectors = jnp.concatenate([vectors, kept[:1]], axis=0) + over
    bit = 1
    while bit < dp:
        vectors = vectors + scoped(
            f"sums_{bit}", lambda x: lax.ppermute(x, "dp", flip_pairs(dp, bit)), vectors
        )
        bit *= 2

    def place(*pieces):
        return call(
            place_kernel,
            [((long_count, long_len, width), BF16), ((short_count, short_len, width), BF16)],
            [info, *pieces],
            [SMEM] + [VMEM] * len(pieces),
            [pltpu.SemaphoreType.DMA((8,))],
            0, 16 * rows * width,
            out_specs=[ANY, ANY],
            vmem=16,
        )

    layer_long, layer_short = place(
        layer, layer_core, layer_far, scoped("layer_far_core", to_core, layer_far)
    )
    near_far_core = scoped("delta_near_far_core", to_core, near_far)
    rows_core = scoped("delta_core", to_core, delta_rows)
    rows_far = tie(rows_far, layer_long, vectors, near_core, near_far_core, rows_core)
    rows_far_core = scoped("delta_far_core", to_core, rows_far)
    delta_long, delta_short = place(
        delta_rows, rows_core, rows_far, rows_far_core,
        delta_near, near_core, near_far, near_far_core,
    )
    return (
        layer_long, layer_short, delta_long, delta_short,
        vectors[4], vectors[5], vectors[3], vectors[2],
        vectors[6], vectors[1], vectors[0],
    )


def solution(mesh):
    in_specs = (
        P("dp", None, None), P("dp", None, None), P("dp"), P("dp"),
        P("dp", None), P("dp", None), P("dp", "tensor"), P("tensor", "dp"),
        P(), P(), P(), P(), P(), P("tensor"), P(), P(), P(),
        P("dp", None, None), P("dp", None, None),
    )
    out_specs = (
        P("dp", None, None), P("dp", None, None), P("dp", None, None), P("dp", None, None),
        P(), P(), P(), P(), P("tensor"), P(), P(),
    )
    body = functools.partial(local, mesh.shape["dp"], mesh.shape["tensor"])
    return jax.shard_map(body, mesh=mesh, in_specs=in_specs, out_specs=out_specs, check_vma=False)
```

```python
import functools
import math

import jax
import jax.numpy as jnp
from jax import lax
from jax.experimental import pallas as pl
from jax.experimental.pallas import tpu as pltpu
from jax.sharding import PartitionSpec as P

H = 16
DH = 64
PAIR = 2 * DH
BLOCKS = 8
TILE = 256
WIDE = 1024
STRIP = 192
GROUP = 4
PROJECT_MIB, ATTEND_MIB = 56, 56
MIDDLE_MIB, BACK_MIB, LATE_MIB = 56, 56, 56

EPSILON = 1e-05
MASKED = -1000000000.0
F32 = jnp.float32
BF16 = jnp.bfloat16

NN = (((1,), (0,)), ((), ()))
NT = (((1,), (1,)), ((), ()))
TN = (((0,), (0,)), ((), ()))

ANY = pl.BlockSpec(memory_space=pl.ANY)
VMEM = pl.BlockSpec(memory_space=pltpu.VMEM)
SMEM = pl.BlockSpec(memory_space=pltpu.SMEM)

CORE, SEQ, HALF, RANK, LEN_LONG, LEN_SHORT = range(BLOCKS, BLOCKS + 6)


def dot(a, b, dims):
    return lax.dot_general(a, b, dims, preferred_element_type=F32)


def call(body, outs, ins, in_specs, scratch, flops, nbytes, out_specs=None, vmem=56, exps=0,
         grid=()):
    if out_specs is None:
        out_specs = [VMEM] * len(outs)
    return pl.pallas_call(
        body,
        grid=grid,
        out_shape=[jax.ShapeDtypeStruct(s, d) for s, d in outs],
        in_specs=in_specs,
        out_specs=out_specs,
        scratch_shapes=scratch,
        compiler_params=pltpu.CompilerParams(vmem_limit_bytes=vmem << 20),
        cost_estimate=pl.CostEstimate(
            flops=int(flops), bytes_accessed=int(nbytes), transcendentals=int(exps)
        ),
        name=body.func.__name__ if isinstance(body, functools.partial) else body.__name__,
    )(*ins)


def columns(i, width):
    return pl.ds(pl.multiple_of(i * width, width), width)


def run_all(copies, what):
    for copy in copies:
        getattr(copy, what)()


def load_columns(info, blocks, chunk, target, sem):
    rows, width = blocks[0].shape[0], target.shape[1]
    places = [columns(info[j], rows) for j in range(BLOCKS - 1)]
    for half in (info[CORE], 1 - info[CORE]):
        places.append(columns(2 * info[BLOCKS - 1] + half, rows // 2))
    at = pl.ds(chunk * width, width)
    return [
        pltpu.make_async_copy(block.at[:, at], target.at[place], sem.at[j])
        for j, (block, place) in enumerate(zip(blocks, places))
    ]


def project_kernel(info, tokens_long, tokens_short, *rest):
    blocks, rest = rest[:BLOCKS + 1], rest[BLOCKS + 1 :]
    bq, bv, q_out, k_out, v_out, w_out, x, own, held, q, k, v, sem, small = rest
    width = bq.shape[1]
    long_len, short_len = tokens_long.shape[1], tokens_short.shape[1]
    part = q_out.shape[0] - short_len
    loads = [load_columns(info, blocks, c, held.at[c], sem.at[c]) for c in range(3)]
    long_rows, short_rows = tokens_long.at[info[SEQ]], tokens_short.at[info[RANK]]
    pairs = [
        (long_rows.at[columns(info[HALF], part)], own.at[pl.ds(0, part)]),
        (short_rows, own.at[pl.ds(part, short_len)]),
        (long_rows, x.at[pl.ds(0, long_len)]),
        (short_rows, x.at[pl.ds(long_len, short_len)]),
    ]
    tokens = [pltpu.make_async_copy(a, b, small.at[i]) for i, (a, b) in enumerate(pairs)]
    run_all(tokens[:2] + loads[0] + tokens[2:] + loads[1] + loads[2], "start")
    scale = 1.0 / math.sqrt(DH)
    stores = []

    def store(source, target):
        stores.append(pltpu.make_async_copy(source, target, small.at[4 + len(stores)]))
        stores[-1].start()

    for chunk, (result, target) in enumerate(((q, q_out), (k, k_out), (v, v_out))):
        run_all((tokens[:2] if chunk == 0 else tokens[2:] if chunk == 1 else []) + loads[chunk], "wait")
        for i in range(width // WIDE):
            at = slice(i * WIDE, (i + 1) * WIDE)
            w = held[chunk, :, at]
            if chunk == 0:
                q[:, at] = ((dot(own[...], w, NN) + bq[:, at]).astype(BF16) * scale).astype(BF16)
            elif chunk == 1:
                k[:, at] = dot(x[...], w, NN).astype(BF16)
            else:
                v[:, at] = (dot(x[...], w, NN) + bv[:, at]).astype(BF16)
        store(result, target)
        store(held.at[chunk], w_out.at[chunk])
    run_all(stores, "wait")


def join_kernel(first, second, out):
    width = first.shape[1]
    out[:, :width] = first[...]
    out[:, width:] = second[...]


def split_pair(value, axis):
    index = lax.broadcasted_iota(jnp.int32, value.shape, axis)
    zero = jnp.zeros_like(value)
    return jnp.concatenate(
        [jnp.where(index < DH, value, zero), jnp.where(index < DH, zero, value)], axis=1 - axis
    )


def attend_kernel(
    info, q, k, v, bias, gain, shift, tokens_long, tokens_short, *rest
):
    blocks, rest = rest[:BLOCKS + 1], rest[BLOCKS + 1 :]
    p_long, p_short, unit_out, inverse_out, feed_out, att, x, wo, sem, small = rest
    part = p_long.shape[2] // 2
    long_len, short_len = p_long.shape[1], p_short.shape[1]
    width = att.shape[1]
    step, steps = pl.program_id(0), pl.num_programs(0)
    copies = [
        pltpu.make_async_copy(
            tokens_long.at[info[SEQ], columns(info[HALF], part)],
            x.at[pl.ds(0, part)],
            small.at[0],
        ),
        pltpu.make_async_copy(
            tokens_short.at[info[RANK]], x.at[pl.ds(part, short_len)], small.at[1]
        ),
    ]
    copies += load_columns(info, blocks, 3, wo, sem)

    @pl.when(step == 0)
    def _():
        run_all(copies, "start")

    places = (
        (slice(0, part), slice(0, long_len), info[LEN_LONG], p_long),
        (
            slice(part, part + short_len), slice(long_len, long_len + short_len),
            info[LEN_SHORT], p_short,
        ),
    )
    work = [
        (pair, slice(pair * PAIR, (pair + 1) * PAIR), *place)
        for place in places
        for pair in range(q.shape[1] // PAIR)
    ]
    held = [
        dot(k[k_at, at], split_pair(q[q_at, at].T, 0), NN) for _, at, q_at, k_at, _, _ in work
    ]
    lows = []
    for (pair, at, q_at, k_at, length, p_out), scores in zip(work, held):
        position = lax.broadcasted_iota(jnp.int32, scores.shape, 0)
        scores = jnp.where(position < length, scores, MASKED)
        highest = jnp.max(scores, axis=0, keepdims=True)
        exponent = jnp.exp(scores - highest)
        total = jnp.sum(exponent, axis=0, keepdims=True)
        low = (exponent * (1.0 / total)).astype(BF16)
        p_out[pair] = low
        lows.append(low)
    for (pair, at, q_at, k_at, length, p_out), low in zip(work, lows):
        count = q_at.stop - q_at.start
        out = dot(v[k_at, at].T, low, NN)
        out = jnp.concatenate([out[:DH, :count], out[DH:, count:]], axis=0)
        to = pl.ds(pl.multiple_of(step * q.shape[1] + at.start, PAIR), PAIR)
        att[q_at, to] = out.T.astype(BF16)

    @pl.when(step == steps - 1)
    def _():
        run_all(copies, "wait")
        for i in range(width // WIDE):
            at = slice(i * WIDE, (i + 1) * WIDE)
            unit_out[:, at] = x[:, at].astype(F32) + dot(att[...], wo[:, at], NN) + bias[:, at]

        def rows(i, carry):
            at = columns(i, STRIP)
            unit, inverse = moments(unit_out[at, :])
            unit_out[at, :] = unit
            inverse_out[at, :] = jnp.broadcast_to(inverse, (STRIP, 128))
            feed_out[at, :] = (unit * gain[...] + shift[...]).astype(BF16)
            return carry

        lax.fori_loop(0, att.shape[0] // STRIP, rows, 0)


def moments(residual):
    center = residual - jnp.mean(residual, axis=-1, keepdims=True)
    spread = jnp.mean(center * center, axis=-1, keepdims=True)
    inverse = lax.rsqrt(spread + EPSILON)
    return center * inverse, inverse


def pull_norm(scaled, unit, inverse):
    first = jnp.mean(scaled, axis=-1, keepdims=True)
    second = jnp.mean(scaled * unit, axis=-1, keepdims=True)
    return inverse * (scaled - first - unit * second)


def gelu_pair(value):
    phi = 0.5 + 0.5 * lax.erf(value * math.sqrt(0.5))
    density = jnp.exp(value * value * -0.5) * (1.0 / math.sqrt(2.0 * math.pi))
    return value * phi, phi + value * density


NEAR_PLAN = [(j, None) for j in range(BLOCKS - 1)] + [(BLOCKS - 1, CORE), (BLOCKS - 1, -1)]
FAR_PLAN = (
    [(0, CORE), (0, -1), (1, None), (2, None), (3, 0), (3, 1)]
    + [(4, None), (5, None), (6, 0), (6, 1), (BLOCKS - 1, CORE), (BLOCKS - 1, -1)]
)
NEAR, FAR = len(NEAR_PLAN), len(FAR_PLAN)


def load_feed(info, plan, pieces, target, sem):
    copies = [[], []]
    for piece, (place, parity) in zip(pieces, plan):
        for which in range(2):
            if parity in (CORE, -1):
                own = info[CORE] if parity == CORE else 1 - info[CORE]
                source, where, late = piece, target.at[own, :, info[place]], 0
            elif parity is None:
                source, where, late = piece.at[which], target.at[which, :, info[place]], which
            else:
                source, where, late = piece, target.at[parity, :, info[place]], parity
            if parity is None or which == 0:
                at = len(copies[0]) + len(copies[1])
                copies[late].append(pltpu.make_async_copy(source, where, sem.at[at]))
    return copies


def side_of(weights, b, side, at):
    value = weights[b, side, :, :, at]
    return value.reshape(value.shape[0] * value.shape[1], value.shape[2])


def feed_step(feed, weights, b, bias_row, slope_out, total):
    for i in range(feed.shape[1] // WIDE):
        at = slice(i * WIDE, (i + 1) * WIDE)
        value = dot(feed[...], side_of(weights, b, 0, at), NN) + bias_row[:, at]
        act, slope = gelu_pair(value)
        slope_out[:, at] = slope.astype(BF16)
        total[...] += dot(act.astype(BF16), side_of(weights, b, 1, at), NT)


def middle_kernel(
    info, feed, bias, unit_one, inverse_one, gain_one, shift_one, bias_down, gain_two, shift_two,
    cot_long, cot_short, *rest,
):
    blocks, rest = rest[:BLOCKS + 1], rest[BLOCKS + 1 :]
    pieces, rest = rest[: NEAR + FAR], rest[NEAR + FAR :]
    (
        layer_out, hidden_out, delta_out, att_out, sums_out,
        total, low, slopes, cot, held, wo, layer, sem, small,
    ) = rest
    stores = [
        pltpu.make_async_copy(layer, layer_out, small.at[BLOCKS + 3]),
        pltpu.make_async_copy(total, delta_out, small.at[BLOCKS + 4]),
    ]
    width = feed.shape[1]
    count = feed.shape[0]
    short_len = cot_short.shape[1]
    part = count - short_len
    loads = load_feed(info, NEAR_PLAN, pieces[:NEAR], held.at[pl.ds(0, 2)], sem.at[0])
    loads += load_feed(info, FAR_PLAN, pieces[NEAR:], held.at[pl.ds(2, 2)], sem.at[1])
    last = load_columns(info, blocks, 3, wo, small)
    extra = [
        pltpu.make_async_copy(
            cot_long.at[info[SEQ], columns(info[HALF], part)],
            cot.at[pl.ds(0, part)],
            small.at[BLOCKS + 1],
        ),
        pltpu.make_async_copy(
            cot_short.at[info[RANK]], cot.at[pl.ds(part, short_len)], small.at[BLOCKS + 2]
        ),
    ]
    for load in loads:
        run_all(load, "start")
    run_all(extra + last, "start")
    total[...] = jnp.zeros_like(total)
    for b in range(4):
        run_all(loads[b], "wait")
        feed_step(feed, held, b, bias.at[pl.ds(b, 1)], slopes.at[b], total)
    run_all(extra, "wait")
    sums_out[...] = jnp.zeros_like(sums_out)

    def second(i, carry):
        at = columns(i, STRIP)
        normed = unit_one[at, :] * gain_one[...] + shift_one[...]
        unit, inverse = moments(normed + (total[at, :] + bias_down[...]))
        layer[at, :] = (unit * gain_two[...] + shift_two[...]).astype(BF16)
        g = cot[at, :].astype(F32)
        delta = pull_norm(g * gain_two[...], unit, inverse)
        total[at, :] = delta
        low[at, :] = delta.astype(BF16)
        sums_out[0:1, :] += jnp.sum(g, axis=0, keepdims=True)
        sums_out[1:2, :] += jnp.sum(delta, axis=0, keepdims=True)
        return carry

    lax.fori_loop(0, count // STRIP, second, 0)
    stores[0].start()
    for b in range(4):
        for i in range(width // WIDE):
            at = slice(i * WIDE, (i + 1) * WIDE)
            grad = dot(low[...], side_of(held, b, 1, at), NN) * slopes[b, :, at].astype(F32)
            hidden_out[b : b + 1, at] = jnp.sum(grad, axis=0, keepdims=True)
            total[...] += dot(grad.astype(BF16), side_of(held, b, 0, at), NT)

    def first(i, carry):
        at = columns(i, STRIP)
        grad = total[at, :]
        delta = pull_norm(grad * gain_one[...], unit_one[at, :], inverse_one[at, 0:1])
        total[at, :] = delta
        low[at, :] = delta.astype(BF16)
        sums_out[2:3, :] += jnp.sum(grad, axis=0, keepdims=True)
        sums_out[3:4, :] += jnp.sum(delta, axis=0, keepdims=True)
        return carry

    lax.fori_loop(0, count // STRIP, first, 0)
    stores[1].start()
    run_all(last, "wait")
    att_out[...] = dot(low[...], wo[...], NT).astype(BF16)
    run_all(stores, "wait")


def attend_back_kernel(
    info, q, k, v, grad, p_long, p_short, delta_one, weights,
    keep_out, send_out, sums_out, rest_out, near_out, pool, near_pool, dq_all, short, delta, w, sem,
):
    part = p_long.shape[2] // 2
    long_len, short_len = p_long.shape[1], p_short.shape[1]
    width = dq_all.shape[1]
    step, steps = pl.program_id(0), pl.num_programs(0)
    loads = [pltpu.make_async_copy(weights.at[c], w.at[c], sem.at[c]) for c in range(3)]
    loads.append(pltpu.make_async_copy(delta_one, delta, sem.at[3]))

    @pl.when(step == 0)
    def _():
        run_all(loads, "start")

    scale = 1.0 / math.sqrt(DH)
    places = (
        (slice(0, part), slice(0, long_len), p_long, pool),
        (
            slice(part, part + short_len), slice(long_len, long_len + short_len),
            p_short, near_pool,
        ),
    )
    work = [
        (pair, slice(pair * PAIR, (pair + 1) * PAIR), *place)
        for pair in range(q.shape[1] // PAIR)
        for place in places
    ]
    held = [
        dot(v[k_at, at], split_pair(grad[q_at, at].T, 0), NN) for _, at, q_at, k_at, _, _ in work
    ]
    rounded = []
    for (pair, at, q_at, k_at, p_in, target), dp in zip(work, held):
        prob = p_in[pair].astype(F32)
        inner = jnp.sum(dp * prob, axis=0, keepdims=True)
        rounded.append((prob * (dp - inner)).astype(BF16))
    sums_out[...] = jnp.zeros_like(sums_out)
    for (pair, at, q_at, k_at, p_in, target), ds in zip(work, rounded):
        count = q_at.stop - q_at.start
        dv = dot(p_in[pair], split_pair(grad[q_at, at], 1), NN)
        dk = dot(ds, split_pair(q[q_at, at], 1), NN)
        dq = dot(k[k_at, at].T, ds, NN)
        dq = (jnp.concatenate([dq[:DH, :count], dq[DH:, count:]], axis=0) * scale).T
        to = pl.ds(pl.multiple_of(step * q.shape[1] + at.start, PAIR), PAIR)
        dq_all[q_at, to] = dq.astype(BF16)
        target[0, :, at] = dk.astype(BF16)
        target[1, :, at] = dv.astype(BF16)
        sums_out[0:1, at] += jnp.sum(dq, axis=0, keepdims=True)
        sums_out[1:2, at] += jnp.sum(dv, axis=0, keepdims=True)
    keep_out[...] = pool[:, columns(info[HALF], part), :]
    send_out[...] = pool[:, columns(1 - info[HALF], part), :]
    short[:, :, columns(step, q.shape[1])] = near_pool[...]

    @pl.when(step == steps - 1)
    def _():
        run_all(loads, "wait")
        for i in range(width // WIDE):
            at = slice(i * WIDE, (i + 1) * WIDE)
            total = delta[:, at] + dot(dq_all[...], w[0, at, :], NT)
            rest_out[:, at] = total[:part]
            total = total[part:] + dot(short[0], w[1, at, :], NT)
            near_out[:, at] = (total + dot(short[1], w[2, at, :], NT)).astype(BF16)


def late_kernel(
    rest_in, keep, received, weights, out, delta, mine, other, w, small, sem
):
    width = w.shape[1]
    pairs = [(keep, mine), (received, other), (rest_in, delta)]
    loads = [pltpu.make_async_copy(a, b, small.at[i]) for i, (a, b) in enumerate(pairs)]
    parts = [[pltpu.make_async_copy(weights.at[1 + c], w.at[c], sem.at[c])] for c in range(2)]
    run_all(loads[:2] + parts[0] + loads[2:] + parts[1], "start")
    run_all(loads[:2], "wait")
    dk, dv = [
        (mine[side].astype(F32) + other[side].astype(F32)).astype(BF16) for side in range(2)
    ]
    run_all(loads[2:] + parts[0], "wait")
    totals = []
    for i in range(width // WIDE):
        at = slice(i * WIDE, (i + 1) * WIDE)
        totals.append(delta[:, at] + dot(dk, w[0, at, :], NT))
    run_all(parts[1], "wait")
    for i in range(width // WIDE):
        at = slice(i * WIDE, (i + 1) * WIDE)
        out[:, at] = (totals[i] + dot(dv, w[1, at, :], NT)).astype(BF16)


def place_kernel(info, *rest):
    pieces, (long_out, short_out, sem) = rest[:-3], rest[-3:]
    rank = info[RANK]
    part = long_out.shape[0] * long_out.shape[1] // 4
    parts = long_out.shape[1] // part
    copies = []
    for flip in range(4):
        low = rank % 2 if flip % 2 == 0 else 1 - rank % 2
        high = rank // 2 if flip // 2 == 0 else 1 - rank // 2
        who = high * 2 + low
        if len(pieces) == 4:
            long_rows = pieces[flip].at[pl.ds(0, part)]
            short_rows = pieces[flip].at[pl.ds(part, short_out.shape[1])]
        else:
            long_rows, short_rows = pieces[flip], pieces[4 + flip]
        target = long_out.at[who // parts, columns(who % parts, part)]
        copies.append(pltpu.make_async_copy(long_rows, target, sem.at[2 * flip]))
        copies.append(pltpu.make_async_copy(short_rows, short_out.at[who], sem.at[2 * flip + 1]))
    for copy in copies:
        copy.start()
    for copy in copies:
        copy.wait()


def flip_pairs(size, bit):
    return [(i, i ^ bit) for i in range(size)]


def ring_of(size):
    return list(range(0, size, 2)) + list(range(size - 1, 0, -2))


def ring_move(dp, tensor):
    ring = ring_of(dp)
    pairs = []
    for i in range(dp):
        for t in range(tensor):
            to = ring[(i + 1) % dp] if t % 2 == 0 else ring[(i - 1) % dp]
            pairs.append((ring[i] * tensor + t, to * tensor + t))
    return lambda x: lax.ppermute(x, ("dp", "tensor"), pairs)


def tie(value, *after):
    return lax.optimization_barrier((value, *after))[0]


def scoped(name, move, x):
    with jax.named_scope(name):
        return move(x)


class Moves:
    def __init__(self, **start):
        self.held = dict(start)

    def __getitem__(self, names):
        return [self.held[n] for n in names]

    def tie(self, value, *names):
        return lax.optimization_barrier((value, *self[names]))[0]

    def go(self, name, source, move, *after):
        value = self.held[source] if isinstance(source, str) else source
        if after:
            value = self.tie(value, *after)
        with jax.named_scope(name):
            self.held[name] = move(value)


def block_places(size, core):
    if size != BLOCKS:
        return jnp.arange(BLOCKS, dtype=jnp.int32)
    ring = ring_of(size)
    place = [ring.index(d) for d in range(size)]
    table = []
    for sign in (-1, 1):
        steps = [0] + [sign * j for j in (1, 2, 3)] + [-sign * j for j in (1, 2, 3)] + [4]
        table.append([[ring[(place[d] + s) % size] for s in steps] for d in range(size)])
    return jnp.array(table, jnp.int32)[core, lax.axis_index("dp")]


def local(
    dp, tensor,
    tokens_long, tokens_short, lengths_long, lengths_short,
    weight_project, weight_output, weight_in, weight_down,
    bias_query, bias_value, bias_output, gain_one, shift_one, bias_hidden, bias_down,
    gain_two, shift_two, cotangent_long, cotangent_short,
):
    long_count, long_len, width = tokens_long.shape
    short_count, short_len, _ = tokens_short.shape
    parts = tensor // long_count
    assert tensor == 4 and parts == 2 and short_count == tensor
    part = long_len // parts
    rows = part + short_len
    keys = long_len + short_len
    units = weight_in.shape[1]

    rank = lax.axis_index("tensor")
    core, seq, half = rank % 2, rank // parts, rank % parts
    info = jnp.concatenate(
        [
            block_places(dp, core),
            jnp.stack(
                [core, seq, half, rank, lengths_long[seq], lengths_short[rank]]
            ).astype(jnp.int32),
        ]
    )
    core_pairs = flip_pairs(tensor, 1)
    far_pairs = flip_pairs(tensor, 2)

    def to_core(x):
        return lax.ppermute(x, "tensor", core_pairs)

    def to_far(x):
        return lax.ppermute(x, "tensor", far_pairs)

    def by_parity(mine, other):
        first = jnp.where(core == 0, mine, other)
        return jnp.stack([first, jnp.where(core == 0, other, mine)])

    def own_half(x, index):
        return lax.dynamic_slice_in_dim(x, index * (x.shape[0] // 2), x.shape[0] // 2, axis=0)

    (both,) = call(
        join_kernel,
        [((weight_project.shape[0], 4 * width), BF16)],
        [weight_project, weight_output],
        [VMEM] * 2,
        [],
        0, 4 << 20,
        vmem=16,
    )
    f = jnp.stack([weight_in, weight_down.T])
    hidden_row = bias_hidden.reshape(1, units)
    if dp == BLOCKS:
        round_ring = ring_move(dp, tensor)
        s = Moves(w0=both, f=f, b=hidden_row, info=info)
        h = s.held
        s.go("c0", "f", to_core)
        s.go("by", "b", to_far)
        s.go("y0", "f", to_far, "by")
        h["bb"] = jnp.concatenate(s["b", "by"], axis=0)
        s.go("bc", "bb", to_core)
        s.go("w1", "w0", round_ring)
        h["f0"] = by_parity(f, h["c0"])
        s.go("f1", "f0", round_ring)
        s.go("v1", "w1", to_core)
        s.go("w2", "w1", round_ring, "y0", "info")
        s.go("d0", "y0", to_core, "bc")
        s.go("f2", "f1", round_ring)
        s.go("y1", "f1", to_far, "y0")
        s.go("w3", "w2", round_ring, "f1", "v1", "d0")
        s.go("c1", "f1", to_core)
        s.go("v2", "w2", to_core)
        s.go("f3", "f2", round_ring, "y1", "c1")
        s.go("y2", "f2", to_far, "y1")
        s.go("w4", own_half(h["w3"], core), round_ring, "f2", "v2")
        s.go("v3", "w3", to_core)
        s.go("c2", "f2", to_core)
        s.go("d1", "y1", to_core)
        s.go("f4", own_half(h["f3"], core)[0], round_ring, "y2")
        s.go("y3a", h["f3"][0], to_far, "y2", "w3")
        s.go("y3b", h["y2"][1], round_ring, "v3")
        s.go("v4", "w4", to_core, "y2")
        blocks = s["w0", "w1", "w2", "w3", "v1", "v2", "v3", "w4", "v4"]
        blocks[0] = s.tie(blocks[0], "f3", "y2", "c2", "d1")
    else:
        s = None

        def cut(whole, axis):
            return jnp.split(whole, BLOCKS, axis=axis)

        blocks = cut(lax.all_gather(both, "dp", axis=0, tiled=True), 0)
        last = blocks.pop()
        blocks += [own_half(last, core), own_half(last, 1 - core)]
        full = lax.all_gather(f, "dp", axis=1, tiled=True)
        full = by_parity(full, to_core(full))
        across = to_far(full)
        near = cut(full, 2)
        last = near.pop()
        near += [own_half(last, core)[0], own_half(last, 1 - core)[0]]
        far = cut(across, 2)
        pick = {CORE: core, -1: 1 - core}
        far = [
            far[j] if parity is None else own_half(far[j], pick.get(parity, parity))[0]
            for j, parity in FAR_PLAN
        ]
        near_bias = jnp.concatenate([hidden_row, to_far(hidden_row)], axis=0)
        across = to_core(near_bias)

    def row(vector):
        return vector.reshape(1, width)

    def lanes(*lead):
        return pl.BlockSpec((*lead, GROUP * PAIR), lambda i: (0,) * len(lead) + (i,))

    def heads(*last):
        return pl.BlockSpec((GROUP, *last), lambda i: (i, 0, 0))

    q, k, v, weights = call(
        project_kernel,
        [((rows, width), BF16), ((keys, width), BF16), ((keys, width), BF16),
         ((3, width, width), BF16)],
        [info, tokens_long, tokens_short, *blocks, row(bias_query), row(bias_value)],
        [SMEM] + [ANY] * (BLOCKS + 3) + [VMEM] * 2,
        [pltpu.VMEM((keys, width), BF16), pltpu.VMEM((rows, width), BF16),
         pltpu.VMEM((3, width, width), BF16),
         pltpu.VMEM((rows, width), BF16), pltpu.VMEM((keys, width), BF16),
         pltpu.VMEM((keys, width), BF16), pltpu.SemaphoreType.DMA((3, BLOCKS + 1)),
         pltpu.SemaphoreType.DMA((10,))],
        2 * width * width * (rows + 2 * keys), 10 << 20,
        out_specs=[ANY] * 4,
        vmem=PROJECT_MIB,
    )
    if s is not None:
        h["q"] = q
        s.go("c3", "f3", to_core, "q")
        s.go("c4", "f4", to_core, "q")
        s.go("d2", "y2", to_core, "q")
        s.go("d3a", "y3a", to_core, "q")
        near = s["f0", "f1", "f2", "f3", "c1", "c2", "c3", "f4", "c4"]
        s.go("y4", jnp.where(core == 0, h["y3a"], h["y3b"]), round_ring, "q")
        q = s.tie(q, "y3a", "y3b", "f4")

    def whole(*shape):
        return pl.BlockSpec(shape, lambda i: (0,) * len(shape))

    p_long, p_short, unit_one, inverse_one, feed = call(
        attend_kernel,
        [((H // 2, long_len, 2 * part), BF16), ((H // 2, short_len, 2 * short_len), BF16),
         ((rows, width), F32), ((rows, 128), F32), ((rows, width), BF16)],
        [info, q, k, v, row(bias_output), row(gain_one), row(shift_one), tokens_long,
         tokens_short, *blocks],
        [SMEM, lanes(rows), lanes(keys), lanes(keys)] + [whole(1, width)] * 3
        + [ANY] * (BLOCKS + 3),
        [pltpu.VMEM((rows, width), BF16), pltpu.VMEM((rows, width), BF16),
         pltpu.VMEM((width, width), BF16), pltpu.SemaphoreType.DMA((BLOCKS + 1,)),
         pltpu.SemaphoreType.DMA((2,))],
        4 * width * (long_len * part + short_len * short_len) + 2 * width * width * rows, 14 << 20,
        exps=H * (long_len * part + short_len * short_len),
        out_specs=[heads(long_len, 2 * part), heads(short_len, 2 * short_len),
                   whole(rows, width), whole(rows, 128), whole(rows, width)],
        vmem=ATTEND_MIB,
        grid=(H // (2 * GROUP),),
    )
    if s is not None:
        h["feed"] = feed
        s.go("d3b", "y3b", to_core, "feed")
        s.go("d4", "y4", to_core, "feed")
        near_bias, across = s["bb", "bc"]
        far = s["y0", "d0", "y1", "y2", "y3a", "y3b", "d1", "d2", "d3a", "d3b", "y4", "d4"]
    bias_rows = jnp.concatenate([by_parity(near_bias[j], across[j]) for j in range(2)], axis=0)
    layer, hidden_sums, delta_one, grad_att, sums_a = call(
        middle_kernel,
        [((rows, width), BF16), ((4, units), F32),
         ((rows, width), F32), ((rows, width), BF16), ((4, width), F32)],
        [info, feed, bias_rows, unit_one, inverse_one, row(gain_one), row(shift_one),
         row(bias_down), row(gain_two), row(shift_two), cotangent_long, cotangent_short, *blocks,
         *near, *far],
        [SMEM] + [VMEM] * 9 + [ANY] * (3 + BLOCKS + NEAR + FAR),
        [pltpu.VMEM((rows, width), F32), pltpu.VMEM((rows, width), BF16),
         pltpu.VMEM((4, rows, units), BF16), pltpu.VMEM((rows, width), BF16),
         pltpu.VMEM((4, 2, BLOCKS, width // BLOCKS, units), BF16),
         pltpu.VMEM((width, width), BF16), pltpu.VMEM((rows, width), BF16),
         pltpu.SemaphoreType.DMA((2, 2 * FAR)), pltpu.SemaphoreType.DMA((BLOCKS + 5,))],
        34 * width * units * rows, 26 << 20,
        out_specs=[ANY, VMEM, ANY, VMEM, VMEM],
        vmem=MIDDLE_MIB,
    )
    layer_far = scoped("layer_far", to_far, layer)
    layer_core = scoped("layer_core", to_core, layer)
    keep, send, sums_c, rest, delta_near = call(
        attend_back_kernel,
        [((2, part, width), BF16), ((2, part, width), BF16), ((2, width), F32),
         ((part, width), F32), ((short_len, width), BF16)],
        [info, q, k, v, grad_att, p_long, p_short, delta_one, weights],
        [SMEM, lanes(rows), lanes(keys), lanes(keys), lanes(rows), heads(long_len, 2 * part),
         heads(short_len, 2 * short_len), ANY, ANY],
        [pltpu.VMEM((2, long_len, GROUP * PAIR), BF16),
         pltpu.VMEM((2, short_len, GROUP * PAIR), BF16), pltpu.VMEM((rows, width), BF16),
         pltpu.VMEM((2, short_len, width), BF16), pltpu.VMEM((rows, width), F32),
         pltpu.VMEM((3, width, width), BF16), pltpu.SemaphoreType.DMA((4,))],
        8 * width * (long_len * part + short_len * short_len)
        + 2 * width * width * (rows + 2 * short_len), 20 << 20,
        out_specs=[lanes(2, part), lanes(2, part), lanes(2), whole(part, width),
                   whole(short_len, width)],
        vmem=BACK_MIB,
        grid=(H // (2 * GROUP),),
    )
    received = scoped("keys_core", to_core, send)
    vectors = jnp.concatenate([sums_a, sums_c], axis=0)
    count = vectors.shape[0]
    paired = hidden_sums.reshape(2, 2, units)
    kept, given = [
        lax.dynamic_index_in_dim(paired, which, axis=1, keepdims=False) for which in (core, 1 - core)
    ]
    over = jnp.concatenate([vectors, given], axis=0)
    over = scoped("sums_core", to_core, tie(over, layer_core))
    vectors, kept = vectors + over[:count], kept + over[count:]
    over = scoped("sums_far", to_far, jnp.concatenate([vectors, kept[1:]], axis=0))
    near_far = scoped("delta_near_far", to_far, tie(delta_near, layer_far))
    near_core = scoped("delta_near_core", to_core, delta_near)
    (delta_rows,) = call(
        late_kernel,
        [((part, width), BF16)],
        [rest, keep, tie(received, layer_far, layer_core, near_core), weights],
        [ANY] * 4,
        [pltpu.VMEM((part, width), F32), pltpu.VMEM((2, part, width), BF16),
         pltpu.VMEM((2, part, width), BF16), pltpu.VMEM((2, width, width), BF16),
         pltpu.SemaphoreType.DMA((3,)), pltpu.SemaphoreType.DMA((2,))],
        4 * width * width * part, 8 << 20,
        vmem=LATE_MIB,
    )
    rows_far = scoped("delta_far", to_far, delta_rows)
    over, near_far, layer_far, delta_near = lax.optimization_barrier(
        (over, near_far, layer_far, delta_near, delta_rows)
    )[:4]
    vectors = jnp.concatenate([vectors, kept[:1]], axis=0) + over
    def place(*pieces):
        return call(
            place_kernel,
            [((long_count, long_len, width), BF16), ((short_count, short_len, width), BF16)],
            [info, *pieces],
            [SMEM] + [VMEM] * len(pieces),
            [pltpu.SemaphoreType.DMA((8,))],
            0, 16 * rows * width,
            out_specs=[ANY, ANY],
            vmem=16,
        )

    layer_long, layer_short = place(
        layer, layer_core, layer_far, scoped("layer_far_core", to_core, layer_far)
    )
    bit = 1
    while bit < dp:
        got = scoped(f"sums_{bit}", lambda x: lax.ppermute(x, "dp", flip_pairs(dp, bit)), vectors)
        vectors = vectors + (tie(got, layer_long) if bit == 2 else got)
        bit *= 2
    near_far_core = scoped("delta_near_far_core", to_core, near_far)
    rows_core = scoped("delta_core", to_core, delta_rows)
    rows_far = tie(rows_far, layer_long, vectors, near_core, near_far_core, rows_core)
    rows_far_core = scoped("delta_far_core", to_core, rows_far)
    delta_long, delta_short = place(
        delta_rows, rows_core, rows_far, rows_far_core,
        delta_near, near_core, near_far, near_far_core,
    )
    return (
        layer_long, layer_short, delta_long, delta_short,
        vectors[4], vectors[5], vectors[3], vectors[2],
        vectors[6], vectors[1], vectors[0],
    )


def solution(mesh):
    in_specs = (
        P("dp", None, None), P("dp", None, None), P("dp"), P("dp"),
        P("dp", None), P("dp", None), P("dp", "tensor"), P("tensor", "dp"),
        P(), P(), P(), P(), P(), P("tensor"), P(), P(), P(),
        P("dp", None, None), P("dp", None, None),
    )
    out_specs = (
        P("dp", None, None), P("dp", None, None), P("dp", None, None), P("dp", None, None),
        P(), P(), P(), P(), P("tensor"), P(), P(),
    )
    body = functools.partial(local, mesh.shape["dp"], mesh.shape["tensor"])
    return jax.shard_map(body, mesh=mesh, in_specs=in_specs, out_specs=out_specs, check_vma=False)
```
